32 devices in a mesh: frame: 4 (over z), fsdp: 8 (over y, x, core).
Axes of the slice: x: 2, y: 2, z: 4, core: 2. Of those that a mesh axis runs over, the one named last changes fastest.
Arguments:
- video: bfloat16 [8, 8, 196, 768], P('fsdp', 'frame'), may hold values from -6 to 6
- temporal_entry: bfloat16 [768, 2304], P('fsdp'), may hold values from -0.3125 to 0.3125
- temporal_exit: bfloat16 [768, 768], P('fsdp'), may hold values from -0.625 to 0.625
- spatial_entry: bfloat16 [768, 2304], P('fsdp'), may hold values from -0.3125 to 0.3125
- spatial_exit: bfloat16 [768, 768], P('fsdp'), may hold values from -1.25 to 1.25
- expand_weight: bfloat16 [768, 3072], P('fsdp'), may hold values from -0.21875 to 0.21875
- contract_weight: bfloat16 [3072, 768], P('fsdp'), may hold values from -0.109375 to 0.109375
- layer_gains: bfloat16 [3, 768], P(None, 'fsdp'), may hold values from 0.25 to 1.75
- layer_shifts: bfloat16 [3, 768], P(None, 'fsdp'), may hold values from -4 to 4
- branch_biases: bfloat16 [3, 768], P(None, 'fsdp'), may hold values from -4 to 4
- expand_bias: bfloat16 [3072], P('fsdp'), may hold values from -4 to 4
- cotangent: bfloat16 [8, 8, 196, 768], P('fsdp', 'frame'), may hold values from -6 to 6
Outputs:
- layer_output: bfloat16 [8, 8, 196, 768], P('fsdp', 'frame')
- input_grad: float32 [8, 8, 196, 768], P('fsdp', 'frame')
- temporal_entry_grad: float32 [768, 2304], P('fsdp')
- temporal_exit_grad: float32 [768, 768], P('fsdp')
- spatial_entry_grad: float32 [768, 2304], P('fsdp')
- spatial_exit_grad: float32 [768, 768], P('fsdp')
- expand_weight_grad: float32 [768, 3072], P('fsdp')
- contract_weight_grad: float32 [3072, 768], P('fsdp')
- layer_gains_grad: float32 [3, 768], P(None, 'fsdp')
- layer_shifts_grad: float32 [3, 768], P(None, 'fsdp')
- branch_biases_grad: float32 [3, 768], P(None, 'fsdp')
- expand_bias_grad: float32 [3072], P('fsdp')
The draws below stay inside these ranges and needn't reach their ends.
All inputs are finite; a program needn't handle non-finite values.
Results may differ from the reference program's by a relative error of at most 0.024.
The reference program's roundings to bfloat16 on the way count: a program that leaves them out, or rounds other values in their place, can miss the bound.
Values may be sent and summed in bfloat16 or wider, within the bound.
No kernel may reach another device: no remote copies, remote signals or barrier semaphores. Data moves between devices by JAX's collectives and lax.ppermute only.
A program may use at most 192 MiB of HBM per device.

```python
import jax
import jax.numpy as jnp
from jax import lax

D = 768
HEADS = 12
FF = 3072
FRAMES = 8
PLACES = 196
CLIPS = 8


def with_spikes(drawn, key, source, target, shards_of, factor):
    def block_of(axis_at):
        return (jnp.arange(drawn.shape[axis_at]) // (drawn.shape[axis_at] // shards_of)).reshape((-1,) + (1,) * (drawn.ndim - 1 - axis_at))

    one_side = jax.random.permutation(key, shards_of)[block_of(target)]
    far = (block_of(target) + shards_of // 2) % shards_of
    return jnp.where((block_of(source) == one_side) | (block_of(source) == far), factor * drawn, drawn)


def shard_levels(stream_key, extent, shards, smallest, largest):
    gain = 1.0
    for axis_at, parts in shards:
        steps = jax.random.uniform(jax.random.fold_in(jax.random.fold_in(stream_key, 6), axis_at), (parts,), jnp.float32, smallest / len(shards), largest / len(shards))
        gain = gain * jnp.repeat(jnp.exp(steps), extent[axis_at] // parts).reshape((-1,) + (1,) * (len(extent) - 1 - axis_at))
    return gain


def scatter_about(key, extent, deviation, limit, pieces=(), held_as=jnp.bfloat16):
    loudness = shard_levels(key, extent, pieces, -0.22, 0.18) if pieces else 1.0
    entries = jax.random.normal(key, extent, jnp.float32) * deviation * loudness
    return jnp.minimum(jnp.maximum(entries, -limit), limit).astype(held_as)


def bell_draw_with(stream_key, extent, deviation, bound, shards, heavy, dtype=jnp.bfloat16):
    values = deviation * jax.random.normal(stream_key, extent, jnp.float32)
    if shards:
        values = values * shard_levels(stream_key, extent, shards, -0.22, 0.18)
    return jnp.clip(with_spikes(values, jax.random.fold_in(stream_key, 3), *heavy), -bound, bound).astype(dtype)


def setup_inputs(seed: int = 0) -> dict:
    seeds = jax.random.split(jax.random.key(seed), 13)
    video = bell_draw_with(seeds[0], (CLIPS, FRAMES, PLACES, D), 1.0, 6.0, ((0, 8), (1, 4)), (0, 3, 8, 2.0))
    temporal_entry = scatter_about(seeds[1], (D, 3 * D), (D // 2) ** -0.5, 0.3125, ((0, 8),))
    temporal_exit = scatter_about(seeds[2], (D, D), (D // 8) ** -0.5, 0.625, ((0, 8),))
    spatial_entry = scatter_about(seeds[3], (D, 3 * D), (D // 2) ** -0.5, 0.3125, ((0, 8),))
    spatial_exit = scatter_about(seeds[4], (D, D), (D // 32) ** -0.5, 1.25, ((0, 8),))
    expand_weight = scatter_about(seeds[5], (D, FF), D ** -0.5, 0.21875, ((0, 8),))
    contract_weight = scatter_about(seeds[6], (FF, D), FF ** -0.5, 0.109375, ((0, 8),))
    layer_gains = jnp.clip(1.0 + 0.15 * jax.random.normal(seeds[7], (3, D), jnp.float32), 0.25, 1.75).astype(jnp.bfloat16)
    layer_shifts = scatter_about(seeds[8], (3, D), 0.3, 4.0, ((1, 8),))
    branch_biases = scatter_about(seeds[9], (3, D), 0.3, 4.0, ((1, 8),))
    expand_bias = scatter_about(seeds[10], (FF,), 0.3, 4.0, ((0, 8),))
    cotangent = bell_draw_with(seeds[11], (CLIPS, FRAMES, PLACES, D), 1.0, 6.0, ((0, 8), (1, 4)), (0, 3, 8, 2.0))
    return {"video": video, "temporal_entry": temporal_entry, "temporal_exit": temporal_exit, "spatial_entry": spatial_entry, "spatial_exit": spatial_exit, "expand_weight": expand_weight, "contract_weight": contract_weight, "layer_gains": layer_gains, "layer_shifts": layer_shifts, "branch_biases": branch_biases, "expand_bias": expand_bias, "cotangent": cotangent}


@jax.custom_vjp
def low(v):
    return lax.optimization_barrier(v.astype(jnp.bfloat16)).astype(jnp.float32)

@jax.custom_vjp
def low_back(v):
    return v

def low_keep(v):
    return (low(v), None)

def low_pass(kept, grad):
    return (grad,)

def back_keep(v):
    return (v, None)

def back_low(kept, grad):
    return (low(grad),)
low.defvjp(low_keep, low_pass)
low_back.defvjp(back_keep, back_low)
norm_eps = 1e-05

def matmul_high(first_op, second_op):
    return jnp.einsum('...i,ij->...j', first_op, second_op, precision=lax.Precision.HIGHEST)

def layer_norm(values, norm_gain, norm_shift):
    average = lax.optimization_barrier(jnp.mean(values, axis=-1, keepdims=True))
    centred = values - average
    variance = lax.optimization_barrier(jnp.mean(centred * centred, axis=-1, keepdims=True))
    return centred * lax.rsqrt(variance + norm_eps) * norm_gain + norm_shift

def attend(packed):
    groups, length, triple = packed.shape
    head_size = triple // (3 * HEADS)
    parted = packed.reshape(groups, length, 3, HEADS, head_size)
    queries = parted[:, :, 0]
    key_rows = parted[:, :, 1]
    values = parted[:, :, 2]
    factor = head_size ** (-0.5)
    scores = low_back(jnp.einsum('blhd,bmhd->bhlm', queries, key_rows, precision=lax.Precision.HIGHEST) * factor)
    attention = low(jax.nn.softmax(scores, axis=-1))
    blended = jnp.einsum('bhlm,bmhd->blhd', attention, values, precision=lax.Precision.HIGHEST)
    return low_back(low(blended.reshape(groups, length, triple // 3)))

def layer(clip, params):
    temporal_entry, temporal_exit, spatial_entry, spatial_exit, expand_weight, contract_weight, layer_gains, layer_shifts, branch_biases, expand_bias = params
    normed = low_back(low(layer_norm(clip, layer_gains[0], layer_shifts[0])))
    packed = low_back(low(matmul_high(normed, temporal_entry)))
    blended = jnp.swapaxes(attend(jnp.swapaxes(packed, 0, 1)), 0, 1)
    after_time = clip + low_back(matmul_high(blended, temporal_exit) + branch_biases[0])
    normed = low_back(low(layer_norm(after_time, layer_gains[1], layer_shifts[1])))
    packed = low_back(low(matmul_high(normed, spatial_entry)))
    blended = attend(packed)
    after_space = after_time + low_back(matmul_high(blended, spatial_exit) + branch_biases[1])
    normed = low_back(low(layer_norm(after_space, layer_gains[2], layer_shifts[2])))
    hidden = low_back(matmul_high(normed, expand_weight) + expand_bias)
    active = low(jax.nn.gelu(hidden, approximate=False))
    return after_space + low_back(matmul_high(active, contract_weight) + branch_biases[2])

def reference(video, temporal_entry, temporal_exit, spatial_entry, spatial_exit, expand_weight, contract_weight, layer_gains, layer_shifts, branch_biases, expand_bias, cotangent):
    params = tuple((weight.astype(jnp.float32) for weight in (temporal_entry, temporal_exit, spatial_entry, spatial_exit, expand_weight, contract_weight, layer_gains, layer_shifts, branch_biases, expand_bias)))

    def one_clip(running, inputs):
        clip_in, clip_cot = inputs
        result, pullback = jax.vjp(layer, clip_in.astype(jnp.float32), params)
        grad_clip, grad_params = pullback(clip_cot.astype(jnp.float32))
        running = tuple((before + increment for before, increment in zip(running, grad_params)))
        return (running, (result.astype(jnp.bfloat16), grad_clip))
    initial = tuple((jnp.zeros_like(weight) for weight in params))
    totals, (outputs, input_grad) = lax.scan(one_clip, initial, (video, cotangent))
    return (outputs, input_grad, totals[0], totals[1], totals[2], totals[3], totals[4], totals[5], totals[6], totals[7], totals[8], totals[9])
```

```python
import functools

import jax
import jax.numpy as jnp
from jax import lax
from jax.experimental import pallas as pl
from jax.experimental.pallas import tpu as pltpu
from jax.sharding import PartitionSpec as P

HEADS = 12


norm_eps = 1e-05


def layer_norm(values, norm_gain, norm_shift):
    average = jnp.mean(values, axis=-1, keepdims=True)
    centred = values - average
    variance = jnp.mean(centred * centred, axis=-1, keepdims=True)
    return centred * lax.rsqrt(variance + norm_eps) * norm_gain + norm_shift


def rounded(values):
    return lax.optimization_barrier(values.astype(jnp.bfloat16)).astype(jnp.float32)


def dense(first_op, second_op):
    return jnp.dot(first_op, second_op, preferred_element_type=jnp.float32)


def dense_left(first_op, second_op):
    return lax.dot_general(
        first_op, second_op, (((0,), (0,)), ((), ())), preferred_element_type=jnp.float32
    )


def dense_right(first_op, second_op):
    return lax.dot_general(
        first_op, second_op, (((1,), (1,)), ((), ())), preferred_element_type=jnp.float32
    )


def split_heads(packed):
    outer = packed.shape
    parted = packed.reshape(outer[:-1] + (3, HEADS, outer[-1] // (3 * HEADS)))
    return (parted[..., 0, :, :], parted[..., 1, :, :], parted[..., 2, :, :])


def attend_forward(packed, layout):
    key_layout = layout.replace("l", "m")
    queries, key_rows, values = split_heads(packed)
    factor = queries.shape[-1] ** (-0.5)
    scores = (
        jnp.einsum(
            layout + "hd," + key_layout + "hd->cqhlm",
            queries,
            key_rows,
            preferred_element_type=jnp.float32,
        )
        * factor
    )
    highest = jnp.max(scores, axis=-1, keepdims=True)
    raised = jnp.exp(scores - highest)
    row_totals = jnp.sum(raised, axis=-1, keepdims=True)
    attention = (raised / row_totals).astype(jnp.bfloat16)
    blended = jnp.einsum(
        "cqhlm," + key_layout + "hd->" + layout + "hd",
        attention,
        values,
        preferred_element_type=jnp.float32,
    )
    outer = packed.shape
    return (
        blended.reshape(outer[:-1] + (outer[-1] // 3,)).astype(jnp.bfloat16),
        highest + jnp.log(row_totals),
    )


def attend_backward(packed, logsum, grad_blended, layout):
    key_layout = layout.replace("l", "m")
    queries, key_rows, values = split_heads(packed)
    factor = queries.shape[-1] ** (-0.5)
    outer = grad_blended.shape
    grad_heads = grad_blended.reshape(outer[:-1] + (HEADS, outer[-1] // HEADS))
    scores = (
        jnp.einsum(
            layout + "hd," + key_layout + "hd->cqhlm",
            queries,
            key_rows,
            preferred_element_type=jnp.float32,
        )
        * factor
    )
    attention = jnp.exp(scores - logsum)
    grad_values = jnp.einsum(
        "cqhlm," + layout + "hd->" + key_layout + "hd",
        attention.astype(jnp.bfloat16),
        grad_heads,
        preferred_element_type=jnp.float32,
    )
    grad_attention = jnp.einsum(
        layout + "hd," + key_layout + "hd->cqhlm",
        grad_heads,
        values,
        preferred_element_type=jnp.float32,
    )
    grad_scores = (
        attention * (grad_attention - jnp.sum(grad_attention * attention, axis=-1, keepdims=True))
    ).astype(jnp.bfloat16)
    grad_queries = (
        jnp.einsum(
            "cqhlm," + key_layout + "hd->" + layout + "hd",
            grad_scores,
            key_rows,
            preferred_element_type=jnp.float32,
        )
        * factor
    )
    grad_keys = (
        jnp.einsum(
            "cqhlm," + layout + "hd->" + key_layout + "hd",
            grad_scores,
            queries,
            preferred_element_type=jnp.float32,
        )
        * factor
    )
    stacked = jnp.stack([grad_queries, grad_keys, grad_values], axis=-3)
    return stacked.reshape(packed.shape).astype(jnp.bfloat16)


def general_body(
    video,
    temporal_entry,
    temporal_exit,
    spatial_entry,
    spatial_exit,
    expand_weight,
    contract_weight,
    layer_gains,
    layer_shifts,
    branch_biases,
    expand_bias,
    cotangent,
):
    clips_here, frames_here, places, model_width = video.shape
    rows_shape = (clips_here, frames_here, places)
    entry_time, exit_time, entry_space, exit_space, gains_low, shifts_low, biases_low = (
        lax.all_gather(temporal_entry, "fsdp", axis=0, tiled=True),
        lax.all_gather(temporal_exit, "fsdp", axis=0, tiled=True),
        lax.all_gather(spatial_entry, "fsdp", axis=0, tiled=True),
        lax.all_gather(spatial_exit, "fsdp", axis=0, tiled=True),
        lax.all_gather(layer_gains, "fsdp", axis=1, tiled=True),
        lax.all_gather(layer_shifts, "fsdp", axis=1, tiled=True),
        lax.all_gather(branch_biases, "fsdp", axis=1, tiled=True),
    )
    expand_full, contract_full, expand_bias_full = (
        lax.all_gather(expand_weight, "fsdp", axis=0, tiled=True),
        lax.all_gather(contract_weight, "fsdp", axis=0, tiled=True),
        lax.all_gather(expand_bias, "fsdp", axis=0, tiled=True),
    )
    gains = gains_low.astype(jnp.float32)
    shifts = shifts_low.astype(jnp.float32)
    biases = biases_low.astype(jnp.float32)
    tokens = video.astype(jnp.float32).reshape(-1, model_width)
    normed_one = layer_norm(tokens, gains[0], shifts[0]).astype(jnp.bfloat16)
    packed_frame = dense(normed_one, entry_time).astype(jnp.bfloat16)
    packed_place = lax.all_to_all(
        packed_frame.reshape(rows_shape + (3 * model_width,)),
        "frame",
        split_axis=2,
        concat_axis=1,
        tiled=True,
    )
    blended_place, logsum_time = attend_forward(packed_place, "clq")
    blended_time = lax.all_to_all(
        blended_place, "frame", split_axis=1, concat_axis=2, tiled=True
    ).reshape(-1, model_width)
    after_time = tokens + (dense(blended_time, exit_time) + biases[0])
    normed_two = layer_norm(after_time, gains[1], shifts[1]).astype(jnp.bfloat16)
    packed_space = (
        dense(normed_two, entry_space).astype(jnp.bfloat16).reshape(rows_shape + (3 * model_width,))
    )
    blended_space, logsum_space = attend_forward(packed_space, "cql")
    blended_rows = blended_space.reshape(-1, model_width)
    after_space = after_time + (dense(blended_rows, exit_space) + biases[1])
    normed_three = layer_norm(after_space, gains[2], shifts[2]).astype(jnp.bfloat16)
    hidden = dense(normed_three, expand_full) + expand_bias_full.astype(jnp.float32)
    active = jax.nn.gelu(hidden, approximate=False).astype(jnp.bfloat16)
    layer_output = (
        (after_space + (dense(active, contract_full) + biases[2]))
        .astype(jnp.bfloat16)
        .reshape(video.shape)
    )
    grad_top = cotangent.astype(jnp.float32).reshape(-1, model_width)
    grad_branch = grad_top.astype(jnp.bfloat16)
    grad_bias_last = jnp.sum(grad_branch.astype(jnp.float32), axis=0)
    grad_contract = dense_left(active, grad_branch)
    grad_active = dense_right(grad_branch, contract_full)
    gelu_pull = jax.vjp(lambda inner: jax.nn.gelu(inner, approximate=False), hidden)[1]
    grad_hidden = gelu_pull(grad_active)[0].astype(jnp.bfloat16)
    grad_expand = dense_left(normed_three, grad_hidden)
    grad_expand_bias = jnp.sum(grad_hidden.astype(jnp.float32), axis=0)
    grad_normed = rounded(dense_right(grad_hidden, expand_full))
    norm_pull = jax.vjp(layer_norm, after_space, gains[2], shifts[2])[1]
    grad_inner, grad_gain_last, grad_shift_last = norm_pull(grad_normed)
    grad_after_space = grad_top + grad_inner
    mlp_parts = (
        lax.psum_scatter(grad_expand, "fsdp", scatter_dimension=0, tiled=True),
        lax.psum_scatter(grad_contract, "fsdp", scatter_dimension=0, tiled=True),
        lax.psum_scatter(grad_expand_bias, "fsdp", scatter_dimension=0, tiled=True),
    )
    grad_branch = grad_after_space.astype(jnp.bfloat16)
    grad_bias_space = jnp.sum(grad_branch.astype(jnp.float32), axis=0)
    grad_exit_space = dense_left(blended_rows, grad_branch)
    grad_blended = (
        dense_right(grad_branch, exit_space)
        .astype(jnp.bfloat16)
        .reshape(rows_shape + (model_width,))
    )
    grad_packed = attend_backward(packed_space, logsum_space, grad_blended, "cql").reshape(
        -1, 3 * model_width
    )
    grad_entry_space = dense_left(normed_two, grad_packed)
    grad_normed = rounded(dense_right(grad_packed, entry_space))
    norm_pull = jax.vjp(layer_norm, after_time, gains[1], shifts[1])[1]
    grad_inner, grad_gain_space, grad_shift_space = norm_pull(grad_normed)
    grad_after_time = grad_after_space + grad_inner
    grad_branch = grad_after_time.astype(jnp.bfloat16)
    grad_bias_time = jnp.sum(grad_branch.astype(jnp.float32), axis=0)
    grad_exit_time = dense_left(blended_time, grad_branch)
    grad_blended = (
        dense_right(grad_branch, exit_time)
        .astype(jnp.bfloat16)
        .reshape(rows_shape + (model_width,))
    )
    grad_blended_place = lax.all_to_all(
        grad_blended, "frame", split_axis=2, concat_axis=1, tiled=True
    )
    grad_packed_place = attend_backward(packed_place, logsum_time, grad_blended_place, "clq")
    grad_packed_frame = lax.all_to_all(
        grad_packed_place, "frame", split_axis=1, concat_axis=2, tiled=True
    ).reshape(-1, 3 * model_width)
    grad_entry_time = dense_left(normed_one, grad_packed_frame)
    grad_normed_one = rounded(dense_right(grad_packed_frame, entry_time))
    norm_pull = jax.vjp(layer_norm, tokens, gains[0], shifts[0])[1]
    grad_inner, grad_gain_time, grad_shift_time = norm_pull(grad_normed_one)
    input_grad = (grad_after_time + grad_inner).reshape(video.shape)
    grad_gains = jnp.stack([grad_gain_time, grad_gain_space, grad_gain_last])
    grad_shifts = jnp.stack([grad_shift_time, grad_shift_space, grad_shift_last])
    grad_biases = jnp.stack([grad_bias_time, grad_bias_space, grad_bias_last])
    attention_parts = (
        lax.psum_scatter(grad_entry_time, "fsdp", scatter_dimension=0, tiled=True),
        lax.psum_scatter(grad_exit_time, "fsdp", scatter_dimension=0, tiled=True),
        lax.psum_scatter(grad_entry_space, "fsdp", scatter_dimension=0, tiled=True),
        lax.psum_scatter(grad_exit_space, "fsdp", scatter_dimension=0, tiled=True),
        lax.psum_scatter(grad_gains, "fsdp", scatter_dimension=1, tiled=True),
        lax.psum_scatter(grad_shifts, "fsdp", scatter_dimension=1, tiled=True),
        lax.psum_scatter(grad_biases, "fsdp", scatter_dimension=1, tiled=True),
    )
    shares = (
        lax.psum_scatter(
            attention_parts[0].astype(jnp.bfloat16), "frame", scatter_dimension=0, tiled=True
        ).astype(jnp.float32),
        lax.psum_scatter(
            attention_parts[1].astype(jnp.bfloat16), "frame", scatter_dimension=0, tiled=True
        ).astype(jnp.float32),
        lax.psum_scatter(
            attention_parts[2].astype(jnp.bfloat16), "frame", scatter_dimension=0, tiled=True
        ).astype(jnp.float32),
        lax.psum_scatter(
            attention_parts[3].astype(jnp.bfloat16), "frame", scatter_dimension=0, tiled=True
        ).astype(jnp.float32),
        lax.psum_scatter(
            mlp_parts[0].astype(jnp.bfloat16), "frame", scatter_dimension=0, tiled=True
        ).astype(jnp.float32),
        lax.psum_scatter(
            mlp_parts[1].astype(jnp.bfloat16), "frame", scatter_dimension=0, tiled=True
        ).astype(jnp.float32),
        lax.psum_scatter(
            jnp.moveaxis(attention_parts[4], 0, 1).astype(jnp.bfloat16),
            "frame",
            scatter_dimension=0,
            tiled=True,
        ).astype(jnp.float32),
        lax.psum_scatter(
            jnp.moveaxis(attention_parts[5], 0, 1).astype(jnp.bfloat16),
            "frame",
            scatter_dimension=0,
            tiled=True,
        ).astype(jnp.float32),
        lax.psum_scatter(
            jnp.moveaxis(attention_parts[6], 0, 1).astype(jnp.bfloat16),
            "frame",
            scatter_dimension=0,
            tiled=True,
        ).astype(jnp.float32),
        lax.psum_scatter(
            mlp_parts[2].astype(jnp.bfloat16), "frame", scatter_dimension=0, tiled=True
        ).astype(jnp.float32),
    )
    pieces = (
        lax.all_gather(shares[0].astype(jnp.bfloat16), "frame", axis=0, tiled=True).astype(
            jnp.float32
        ),
        lax.all_gather(shares[1].astype(jnp.bfloat16), "frame", axis=0, tiled=True).astype(
            jnp.float32
        ),
        lax.all_gather(shares[2].astype(jnp.bfloat16), "frame", axis=0, tiled=True).astype(
            jnp.float32
        ),
        lax.all_gather(shares[3].astype(jnp.bfloat16), "frame", axis=0, tiled=True).astype(
            jnp.float32
        ),
        lax.all_gather(shares[4].astype(jnp.bfloat16), "frame", axis=0, tiled=True).astype(
            jnp.float32
        ),
        lax.all_gather(shares[5].astype(jnp.bfloat16), "frame", axis=0, tiled=True).astype(
            jnp.float32
        ),
        lax.all_gather(shares[6].astype(jnp.bfloat16), "frame", axis=0, tiled=True).astype(
            jnp.float32
        ),
        lax.all_gather(shares[7].astype(jnp.bfloat16), "frame", axis=0, tiled=True).astype(
            jnp.float32
        ),
        lax.all_gather(shares[8].astype(jnp.bfloat16), "frame", axis=0, tiled=True).astype(
            jnp.float32
        ),
        lax.all_gather(shares[9].astype(jnp.bfloat16), "frame", axis=0, tiled=True).astype(
            jnp.float32
        ),
    )
    totals = (
        pieces[0],
        pieces[1],
        pieces[2],
        pieces[3],
        pieces[4],
        pieces[5],
        jnp.moveaxis(pieces[6], 0, 1),
        jnp.moveaxis(pieces[7], 0, 1),
        jnp.moveaxis(pieces[8], 0, 1),
        pieces[9],
    )
    return (
        layer_output,
        input_grad,
        totals[0],
        totals[1],
        totals[2],
        totals[3],
        totals[4],
        totals[5],
        totals[6],
        totals[7],
        totals[8],
        totals[9],
    )


BF = jnp.bfloat16
F32 = jnp.float32
D = 768
FRAME_ROWS = 208
PLACES = 196
HERE = 49
PIECE = 104
ROWS = 416
SPOTS = 400
GROUP = 80
SHARD = 96
HALF = 48
WIDE = 3072
NEG = -1e30
HBM = pl.BlockSpec(memory_space=pl.ANY)
VMEM = pl.BlockSpec(memory_space=pltpu.VMEM)


def nn(a, b):
    return jnp.dot(a, b, preferred_element_type=F32)


def nt(a, b):
    return lax.dot_general(a, b, (((1,), (1,)), ((), ())), preferred_element_type=F32)


def tn(a, b):
    return lax.dot_general(a, b, (((0,), (0,)), ((), ())), preferred_element_type=F32)


def normalised(values):
    average = jnp.mean(values, axis=-1, keepdims=True)
    centred = values - average
    variance = jnp.mean(centred * centred, axis=-1, keepdims=True)
    scale = lax.rsqrt(variance + norm_eps)
    return centred * scale, scale


def norm_back(grad, unit, scale, gain):
    moved = grad * gain
    inner = scale * (
        moved
        - jnp.mean(moved, axis=-1, keepdims=True)
        - unit * jnp.mean(moved * unit, axis=-1, keepdims=True)
    )
    return (
        inner,
        jnp.sum(grad * unit, axis=0, keepdims=True),
        jnp.sum(grad, axis=0, keepdims=True),
    )


def picks(target, columns):
    lanes = lax.broadcasted_iota(jnp.int32, (target.shape[0], columns), 1)
    return jnp.where(lanes == target, 1.0, 0.0).astype(BF)


def row_index(rows):
    return lax.broadcasted_iota(jnp.int32, (rows, 1), 0)


def at_least(value, limit):
    return jnp.where(value >= limit, 1, 0)


def place_from_piece():
    r = row_index(SPOTS)
    col = ((r >> 1) & 3) * PIECE + (r & 1) * HERE + (r >> 3)
    return picks(jnp.where(r < 8 * HERE, col, -1), ROWS)


def piece_parts():
    c = row_index(ROWS)
    k = at_least(c, PIECE) + at_least(c, 2 * PIECE) + at_least(c, 3 * PIECE)
    rem = c - PIECE * k
    f = at_least(rem, HERE)
    return k, f, rem - HERE * f, rem < 2 * HERE


def piece_from_place():
    k, f, p, valid = piece_parts()
    return picks(jnp.where(valid, p * 8 + k * 2 + f, -1), SPOTS)


def frame_from_piece(me):
    r = row_index(ROWS)
    f = at_least(r, FRAME_ROWS)
    pl_ = r - FRAME_ROWS * f
    q = at_least(pl_, HERE) + at_least(pl_, 2 * HERE) + at_least(pl_, 3 * HERE)
    k = (q - me) & 3
    col = k * PIECE + f * HERE + pl_ - HERE * q
    return picks(jnp.where(pl_ < PLACES, col, -1), ROWS)


def piece_from_frame(me):
    k, f, p, valid = piece_parts()
    q = (me + k) & 3
    return picks(jnp.where(valid, f * FRAME_ROWS + HERE * q + p, -1), ROWS)


def small_row(params, index, width=D):
    block = index // 8
    return params[index % 8 : index % 8 + 1, block * D : block * D + width]


def lane_low(rows):
    return lax.broadcasted_iota(jnp.int32, (rows, 128), 1) < 64


def head_masks(factor):
    lane = lax.broadcasted_iota(jnp.int32, (1, 128), 1)
    low = jnp.where(lane < 64, factor, 0.0).astype(BF)
    high = jnp.where(lane < 64, 0.0, factor).astype(BF)
    return low, high


def soft_rows(scores):
    top = jnp.max(scores, axis=-1, keepdims=True)
    raised = jnp.exp(scores - top)
    return raised * (1.0 / jnp.sum(raised, axis=-1, keepdims=True))


def soft_cols(scores):
    top = jnp.max(scores, axis=0, keepdims=True)
    raised = jnp.exp(scores - top)
    return raised * (1.0 / jnp.sum(raised, axis=0, keepdims=True))


def attend_block(q, k, v, keep):
    outs = []
    for mask in head_masks(0.125):
        scores = jnp.where(keep, nt(q * mask, k), NEG)
        outs.append(nn(soft_rows(scores).astype(BF), v))
    return jnp.where(lane_low(q.shape[0]), outs[0], outs[1]).astype(BF)


def attend_block_back(q, k, v, do, keep):
    dq, dk, dv = [], [], []
    for scaled, mask in zip(head_masks(0.125), head_masks(1.0), strict=True):
        scores = jnp.where(keep, nt(k, q * scaled), NEG)
        weight = soft_cols(scores)
        dv.append(nn(weight.astype(BF), do))
        dweight = nt(v, do * mask)
        delta = jnp.sum(dweight * weight, axis=0, keepdims=True)
        dscore = (weight * (dweight - delta)).astype(BF)
        dq.append(tn(dscore, k))
        dk.append(nn(dscore, q))
    low = lane_low(q.shape[0])
    return (
        (jnp.where(low, dq[0], dq[1]) * 0.125).astype(BF),
        (jnp.where(low, dk[0], dk[1]) * 0.125).astype(BF),
        jnp.where(low, dv[0], dv[1]).astype(BF),
    )


def wide_product(a_ref, w_ref, out_ref, columns, step, w_offset=0):
    def body(i, carry):
        at = pl.multiple_of(i * step, 128)
        out_ref[:, pl.ds(at, step)] = nn(
            a_ref[...], w_ref[:, pl.ds(at + w_offset, step)]
        ).astype(BF)
        return carry

    lax.fori_loop(0, columns // step, body, 0)


def piece_copies(refs, own, weights, extra, sems):
    copies = []

    def add(src, dst):
        copies.append(pltpu.make_async_copy(src, dst, sems.at[len(copies)]))

    for core in (0, 1):
        a, b, xa, yb, a2, b2 = refs[core]
        for ref, index, relative, half in (
            (a, None, 0, 0),
            (b, None, 0, 1),
            (xa, None, 2, 0),
            (yb, None, 4, 1),
            (a2, 0, 4, 0),
            (a2, 1, 6, 0),
            (b2, 0, 2, 1),
            (b2, 1, 6, 1),
        ):
            whole = ref if index is None else ref.at[index]
            shard = own ^ (relative ^ core)
            rows = pl.ds(pl.multiple_of(shard * SHARD + half * HALF, 16), HALF)
            add(whole.at[pl.ds(0, HALF)], weights.at[rows])
            if half == 0 and extra is not None:
                add(whole.at[pl.ds(HALF, 8)], extra.at[relative ^ core])
    return copies


def temporal_forward(*refs):
    (x0, x1, x2, x3), refs = refs[:4], refs[4:]
    pieces, refs = (refs[:6], refs[6:12]), refs[12:]
    (o0, o1, o2, o3, normed_ref, packed_ref, weight_out, params_out, bias_out), refs = refs[:9], refs[9:]
    weights, extra, stack, blended, sems, out_sem = refs
    own = lax.axis_index("fsdp")
    copies = piece_copies(pieces, own, weights, extra, sems)
    for c in copies:
        c.start()
    for k, ref in enumerate((x0, x1, x2, x3)):
        stack[pl.ds(k * PIECE, PIECE), :] = ref[...]
    unit, _ = normalised(stack[...].astype(F32))
    for c in copies:
        c.wait()
    out_copy = pltpu.make_async_copy(weights, weight_out, out_sem)
    out_copy.start()
    params = extra[0].astype(F32)
    for k in range(1, 8):
        params = params + extra[k].astype(F32)
    params_out[...] = params
    for r in range(4):
        row = small_row(params, 9 + r)
        bias_out[2 * r : 2 * r + 1, :] = row[:, :384]
        bias_out[2 * r + 1 : 2 * r + 2, :] = row[:, 384:]
    normed = (unit * small_row(params, 0) + small_row(params, 3)).astype(BF)
    normed_ref[...] = nn(place_from_piece(), normed).astype(BF)
    wide_product(normed_ref, weights, packed_ref, 3 * D, 384)
    r = lax.broadcasted_iota(jnp.int32, (GROUP, GROUP), 0)
    c = lax.broadcasted_iota(jnp.int32, (GROUP, GROUP), 1)
    keep = (r >> 3) == (c >> 3)

    def heads(i, carry):
        at = pl.multiple_of(i * 128, 128)
        for t in range(SPOTS // GROUP):
            rows = pl.ds(t * GROUP, GROUP)
            blended[rows, pl.ds(at, 128)] = attend_block(
                packed_ref[rows, pl.ds(at, 128)],
                packed_ref[rows, pl.ds(at + D, 128)],
                packed_ref[rows, pl.ds(at + 2 * D, 128)],
                keep,
            )
        return carry

    lax.fori_loop(0, HEADS // 2, heads, 0)
    back = nn(piece_from_place(), blended[...]).astype(BF)
    for k, ref in enumerate((o0, o1, o2, o3)):
        ref[...] = back[k * PIECE : (k + 1) * PIECE]
    out_copy.wait()


def spatial_forward(*refs):
    (video, params_ref, o0, o1, o2, o3), refs = refs[:6], refs[6:]
    pieces, refs = (refs[:6], refs[6:12]), refs[12:]
    outs, refs = refs[:10], refs[10:]
    after_ref, normed_ref, packed_ref, blended, after_two, normed_three, blended_time, w_exit, w_entry, w_last = outs
    weights, stack, sems, out_sems = refs
    own = lax.axis_index("fsdp")
    me = lax.axis_index("frame")
    copies = piece_copies(pieces, own, weights, None, sems)
    for c in copies:
        c.start()
    params = params_ref[...]
    for k, ref in enumerate((o0, o1, o2, o3)):
        stack[pl.ds(k * PIECE, PIECE), :] = ref[...]
    blended_time[...] = nn(frame_from_piece(me), stack[...]).astype(BF)
    for c in copies:
        c.wait()
    outs_copies = [
        pltpu.make_async_copy(weights.at[:, pl.ds(0, D)], w_exit, out_sems.at[0]),
        pltpu.make_async_copy(weights.at[:, pl.ds(D, 3 * D)], w_entry, out_sems.at[1]),
        pltpu.make_async_copy(weights.at[:, pl.ds(4 * D, D)], w_last, out_sems.at[2]),
    ]
    for c in outs_copies:
        c.start()
    after = (
        video[...].astype(F32)
        + nn(blended_time[...], weights[:, 0:D])
        + small_row(params, 6)
    )
    after_ref[...] = after
    unit, _ = normalised(after)
    normed_ref[...] = (unit * small_row(params, 1) + small_row(params, 4)).astype(BF)
    wide_product(normed_ref, weights, packed_ref, 3 * D, 384, D)
    keep = lax.broadcasted_iota(jnp.int32, (FRAME_ROWS, FRAME_ROWS), 1) < PLACES

    def heads(i, carry):
        at = pl.multiple_of(i * 128, 128)
        for f in range(2):
            rows = pl.ds(f * FRAME_ROWS, FRAME_ROWS)
            blended[rows, pl.ds(at, 128)] = attend_block(
                packed_ref[rows, pl.ds(at, 128)],
                packed_ref[rows, pl.ds(at + D, 128)],
                packed_ref[rows, pl.ds(at + 2 * D, 128)],
                keep,
            )
        return carry

    lax.fori_loop(0, HEADS // 2, heads, 0)
    last = after_ref[...] + nn(blended[...], weights[:, 4 * D : 5 * D]) + small_row(params, 7)
    after_two[...] = last
    unit, _ = normalised(last)
    normed_three[...] = (unit * small_row(params, 2) + small_row(params, 5)).astype(BF)
    for c in outs_copies:
        c.wait()


def feed_forward(where, normed, after, cot, params_ref, bias, expand, contract, *refs):
    (output, grad_after, branch, keep_we, send_we, keep_wc, send_wc, small), refs = refs[:8], refs[8:]
    total, grad_normed, shuffle = refs
    step = pl.program_id(0)
    own = where[0]
    tile = own ^ step

    @pl.when(step == 0)
    def _():
        total[...] = jnp.zeros_like(total)
        grad_normed[...] = jnp.zeros_like(grad_normed)
        small[...] = jnp.zeros_like(small)

    w_in = expand[...].reshape(D, 384)
    w_out = jnp.concatenate([contract[0, 0, :, c * D : (c + 1) * D] for c in range(4)], axis=0)
    hidden = nn(normed[...], w_in) + bias[pl.ds(tile, 1), :]
    area = 0.5 + 0.5 * lax.erf(hidden * 0.7071067811865476)
    slope = area + hidden * (0.3989422804014327 * jnp.exp(-0.5 * hidden * hidden))
    active = (hidden * area).astype(BF)
    top = cot[...]
    total[...] += nn(active, w_out)
    grad_hidden = (nt(top, w_out) * slope).astype(BF)
    grad_normed[...] += nt(grad_hidden, w_in)
    small[pl.ds(9 + tile // 2, 1), pl.ds(pl.multiple_of((tile % 2) * 384, 128), 384)] = jnp.sum(
        grad_hidden.astype(F32), axis=0, keepdims=True
    )
    grad_out = tn(active, top).astype(BF)
    for parity, ref in ((0, keep_wc), (1, send_wc)):

        @pl.when(step % 2 == parity)
        def _(ref=ref):
            for c in range(4):
                ref[0, :, c * D : (c + 1) * D] = grad_out[c * SHARD : (c + 1) * SHARD]

    shuffle[...] = tn(normed[...], grad_hidden)
    for j in range(4):
        for parity, ref in ((0, keep_we), (1, send_we)):
            rows = pl.ds(pl.multiple_of((own ^ (2 * j + parity)) * SHARD, 8), SHARD)
            ref[j] = shuffle[rows, :].astype(BF)

    @pl.when(step == pl.num_programs(0) - 1)
    def _():
        params = params_ref[...]
        values = after[...]
        output[...] = (values + (total[...] + small_row(params, 8))).astype(BF)
        unit, scale = normalised(values)
        dn = grad_normed[...].astype(BF).astype(F32)
        inner, dgain, dshift = norm_back(dn, unit, scale, small_row(params, 2))
        top32 = cot[...].astype(F32)
        dafter = top32 + inner
        grad_after[...] = dafter
        branch[...] = dafter.astype(BF)
        small[2:3, :] = dgain
        small[5:6, :] = dshift
        small[8:9, :] = jnp.sum(top32, axis=0, keepdims=True)


def spatial_back(branch, packed, w_last, grad_packed, grad_blended):
    grad_blended[...] = nt(branch[...], w_last[...]).astype(BF)
    keep = lax.broadcasted_iota(jnp.int32, (FRAME_ROWS, FRAME_ROWS), 0) < PLACES

    def heads(i, carry):
        at = pl.multiple_of(i * 128, 128)
        for f in range(2):
            rows = pl.ds(f * FRAME_ROWS, FRAME_ROWS)
            dq, dk, dv = attend_block_back(
                packed[rows, pl.ds(at, 128)],
                packed[rows, pl.ds(at + D, 128)],
                packed[rows, pl.ds(at + 2 * D, 128)],
                grad_blended[rows, pl.ds(at, 128)],
                keep,
            )
            grad_packed[rows, pl.ds(at, 128)] = dq
            grad_packed[rows, pl.ds(at + D, 128)] = dk
            grad_packed[rows, pl.ds(at + 2 * D, 128)] = dv
        return carry

    lax.fori_loop(0, HEADS // 2, heads, 0)


def spatial_back_norm(*refs):
    grad_packed, branch, grad_after, after, params_ref, small_in, w_entry, w_exit = refs[:8]
    grad_first, branch_first, d0, d1, d2, d3, small = refs[8:]
    me = lax.axis_index("frame")
    params = params_ref[...]
    dn = nt(grad_packed[...], w_entry[...]).astype(BF).astype(F32)
    unit, scale = normalised(after[...])
    inner, dgain, dshift = norm_back(dn, unit, scale, small_row(params, 1))
    first = grad_after[...] + inner
    grad_first[...] = first
    low = first.astype(BF)
    branch_first[...] = low
    back = nt(low, w_exit[...]).astype(BF)
    pieces = nn(piece_from_frame(me), back).astype(BF)
    for k, ref in enumerate((d0, d1, d2, d3)):
        ref[...] = pieces[k * PIECE : (k + 1) * PIECE]
    small[...] = small_in[...]
    small[1:2, :] = dgain
    small[4:5, :] = dshift
    small[6:7, :] = jnp.sum(low.astype(F32), axis=0, keepdims=True)
    small[7:8, :] = jnp.sum(branch[...].astype(F32), axis=0, keepdims=True)


def temporal_back(*refs):
    xs, gs, refs = refs[:4], refs[4:8], refs[8:]
    packed, params_ref, small_in, weights = refs[:4]
    grad_packed, n0, n1, n2, n3, small = refs[4:10]
    stack, grads = refs[10:]
    params = params_ref[...]
    for k, ref in enumerate(gs):
        stack[pl.ds(k * PIECE, PIECE), :] = ref[...]
    grads[...] = nn(place_from_piece(), stack[...]).astype(BF)
    r = lax.broadcasted_iota(jnp.int32, (GROUP, GROUP), 0)
    c = lax.broadcasted_iota(jnp.int32, (GROUP, GROUP), 1)
    keep = (r >> 3) == (c >> 3)

    def heads(i, carry):
        at = pl.multiple_of(i * 128, 128)
        for t in range(SPOTS // GROUP):
            rows = pl.ds(t * GROUP, GROUP)
            dq, dk, dv = attend_block_back(
                packed[rows, pl.ds(at, 128)],
                packed[rows, pl.ds(at + D, 128)],
                packed[rows, pl.ds(at + 2 * D, 128)],
                grads[rows, pl.ds(at, 128)],
                keep,
            )
            grad_packed[rows, pl.ds(at, 128)] = dq
            grad_packed[rows, pl.ds(at + D, 128)] = dk
            grad_packed[rows, pl.ds(at + 2 * D, 128)] = dv
        return carry

    lax.fori_loop(0, HEADS // 2, heads, 0)
    dn = nt(grad_packed[...], weights[...]).astype(BF)
    pieces = nn(piece_from_place(), dn)
    low = pieces.astype(BF)
    for k, ref in enumerate((n0, n1, n2, n3)):
        ref[...] = low[k * PIECE : (k + 1) * PIECE]
    for k, ref in enumerate(xs):
        stack[pl.ds(k * PIECE, PIECE), :] = ref[...]
    unit, _ = normalised(stack[...].astype(F32))
    small[...] = small_in[...]
    small[0:1, :] = jnp.sum(pieces * unit, axis=0, keepdims=True)
    small[3:4, :] = jnp.sum(pieces, axis=0, keepdims=True)


def input_back(video, grad_first, params_ref, n0, n1, n2, n3, out, stack):
    me = lax.axis_index("frame")
    for k, ref in enumerate((n0, n1, n2, n3)):
        stack[pl.ds(k * PIECE, PIECE), :] = ref[...]
    dn = nn(frame_from_piece(me), stack[...])
    unit, scale = normalised(video[...].astype(F32))
    moved = dn * small_row(params_ref[...], 0)
    inner = scale * (
        moved
        - jnp.mean(moved, axis=-1, keepdims=True)
        - unit * jnp.mean(moved * unit, axis=-1, keepdims=True)
    )
    out[...] = grad_first[...] + inner


def weight_grads(where, a_one, b_one, a_two, b_two, keep, send, shuffle):
    step = pl.program_id(0)
    own = where[0]

    @pl.when(step < 2)
    def _():
        shuffle[...] = tn(a_one[...], b_one[...])

    @pl.when(step >= 2)
    def _():
        shuffle[...] = tn(a_two[...], b_two[...])

    for j in range(4):
        for parity, ref in ((0, keep), (1, send)):
            rows = pl.ds(pl.multiple_of((own ^ (2 * j + parity)) * SHARD, 8), SHARD)
            ref[j] = shuffle[rows, :].astype(BF)


def shape(*dims, dtype=BF):
    return jax.ShapeDtypeStruct(dims, dtype)


def cost(flops, nbytes, exps=0):
    return pl.CostEstimate(flops=int(flops), bytes_accessed=int(nbytes), transcendentals=int(exps))


def limit(mebibytes):
    return pltpu.CompilerParams(vmem_limit_bytes=mebibytes << 20)


CORE = [(i, i ^ 1) for i in range(8)]
ACROSS = [(i, i ^ 2) for i in range(8)]
UP = [(i, i ^ 4) for i in range(8)]
NEAR = [(i, i ^ 1) for i in range(4)]
FAR = [(i, i ^ 2) for i in range(4)]


def swap(value, pairs, axis="fsdp"):
    return lax.ppermute(value, axis, pairs)


def shift(value, by):
    return lax.ppermute(value, "frame", [(i, (i + by) % 4) for i in range(4)])


def gather_pieces(first, second):
    first_x = swap(first, ACROSS)
    second_y = swap(second, UP)
    first_two = swap(jnp.stack([first, first_x]), UP)
    second_two = swap(jnp.stack([second, second_y]), ACROSS)
    mine = (first, second, first_x, second_y, first_two, second_two)
    return mine + tuple(swap(v, CORE) for v in mine)


def reduce_shards(keep, send, frame):
    got = [swap(v, CORE) for v in send]
    sums = [k.astype(F32) + g.astype(F32) for k, g in zip(keep, got, strict=True)]
    stack = lambda parts: jnp.stack(parts)
    for_x = stack([t[j, :HALF] for t in sums for j in (1, 3)]).astype(BF)
    for_y = stack([t[j, HALF:] for t in sums for j in (2, 3)]).astype(BF)
    from_x = swap(for_x, ACROSS).astype(F32)
    from_y = swap(for_y, UP).astype(F32)
    count = len(keep)
    next_y = stack([sums[i][2, :HALF] + from_x[2 * i + 1] for i in range(count)]).astype(BF)
    next_x = stack([sums[i][1, HALF:] + from_y[2 * i + 1] for i in range(count)]).astype(BF)
    got_y = swap(next_y, UP).astype(F32)
    got_x = swap(next_x, ACROSS).astype(F32)
    first = stack([sums[i][0, :HALF] + from_x[2 * i] + got_y[i] for i in range(count)])
    second = stack([sums[i][0, HALF:] + from_y[2 * i] + got_x[i] for i in range(count)])
    odd = (frame & 1) == 1
    out = jnp.where(odd, first, second).astype(BF)
    held = jnp.where(odd, second, first)
    pair = (held + swap(out, NEAR, "frame").astype(F32)).astype(BF)
    full = (pair.astype(F32) + swap(pair, FAR, "frame").astype(F32)).astype(BF)
    other = swap(full, NEAR, "frame")
    low = jnp.where(odd, other, full)
    high = jnp.where(odd, full, other)
    return [
        jnp.concatenate([low[i], high[i]], axis=0).astype(F32) for i in range(count)
    ]


def reduce_small(small):
    for pairs in (CORE, ACROSS, UP):
        small = small + swap(small, pairs)
    for pairs in (NEAR, FAR):
        small = small + swap(small, pairs, "frame")
    return small


def spread(shard, own, width):
    lanes = jnp.arange(8 * width) // width
    return jnp.where((lanes == own)[None, :], jnp.tile(shard, (1, 8)), jnp.zeros((), shard.dtype))


def body(
    video,
    temporal_entry,
    temporal_exit,
    spatial_entry,
    spatial_exit,
    expand_weight,
    contract_weight,
    layer_gains,
    layer_shifts,
    branch_biases,
    expand_bias,
    cotangent,
):
    own = lax.axis_index("fsdp")
    frame = lax.axis_index("frame")
    where = jnp.stack([own, frame]).astype(jnp.int32)

    contract_rows = contract_weight.reshape(4, SHARD, D).transpose(1, 0, 2).reshape(SHARD, WIDE)
    forward_weights = lax.all_gather(
        jnp.concatenate([expand_weight, contract_rows], axis=0), "fsdp", axis=0, tiled=True
    ).reshape(8, 2, SHARD, WIDE)

    small_rows = jnp.concatenate(
        [
            spread(layer_gains, own, SHARD),
            spread(layer_shifts, own, SHARD),
            spread(branch_biases, own, SHARD),
            spread(expand_bias.reshape(1, 384), own, 384).reshape(4, D),
            jnp.zeros((11, D), BF),
        ],
        axis=0,
    )
    small_rows = jnp.concatenate([small_rows[0:8], small_rows[8:16], small_rows[16:24]], axis=1)
    entry_pieces = gather_pieces(
        jnp.concatenate([temporal_entry[:HALF], small_rows], axis=0), temporal_entry[HALF:]
    )
    plane = jnp.concatenate([temporal_exit, spatial_entry, spatial_exit], axis=1)

    by_place = jnp.pad(
        video.reshape(2, 4, HERE, D).transpose(1, 0, 2, 3).reshape(4, 2 * HERE, D),
        ((0, 0), (0, PIECE - 2 * HERE), (0, 0)),
    )
    pick = lambda k: lax.dynamic_index_in_dim(by_place, (frame + k) & 3, keepdims=False)
    video_pieces = [pick(0)] + [shift(pick(k), k) for k in (1, 2, 3)]
    pad_rows = lambda v: jnp.pad(
        v.reshape(2, PLACES, D), ((0, 0), (0, FRAME_ROWS - PLACES), (0, 0))
    ).reshape(ROWS, D)
    tokens = pad_rows(video)
    cot = pad_rows(cotangent)

    forward = pl.pallas_call(
        temporal_forward,
        name="temporal_forward",
        out_shape=[shape(PIECE, D)] * 4
        + [
            shape(SPOTS, D),
            shape(SPOTS, 3 * D),
            shape(D, 3 * D),
            shape(8, 3 * D, dtype=F32),
            shape(8, 384, dtype=F32),
        ],
        in_specs=[VMEM] * 4 + [HBM] * 12,
        out_specs=[VMEM] * 6 + [HBM] + [VMEM] * 2,
        scratch_shapes=[
            pltpu.VMEM((D, 3 * D), BF),
            pltpu.VMEM((8, 8, 3 * D), BF),
            pltpu.VMEM((ROWS, D), BF),
            pltpu.VMEM((SPOTS, D), BF),
            pltpu.SemaphoreType.DMA((24,)),
            pltpu.SemaphoreType.DMA,
        ],
        compiler_params=limit(32),
        cost_estimate=cost(3e9, 12e6, 2e6),
    )(*video_pieces, *entry_pieces)
    places, (normed_place, packed_place, entry_full, params, bias_full) = forward[:4], forward[4:]
    blended_pieces = [places[0]] + [shift(places[k], -k) for k in (1, 2, 3)]

    plane_pieces = gather_pieces(plane[:HALF], plane[HALF:])
    (
        after_time,
        normed_two,
        packed_space,
        blended_space,
        after_space,
        normed_three,
        blended_time,
        exit_full,
        space_full,
        last_full,
    ) = pl.pallas_call(
        spatial_forward,
        name="spatial_forward",
        out_shape=[
            shape(ROWS, D, dtype=F32),
            shape(ROWS, D),
            shape(ROWS, 3 * D),
            shape(ROWS, D),
            shape(ROWS, D, dtype=F32),
            shape(ROWS, D),
            shape(ROWS, D),
            shape(D, D),
            shape(D, 3 * D),
            shape(D, D),
        ],
        in_specs=[VMEM] * 6 + [HBM] * 12,
        out_specs=[VMEM] * 7 + [HBM] * 3,
        scratch_shapes=[
            pltpu.VMEM((D, 5 * D), BF),
            pltpu.VMEM((ROWS, D), BF),
            pltpu.SemaphoreType.DMA((16,)),
            pltpu.SemaphoreType.DMA((3,)),
        ],
        compiler_params=limit(36),
        cost_estimate=cost(6e9, 20e6, 2e6),
    )(tokens, params, *blended_pieces, *plane_pieces)

    whole = lambda *dims: pl.BlockSpec(dims, lambda i, w: (0,) * len(dims))
    (
        output,
        grad_after,
        branch_last,
        keep_we,
        send_we,
        keep_wc,
        send_wc,
        small,
    ) = pl.pallas_call(
        feed_forward,
        name="feed_forward",
        out_shape=[
            shape(ROWS, D),
            shape(ROWS, D, dtype=F32),
            shape(ROWS, D),
            shape(4, SHARD, WIDE),
            shape(4, SHARD, WIDE),
            shape(4, SHARD, WIDE),
            shape(4, SHARD, WIDE),
            shape(16, D, dtype=F32),
        ],
        grid_spec=pltpu.PrefetchScalarGridSpec(
            num_scalar_prefetch=1,
            grid=(8,),
            in_specs=[
                whole(ROWS, D),
                whole(ROWS, D),
                whole(ROWS, D),
                whole(8, 3 * D),
                whole(8, 384),
                pl.BlockSpec((8, None, SHARD, 384), lambda i, w: (0, 0, 0, w[0] ^ i)),
                pl.BlockSpec((1, 1, SHARD, WIDE), lambda i, w: (w[0] ^ i, 1, 0, 0)),
            ],
            out_specs=[
                whole(ROWS, D),
                whole(ROWS, D),
                whole(ROWS, D),
                pl.BlockSpec((4, SHARD, 384), lambda i, w: (0, 0, w[0] ^ i)),
                pl.BlockSpec((4, SHARD, 384), lambda i, w: (0, 0, w[0] ^ i)),
                pl.BlockSpec((1, SHARD, WIDE), lambda i, w: (i // 2, 0, 0)),
                pl.BlockSpec((1, SHARD, WIDE), lambda i, w: (i // 2, 0, 0)),
                whole(16, D),
            ],
            scratch_shapes=[
                pltpu.VMEM((ROWS, D), F32),
                pltpu.VMEM((ROWS, D), F32),
                pltpu.VMEM((D, 384), F32),
            ],
        ),
        compiler_params=limit(40),
        cost_estimate=cost(12e9, 30e6, 4e6),
    )(where, normed_three, after_space, cot, params, bias_full, forward_weights, forward_weights)
    sums_forward = reduce_shards([keep_we, keep_wc], [send_we, send_wc], frame)

    grad_packed = pl.pallas_call(
        spatial_back,
        name="spatial_back",
        out_shape=shape(ROWS, 3 * D),
        in_specs=[VMEM] * 3,
        out_specs=VMEM,
        scratch_shapes=[pltpu.VMEM((ROWS, D), BF)],
        compiler_params=limit(24),
        cost_estimate=cost(3e9, 6e6, 2e6),
    )(branch_last, packed_space, last_full)
    back = pl.pallas_call(
        spatial_back_norm,
        name="spatial_back_norm",
        out_shape=[shape(ROWS, D, dtype=F32), shape(ROWS, D)]
        + [shape(PIECE, D)] * 4
        + [shape(16, D, dtype=F32)],
        in_specs=[VMEM] * 8,
        out_specs=[VMEM] * 7,
        compiler_params=limit(32),
        cost_estimate=cost(3e9, 12e6, 0),
    )(grad_packed, branch_last, grad_after, after_time, params, small, space_full, exit_full)
    grad_first, branch_first, back_pieces, small = back[0], back[1], back[2:6], back[6]
    grad_pieces = [back_pieces[0]] + [shift(back_pieces[k], k) for k in (1, 2, 3)]

    def grads(a_one, b_one, a_two, b_two):
        return pl.pallas_call(
            weight_grads,
            name="weight_grads",
            out_shape=[shape(4, SHARD, WIDE)] * 2,
            grid_spec=pltpu.PrefetchScalarGridSpec(
                num_scalar_prefetch=1,
                grid=(8,),
                in_specs=[
                    whole(*a_one.shape),
                    pl.BlockSpec((b_one.shape[0], 384), lambda i, w: (0, jnp.minimum(i, 1))),
                    whole(*a_two.shape),
                    pl.BlockSpec((b_two.shape[0], 384), lambda i, w: (0, jnp.maximum(i - 2, 0))),
                ],
                out_specs=[pl.BlockSpec((4, SHARD, 384), lambda i, w: (0, 0, i))] * 2,
                scratch_shapes=[pltpu.VMEM((D, 384), F32)],
            ),
            compiler_params=limit(24),
            cost_estimate=cost(2e9, 10e6, 0),
        )(where, a_one, b_one, a_two, b_two)

    keep_space, send_space = grads(blended_space, branch_last, normed_two, grad_packed)
    sums_space = reduce_shards([keep_space], [send_space], frame)[0]

    back = pl.pallas_call(
        temporal_back,
        name="temporal_back",
        out_shape=[shape(SPOTS, 3 * D)] + [shape(PIECE, D)] * 4 + [shape(16, D, dtype=F32)],
        in_specs=[VMEM] * 12,
        out_specs=[VMEM] * 6,
        scratch_shapes=[pltpu.VMEM((ROWS, D), BF), pltpu.VMEM((SPOTS, D), BF)],
        compiler_params=limit(32),
        cost_estimate=cost(4e9, 10e6, 2e6),
    )(*video_pieces, *grad_pieces, packed_place, params, small, entry_full)
    grad_place, normed_pieces, small = back[0], back[1:5], back[5]
    normed_back = [normed_pieces[0]] + [shift(normed_pieces[k], -k) for k in (1, 2, 3)]

    keep_time, send_time = grads(blended_time, branch_first, normed_place, grad_place)
    sums_time = reduce_shards([keep_time], [send_time], frame)[0]
    small = reduce_small(small)

    input_grad = pl.pallas_call(
        input_back,
        name="input_back",
        out_shape=shape(ROWS, D, dtype=F32),
        in_specs=[VMEM] * 7,
        out_specs=VMEM,
        scratch_shapes=[pltpu.VMEM((ROWS, D), BF)],
        compiler_params=limit(24),
        cost_estimate=cost(1e9, 5e6, 0),
    )(tokens, grad_first, params, *normed_back)

    drop = lambda v: v.reshape(2, FRAME_ROWS, D)[:, :PLACES].reshape(video.shape)
    mine = lax.dynamic_slice_in_dim(small[:9], own * SHARD, SHARD, axis=1)
    return (
        drop(output),
        drop(input_grad),
        sums_time[:, D:],
        sums_time[:, :D],
        sums_space[:, D:],
        sums_space[:, :D],
        sums_forward[0],
        sums_forward[1].reshape(SHARD, 4, D).transpose(1, 0, 2).reshape(384, D),
        mine[0:3],
        mine[3:6],
        mine[6:9],
        lax.dynamic_slice_in_dim(small[9:13].reshape(WIDE), own * 384, 384),
    )


def solution(mesh):
    placed = (
        P("fsdp", "frame", None, None),
        P("fsdp", None),
        P("fsdp", None),
        P("fsdp", None),
        P("fsdp", None),
        P("fsdp", None),
        P("fsdp", None),
        P(None, "fsdp"),
        P(None, "fsdp"),
        P(None, "fsdp"),
        P("fsdp"),
        P("fsdp", "frame", None, None),
    )
    special = mesh.shape["fsdp"] == 8 and mesh.shape["frame"] == 4
    return jax.shard_map(
        body if special else general_body,
        mesh=mesh,
        in_specs=placed,
        out_specs=(
            P("fsdp", "frame", None, None),
            P("fsdp", "frame", None, None),
            P("fsdp", None),
            P("fsdp", None),
            P("fsdp", None),
            P("fsdp", None),
            P("fsdp", None),
            P("fsdp", None),
            P(None, "fsdp"),
            P(None, "fsdp"),
            P(None, "fsdp"),
            P("fsdp"),
        ),
        check_vma=False,
    )
```

```python
import functools

import jax
import jax.numpy as jnp
from jax import lax
from jax.experimental import pallas as pl
from jax.experimental.pallas import tpu as pltpu
from jax.sharding import PartitionSpec as P

HEADS = 12


norm_eps = 1e-05


def layer_norm(values, norm_gain, norm_shift):
    average = jnp.mean(values, axis=-1, keepdims=True)
    centred = values - average
    variance = jnp.mean(centred * centred, axis=-1, keepdims=True)
    return centred * lax.rsqrt(variance + norm_eps) * norm_gain + norm_shift


def rounded(values):
    return lax.optimization_barrier(values.astype(jnp.bfloat16)).astype(jnp.float32)


def dense(first_op, second_op):
    return jnp.dot(first_op, second_op, preferred_element_type=jnp.float32)


def dense_left(first_op, second_op):
    return lax.dot_general(
        first_op, second_op, (((0,), (0,)), ((), ())), preferred_element_type=jnp.float32
    )


def dense_right(first_op, second_op):
    return lax.dot_general(
        first_op, second_op, (((1,), (1,)), ((), ())), preferred_element_type=jnp.float32
    )


def split_heads(packed):
    outer = packed.shape
    parted = packed.reshape(outer[:-1] + (3, HEADS, outer[-1] // (3 * HEADS)))
    return (parted[..., 0, :, :], parted[..., 1, :, :], parted[..., 2, :, :])


def attend_forward(packed, layout):
    key_layout = layout.replace("l", "m")
    queries, key_rows, values = split_heads(packed)
    factor = queries.shape[-1] ** (-0.5)
    scores = (
        jnp.einsum(
            layout + "hd," + key_layout + "hd->cqhlm",
            queries,
            key_rows,
            preferred_element_type=jnp.float32,
        )
        * factor
    )
    highest = jnp.max(scores, axis=-1, keepdims=True)
    raised = jnp.exp(scores - highest)
    row_totals = jnp.sum(raised, axis=-1, keepdims=True)
    attention = (raised / row_totals).astype(jnp.bfloat16)
    blended = jnp.einsum(
        "cqhlm," + key_layout + "hd->" + layout + "hd",
        attention,
        values,
        preferred_element_type=jnp.float32,
    )
    outer = packed.shape
    return (
        blended.reshape(outer[:-1] + (outer[-1] // 3,)).astype(jnp.bfloat16),
        highest + jnp.log(row_totals),
    )


def attend_backward(packed, logsum, grad_blended, layout):
    key_layout = layout.replace("l", "m")
    queries, key_rows, values = split_heads(packed)
    factor = queries.shape[-1] ** (-0.5)
    outer = grad_blended.shape
    grad_heads = grad_blended.reshape(outer[:-1] + (HEADS, outer[-1] // HEADS))
    scores = (
        jnp.einsum(
            layout + "hd," + key_layout + "hd->cqhlm",
            queries,
            key_rows,
            preferred_element_type=jnp.float32,
        )
        * factor
    )
    attention = jnp.exp(scores - logsum)
    grad_values = jnp.einsum(
        "cqhlm," + layout + "hd->" + key_layout + "hd",
        attention.astype(jnp.bfloat16),
        grad_heads,
        preferred_element_type=jnp.float32,
    )
    grad_attention = jnp.einsum(
        layout + "hd," + key_layout + "hd->cqhlm",
        grad_heads,
        values,
        preferred_element_type=jnp.float32,
    )
    grad_scores = (
        attention * (grad_attention - jnp.sum(grad_attention * attention, axis=-1, keepdims=True))
    ).astype(jnp.bfloat16)
    grad_queries = (
        jnp.einsum(
            "cqhlm," + key_layout + "hd->" + layout + "hd",
            grad_scores,
            key_rows,
            preferred_element_type=jnp.float32,
        )
        * factor
    )
    grad_keys = (
        jnp.einsum(
            "cqhlm," + layout + "hd->" + key_layout + "hd",
            grad_scores,
            queries,
            preferred_element_type=jnp.float32,
        )
        * factor
    )
    stacked = jnp.stack([grad_queries, grad_keys, grad_values], axis=-3)
    return stacked.reshape(packed.shape).astype(jnp.bfloat16)


def general_body(
    video,
    temporal_entry,
    temporal_exit,
    spatial_entry,
    spatial_exit,
    expand_weight,
    contract_weight,
    layer_gains,
    layer_shifts,
    branch_biases,
    expand_bias,
    cotangent,
):
    clips_here, frames_here, places, model_width = video.shape
    rows_shape = (clips_here, frames_here, places)
    entry_time, exit_time, entry_space, exit_space, gains_low, shifts_low, biases_low = (
        lax.all_gather(temporal_entry, "fsdp", axis=0, tiled=True),
        lax.all_gather(temporal_exit, "fsdp", axis=0, tiled=True),
        lax.all_gather(spatial_entry, "fsdp", axis=0, tiled=True),
        lax.all_gather(spatial_exit, "fsdp", axis=0, tiled=True),
        lax.all_gather(layer_gains, "fsdp", axis=1, tiled=True),
        lax.all_gather(layer_shifts, "fsdp", axis=1, tiled=True),
        lax.all_gather(branch_biases, "fsdp", axis=1, tiled=True),
    )
    expand_full, contract_full, expand_bias_full = (
        lax.all_gather(expand_weight, "fsdp", axis=0, tiled=True),
        lax.all_gather(contract_weight, "fsdp", axis=0, tiled=True),
        lax.all_gather(expand_bias, "fsdp", axis=0, tiled=True),
    )
    gains = gains_low.astype(jnp.float32)
    shifts = shifts_low.astype(jnp.float32)
    biases = biases_low.astype(jnp.float32)
    tokens = video.astype(jnp.float32).reshape(-1, model_width)
    normed_one = layer_norm(tokens, gains[0], shifts[0]).astype(jnp.bfloat16)
    packed_frame = dense(normed_one, entry_time).astype(jnp.bfloat16)
    packed_place = lax.all_to_all(
        packed_frame.reshape(rows_shape + (3 * model_width,)),
        "frame",
        split_axis=2,
        concat_axis=1,
        tiled=True,
    )
    blended_place, logsum_time = attend_forward(packed_place, "clq")
    blended_time = lax.all_to_all(
        blended_place, "frame", split_axis=1, concat_axis=2, tiled=True
    ).reshape(-1, model_width)
    after_time = tokens + (dense(blended_time, exit_time) + biases[0])
    normed_two = layer_norm(after_time, gains[1], shifts[1]).astype(jnp.bfloat16)
    packed_space = (
        dense(normed_two, entry_space).astype(jnp.bfloat16).reshape(rows_shape + (3 * model_width,))
    )
    blended_space, logsum_space = attend_forward(packed_space, "cql")
    blended_rows = blended_space.reshape(-1, model_width)
    after_space = after_time + (dense(blended_rows, exit_space) + biases[1])
    normed_three = layer_norm(after_space, gains[2], shifts[2]).astype(jnp.bfloat16)
    hidden = dense(normed_three, expand_full) + expand_bias_full.astype(jnp.float32)
    active = jax.nn.gelu(hidden, approximate=False).astype(jnp.bfloat16)
    layer_output = (
        (after_space + (dense(active, contract_full) + biases[2]))
        .astype(jnp.bfloat16)
        .reshape(video.shape)
    )
    grad_top = cotangent.astype(jnp.float32).reshape(-1, model_width)
    grad_branch = grad_top.astype(jnp.bfloat16)
    grad_bias_last = jnp.sum(grad_branch.astype(jnp.float32), axis=0)
    grad_contract = dense_left(active, grad_branch)
    grad_active = dense_right(grad_branch, contract_full)
    gelu_pull = jax.vjp(lambda inner: jax.nn.gelu(inner, approximate=False), hidden)[1]
    grad_hidden = gelu_pull(grad_active)[0].astype(jnp.bfloat16)
    grad_expand = dense_left(normed_three, grad_hidden)
    grad_expand_bias = jnp.sum(grad_hidden.astype(jnp.float32), axis=0)
    grad_normed = rounded(dense_right(grad_hidden, expand_full))
    norm_pull = jax.vjp(layer_norm, after_space, gains[2], shifts[2])[1]
    grad_inner, grad_gain_last, grad_shift_last = norm_pull(grad_normed)
    grad_after_space = grad_top + grad_inner
    mlp_parts = (
        lax.psum_scatter(grad_expand, "fsdp", scatter_dimension=0, tiled=True),
        lax.psum_scatter(grad_contract, "fsdp", scatter_dimension=0, tiled=True),
        lax.psum_scatter(grad_expand_bias, "fsdp", scatter_dimension=0, tiled=True),
    )
    grad_branch = grad_after_space.astype(jnp.bfloat16)
    grad_bias_space = jnp.sum(grad_branch.astype(jnp.float32), axis=0)
    grad_exit_space = dense_left(blended_rows, grad_branch)
    grad_blended = (
        dense_right(grad_branch, exit_space)
        .astype(jnp.bfloat16)
        .reshape(rows_shape + (model_width,))
    )
    grad_packed = attend_backward(packed_space, logsum_space, grad_blended, "cql").reshape(
        -1, 3 * model_width
    )
    grad_entry_space = dense_left(normed_two, grad_packed)
    grad_normed = rounded(dense_right(grad_packed, entry_space))
    norm_pull = jax.vjp(layer_norm, after_time, gains[1], shifts[1])[1]
    grad_inner, grad_gain_space, grad_shift_space = norm_pull(grad_normed)
    grad_after_time = grad_after_space + grad_inner
    grad_branch = grad_after_time.astype(jnp.bfloat16)
    grad_bias_time = jnp.sum(grad_branch.astype(jnp.float32), axis=0)
    grad_exit_time = dense_left(blended_time, grad_branch)
    grad_blended = (
        dense_right(grad_branch, exit_time)
        .astype(jnp.bfloat16)
        .reshape(rows_shape + (model_width,))
    )
    grad_blended_place = lax.all_to_all(
        grad_blended, "frame", split_axis=2, concat_axis=1, tiled=True
    )
    grad_packed_place = attend_backward(packed_place, logsum_time, grad_blended_place, "clq")
    grad_packed_frame = lax.all_to_all(
        grad_packed_place, "frame", split_axis=1, concat_axis=2, tiled=True
    ).reshape(-1, 3 * model_width)
    grad_entry_time = dense_left(normed_one, grad_packed_frame)
    grad_normed_one = rounded(dense_right(grad_packed_frame, entry_time))
    norm_pull = jax.vjp(layer_norm, tokens, gains[0], shifts[0])[1]
    grad_inner, grad_gain_time, grad_shift_time = norm_pull(grad_normed_one)
    input_grad = (grad_after_time + grad_inner).reshape(video.shape)
    grad_gains = jnp.stack([grad_gain_time, grad_gain_space, grad_gain_last])
    grad_shifts = jnp.stack([grad_shift_time, grad_shift_space, grad_shift_last])
    grad_biases = jnp.stack([grad_bias_time, grad_bias_space, grad_bias_last])
    attention_parts = (
        lax.psum_scatter(grad_entry_time, "fsdp", scatter_dimension=0, tiled=True),
        lax.psum_scatter(grad_exit_time, "fsdp", scatter_dimension=0, tiled=True),
        lax.psum_scatter(grad_entry_space, "fsdp", scatter_dimension=0, tiled=True),
        lax.psum_scatter(grad_exit_space, "fsdp", scatter_dimension=0, tiled=True),
        lax.psum_scatter(grad_gains, "fsdp", scatter_dimension=1, tiled=True),
        lax.psum_scatter(grad_shifts, "fsdp", scatter_dimension=1, tiled=True),
        lax.psum_scatter(grad_biases, "fsdp", scatter_dimension=1, tiled=True),
    )
    shares = (
        lax.psum_scatter(
            attention_parts[0].astype(jnp.bfloat16), "frame", scatter_dimension=0, tiled=True
        ).astype(jnp.float32),
        lax.psum_scatter(
            attention_parts[1].astype(jnp.bfloat16), "frame", scatter_dimension=0, tiled=True
        ).astype(jnp.float32),
        lax.psum_scatter(
            attention_parts[2].astype(jnp.bfloat16), "frame", scatter_dimension=0, tiled=True
        ).astype(jnp.float32),
        lax.psum_scatter(
            attention_parts[3].astype(jnp.bfloat16), "frame", scatter_dimension=0, tiled=True
        ).astype(jnp.float32),
        lax.psum_scatter(
            mlp_parts[0].astype(jnp.bfloat16), "frame", scatter_dimension=0, tiled=True
        ).astype(jnp.float32),
        lax.psum_scatter(
            mlp_parts[1].astype(jnp.bfloat16), "frame", scatter_dimension=0, tiled=True
        ).astype(jnp.float32),
        lax.psum_scatter(
            jnp.moveaxis(attention_parts[4], 0, 1).astype(jnp.bfloat16),
            "frame",
            scatter_dimension=0,
            tiled=True,
        ).astype(jnp.float32),
        lax.psum_scatter(
            jnp.moveaxis(attention_parts[5], 0, 1).astype(jnp.bfloat16),
            "frame",
            scatter_dimension=0,
            tiled=True,
        ).astype(jnp.float32),
        lax.psum_scatter(
            jnp.moveaxis(attention_parts[6], 0, 1).astype(jnp.bfloat16),
            "frame",
            scatter_dimension=0,
            tiled=True,
        ).astype(jnp.float32),
        lax.psum_scatter(
            mlp_parts[2].astype(jnp.bfloat16), "frame", scatter_dimension=0, tiled=True
        ).astype(jnp.float32),
    )
    pieces = (
        lax.all_gather(shares[0].astype(jnp.bfloat16), "frame", axis=0, tiled=True).astype(
            jnp.float32
        ),
        lax.all_gather(shares[1].astype(jnp.bfloat16), "frame", axis=0, tiled=True).astype(
            jnp.float32
        ),
        lax.all_gather(shares[2].astype(jnp.bfloat16), "frame", axis=0, tiled=True).astype(
            jnp.float32
        ),
        lax.all_gather(shares[3].astype(jnp.bfloat16), "frame", axis=0, tiled=True).astype(
            jnp.float32
        ),
        lax.all_gather(shares[4].astype(jnp.bfloat16), "frame", axis=0, tiled=True).astype(
            jnp.float32
        ),
        lax.all_gather(shares[5].astype(jnp.bfloat16), "frame", axis=0, tiled=True).astype(
            jnp.float32
        ),
        lax.all_gather(shares[6].astype(jnp.bfloat16), "frame", axis=0, tiled=True).astype(
            jnp.float32
        ),
        lax.all_gather(shares[7].astype(jnp.bfloat16), "frame", axis=0, tiled=True).astype(
            jnp.float32
        ),
        lax.all_gather(shares[8].astype(jnp.bfloat16), "frame", axis=0, tiled=True).astype(
            jnp.float32
        ),
        lax.all_gather(shares[9].astype(jnp.bfloat16), "frame", axis=0, tiled=True).astype(
            jnp.float32
        ),
    )
    totals = (
        pieces[0],
        pieces[1],
        pieces[2],
        pieces[3],
        pieces[4],
        pieces[5],
        jnp.moveaxis(pieces[6], 0, 1),
        jnp.moveaxis(pieces[7], 0, 1),
        jnp.moveaxis(pieces[8], 0, 1),
        pieces[9],
    )
    return (
        layer_output,
        input_grad,
        totals[0],
        totals[1],
        totals[2],
        totals[3],
        totals[4],
        totals[5],
        totals[6],
        totals[7],
        totals[8],
        totals[9],
    )


BF = jnp.bfloat16
F32 = jnp.float32
D = 768
FRAME_ROWS = 208
PLACES = 196
HERE = 49
PIECE = 104
ROWS = 416
SPOTS = 400
GROUP = 80
SHARD = 96
HALF = 48
WIDE = 3072
NEG = -1e30
HBM = pl.BlockSpec(memory_space=pl.ANY)
KEPT = pl.BlockSpec(memory_space=pltpu.HBM)
VMEM = pl.BlockSpec(memory_space=pltpu.VMEM)


def nn(a, b):
    return jnp.dot(a, b, preferred_element_type=F32)


def nt(a, b):
    return lax.dot_general(a, b, (((1,), (1,)), ((), ())), preferred_element_type=F32)


def tn(a, b):
    return lax.dot_general(a, b, (((0,), (0,)), ((), ())), preferred_element_type=F32)


def normalised(values):
    average = jnp.mean(values, axis=-1, keepdims=True)
    centred = values - average
    variance = jnp.mean(centred * centred, axis=-1, keepdims=True)
    scale = lax.rsqrt(variance + norm_eps)
    return centred * scale, scale


def norm_back(grad, unit, scale, gain):
    moved = grad * gain
    inner = scale * (
        moved
        - jnp.mean(moved, axis=-1, keepdims=True)
        - unit * jnp.mean(moved * unit, axis=-1, keepdims=True)
    )
    return (
        inner,
        jnp.sum(grad * unit, axis=0, keepdims=True),
        jnp.sum(grad, axis=0, keepdims=True),
    )


def picks(target, columns):
    lanes = lax.broadcasted_iota(jnp.int32, (target.shape[0], columns), 1)
    return jnp.where(lanes == target, 1.0, 0.0).astype(BF)


def row_index(rows):
    return lax.broadcasted_iota(jnp.int32, (rows, 1), 0)


def at_least(value, limit):
    return jnp.where(value >= limit, 1, 0)


def place_from_piece():
    r = row_index(SPOTS)
    col = ((r >> 1) & 3) * PIECE + (r & 1) * HERE + (r >> 3)
    return picks(jnp.where(r < 8 * HERE, col, -1), ROWS)


def piece_parts():
    c = row_index(ROWS)
    k = at_least(c, PIECE) + at_least(c, 2 * PIECE) + at_least(c, 3 * PIECE)
    rem = c - PIECE * k
    f = at_least(rem, HERE)
    return k, f, rem - HERE * f, rem < 2 * HERE


def piece_from_place():
    k, f, p, valid = piece_parts()
    return picks(jnp.where(valid, p * 8 + k * 2 + f, -1), SPOTS)


def frame_from_piece(me):
    r = row_index(ROWS)
    f = at_least(r, FRAME_ROWS)
    spot = r - FRAME_ROWS * f
    q = at_least(spot, HERE) + at_least(spot, 2 * HERE) + at_least(spot, 3 * HERE)
    col = (q ^ me) * PIECE + f * HERE + spot - HERE * q
    return picks(jnp.where(spot < PLACES, col, -1), ROWS)


def piece_from_frame(me):
    k, f, p, valid = piece_parts()
    return picks(jnp.where(valid, f * FRAME_ROWS + HERE * (me ^ k) + p, -1), ROWS)


def split_pieces(rows, refs):
    for k, ref in enumerate(refs):
        ref[...] = rows[k * PIECE : (k + 1) * PIECE]


def stack_pieces(refs, stack):
    for k, ref in enumerate(refs):
        stack[k * PIECE : (k + 1) * PIECE, :] = ref[...]


def small_row(params, index, width=D):
    block = index // 8
    return params[index % 8 : index % 8 + 1, block * D : block * D + width]


def two_heads(value, factor=1.0):
    lane = lax.broadcasted_iota(jnp.int32, (1, 128), 1)
    low = jnp.where(lane < 64, factor, 0.0).astype(BF)
    high = jnp.where(lane < 64, 0.0, factor).astype(BF)
    return jnp.concatenate([value * low, value * high], axis=0)


def joined(value):
    rows = value.shape[0] // 2
    lane = lax.broadcasted_iota(jnp.int32, (rows, 128), 1)
    return jnp.where(lane < 64, value[:rows], value[rows:])


def attend_block(q, k, v, keep):
    scores = jnp.where(keep, nt(two_heads(q, 0.125), k), NEG)
    raised = jnp.exp(scores - jnp.max(scores, axis=-1, keepdims=True))
    weight = raised * (1.0 / jnp.sum(raised, axis=-1, keepdims=True))
    return joined(nn(weight.astype(BF), v)).astype(BF)


def attend_block_back(q, k, v, do, keep):
    scores = jnp.where(keep, nt(k, two_heads(q, 0.125)), NEG)
    raised = jnp.exp(scores - jnp.max(scores, axis=0, keepdims=True))
    weight = raised * (1.0 / jnp.sum(raised, axis=0, keepdims=True))
    both = two_heads(do)
    dv = nn(weight.astype(BF), both)
    dweight = nt(v, both)
    delta = jnp.sum(dweight * weight, axis=0, keepdims=True)
    dscore = (weight * (dweight - delta)).astype(BF)
    dq = joined(tn(dscore, k)) * 0.125
    dk = nn(dscore, two_heads(q, 0.125))
    return dq.astype(BF), dk.astype(BF), dv.astype(BF)


def spot_mask(rows, columns):
    r = lax.broadcasted_iota(jnp.int32, (rows, columns), 0)
    c = lax.broadcasted_iota(jnp.int32, (rows, columns), 1)
    wrap = lambda i, n: i - jnp.where(i >= GROUP, GROUP, 0) if n > GROUP else i
    return (wrap(r, rows) >> 3) == (wrap(c, columns) >> 3)


def wide_product(a_ref, w_ref, out_ref, columns, step, w_offset=0):
    def body(i, carry):
        at = pl.multiple_of(i * step, 128)
        out_ref[:, pl.ds(at, step)] = nn(
            a_ref[...], w_ref[:, pl.ds(at + w_offset, step)]
        ).astype(BF)
        return carry

    lax.fori_loop(0, columns // step, body, 0)


ENTRY_PIECES = (
    ((0, 0, 0, 0), (1, 0, 0, 1), (2, 0, 2, 0), (3, 0, 4, 1))
    + ((4, 0, 4, 0), (4, 56, 6, 0), (5, 0, 2, 1), (5, 48, 6, 1))
    + ((6, 0, 1, 0), (6, 56, 1, 1), (6, 104, 3, 0), (6, 160, 5, 1))
    + ((6, 208, 5, 0), (6, 264, 7, 0), (6, 320, 3, 1), (6, 368, 7, 1))
)
PLANE_PIECES = (
    ((0, 0, 0, 0), (0, 48, 0, 1), (2, 96, 2, 0), (1, 112, 4, 1))
    + ((3, 0, 4, 0), (3, 48, 6, 0), (4, 0, 2, 1), (4, 48, 6, 1))
    + ((5, 0, 1, 0), (5, 48, 1, 1), (5, 96, 3, 0), (5, 144, 5, 1))
    + ((5, 192, 5, 0), (5, 240, 7, 0), (5, 288, 3, 1), (5, 336, 7, 1))
)
EXPAND_PIECES = ((0, 0), (6, 0), (2, 96), (6, 192), (4, 0), (7, 0), (4, 96), (7, 96))
CONTRACT_PIECES = ((1, 0), (6, 96), (5, 0), (8, 0), (3, 96), (6, 288), (5, 96), (8, 96))


def piece_copies(refs, table, own, weights, extra, sems):
    copies = []
    for array, at, relative, half in table:
        rows = pl.ds(pl.multiple_of((own ^ relative) * SHARD + half * HALF, 16), HALF)
        pairs = [(refs[array].at[pl.ds(at, HALF)], weights.at[rows])]
        if half == 0 and extra is not None:
            pairs.append((refs[array].at[pl.ds(at + HALF, 8)], extra.at[relative]))
        for source, target in pairs:
            copies.append(pltpu.make_async_copy(source, target, sems.at[len(copies)]))
    return copies


def arrange_parameters(where, bias, *refs):
    sources, (first, second), held, sems = refs[:5], refs[5:7], refs[7:12], refs[12]
    copies = [
        pltpu.make_async_copy(source, target, sems.at[i])
        for i, (source, target) in enumerate(zip(sources, held, strict=True))
    ]
    for c in copies:
        c.start()
    entry, leave, gains, shifts, biases = held
    own = where[0]
    lane = lax.broadcasted_iota(jnp.int32, (SHARD, D), 1)
    spread = jnp.where(lane == own * SHARD + row_index(SHARD), 1.0, 0.0).astype(BF)
    lane = lax.broadcasted_iota(jnp.int32, (384, D), 1)
    wide = jnp.where(lane == (own & 1) * 384 + row_index(384), 1.0, 0.0).astype(BF)
    four = lax.broadcasted_iota(jnp.int32, (4, D), 0)
    bias_rows = jnp.where(four == own // 2, nn(bias[...], wide), 0.0)
    for c in copies:
        c.wait()
    rows = jnp.concatenate(
        [nn(gains[...], spread), nn(shifts[...], spread), nn(biases[...], spread), bias_rows], axis=0
    )
    rows = jnp.concatenate([rows, jnp.zeros((3, D), F32)], axis=0)
    first[0:HALF, : 3 * D] = entry[0:HALF]
    first[0:HALF, 3 * D :] = leave[0:HALF]
    first[HALF:, :D] = rows[0:8].astype(BF)
    first[HALF:, D : 2 * D] = rows[8:16].astype(BF)
    first[HALF:, 2 * D :] = jnp.zeros((8, 2 * D), BF)
    second[:, : 3 * D] = entry[HALF:]
    second[:, 3 * D :] = leave[HALF:]


def arrange_tokens(where, video, cotangent, tokens, cot, *pieces):
    for source, target in ((video, tokens), (cotangent, cot)):
        for f in range(2):
            target[f * FRAME_ROWS : f * FRAME_ROWS + PLACES, :] = source[0, f]
            target[f * FRAME_ROWS + PLACES : (f + 1) * FRAME_ROWS, :] = jnp.zeros(
                (FRAME_ROWS - PLACES, D), BF
            )
    split_pieces(nn(piece_from_frame(where[1]), tokens[...]).astype(BF), pieces)


def temporal_forward(*refs):
    video, pieces, refs = refs[:4], refs[4:11], refs[11:]
    out, refs = refs[:4], refs[4:]
    (normed_out, packed_out, weight_out, leave_out, params_out, bias_out), refs = refs[:6], refs[6:]
    weights, extra, stack, normed_ref, packed_ref, blended, sems, out_sems = refs
    own = lax.axis_index("fsdp")
    copies = piece_copies(pieces, ENTRY_PIECES, own, weights, extra, sems)
    for c in copies:
        c.start()
    stack_pieces(video, stack)
    unit, _ = normalised(stack[...].astype(F32))
    for c in copies:
        c.wait()
    outs = [
        pltpu.make_async_copy(weights.at[:, pl.ds(0, 3 * D)], weight_out, out_sems.at[0]),
        pltpu.make_async_copy(normed_ref, normed_out, out_sems.at[1]),
        pltpu.make_async_copy(packed_ref, packed_out, out_sems.at[2]),
        pltpu.make_async_copy(weights.at[:, pl.ds(3 * D, D)], leave_out, out_sems.at[3]),
    ]
    outs[0].start()
    outs[3].start()
    params = extra[0].astype(F32)
    for k in range(1, 8):
        params = params + extra[k].astype(F32)
    params_out[...] = params
    for r in range(4):
        bias_out[r : r + 1, :] = small_row(params, 9 + r)
    normed = (unit * small_row(params, 0) + small_row(params, 3)).astype(BF)
    normed_ref[...] = nn(place_from_piece(), normed).astype(BF)
    outs[1].start()
    wide_product(normed_ref, weights, packed_ref, 3 * D, D)
    outs[2].start()
    keep = spot_mask(2 * GROUP, GROUP)

    def heads(i, carry):
        at = pl.multiple_of(i * 128, 128)
        for t in range(SPOTS // GROUP):
            rows = pl.ds(t * GROUP, GROUP)
            blended[rows, pl.ds(at, 128)] = attend_block(
                packed_ref[rows, pl.ds(at, 128)],
                packed_ref[rows, pl.ds(at + D, 128)],
                packed_ref[rows, pl.ds(at + 2 * D, 128)],
                keep,
            )
        return carry

    lax.fori_loop(0, HEADS // 2, heads, 0)
    split_pieces(nn(piece_from_place(), blended[...]).astype(BF), out)
    for c in outs:
        c.wait()


def spatial_forward(*refs):
    (tokens, params_ref, w_exit), places, pieces, refs = refs[:3], refs[3:7], refs[7:13], refs[13:]
    after_two, normed_three = refs[:2]
    held, refs = refs[2:9], refs[9:]
    weights, stack, after_ref, normed_ref, packed_ref, blended, blended_time, sems, out_sems = refs
    own = lax.axis_index("fsdp")
    me = lax.axis_index("frame")
    copies = piece_copies(pieces, PLANE_PIECES, own, weights, None, sems)
    for c in copies:
        c.start()
    params = params_ref[...]
    stack_pieces(places, stack)
    blended_time[...] = nn(frame_from_piece(me), stack[...]).astype(BF)
    for c in copies:
        c.wait()
    outs = [
        pltpu.make_async_copy(src, dst, out_sems.at[i])
        for i, (src, dst) in enumerate(
            zip(
                (
                    weights.at[:, pl.ds(0, 3 * D)],
                    weights.at[:, pl.ds(3 * D, D)],
                    blended_time,
                    after_ref,
                    normed_ref,
                    packed_ref,
                    blended,
                ),
                held,
                strict=True,
            )
        )
    ]
    for c in outs[:3]:
        c.start()
    after_time = (
        tokens[...].astype(F32)
        + nn(blended_time[...], w_exit[...])
        + small_row(params, 6)
    )
    after_ref[...] = after_time
    outs[3].start()
    unit, _ = normalised(after_time)
    normed_ref[...] = (unit * small_row(params, 1) + small_row(params, 4)).astype(BF)
    outs[4].start()
    wide_product(normed_ref, weights, packed_ref, 3 * D, D)
    outs[5].start()
    keep = lax.broadcasted_iota(jnp.int32, (2 * FRAME_ROWS, FRAME_ROWS), 1) < PLACES

    def heads(i, carry):
        at = pl.multiple_of(i * 128, 128)
        for f in range(2):
            rows = pl.ds(f * FRAME_ROWS, FRAME_ROWS)
            blended[rows, pl.ds(at, 128)] = attend_block(
                packed_ref[rows, pl.ds(at, 128)],
                packed_ref[rows, pl.ds(at + D, 128)],
                packed_ref[rows, pl.ds(at + 2 * D, 128)],
                keep,
            )
        return carry

    lax.fori_loop(0, HEADS // 2, heads, 0)
    outs[6].start()
    last = after_ref[...] + nn(blended[...], weights[:, 3 * D :]) + small_row(params, 7)
    after_two[...] = last
    unit, _ = normalised(last)
    normed_three[...] = (unit * small_row(params, 2) + small_row(params, 5)).astype(BF)
    for c in outs:
        c.wait()


def feed_forward(where, normed, after_ref, cot, params_ref, bias, *refs):
    pieces, refs = refs[:9], refs[9:]
    (output, grad_after, branch, keep_we, send_we, keep_wc, send_wc, small), refs = refs[:8], refs[8:]
    w_in, w_out, normed_own, total, grad_normed, shuffle, sems = refs
    own = where[0]
    parity = own & 1
    first_copies, later = [], []
    for k, (array, at) in enumerate(EXPAND_PIECES):
        source = pieces[array].at[pl.ds(at, SHARD)]
        first_copies.append(
            pltpu.make_async_copy(source, w_in.at[pl.ds(k * SHARD, SHARD)], sems.at[k])
        )
    for k, (array, at) in enumerate(CONTRACT_PIECES):
        for c in range(4):
            source = pieces[array].at[pl.ds(at, SHARD), pl.ds(c * D, D)]
            spot = (k // 2) * D + (parity ^ (k & 1)) * 384 + c * SHARD
            target = w_out.at[pl.ds(pl.multiple_of(spot, 32), SHARD)]
            later.append(pltpu.make_async_copy(source, target, sems.at[8 + len(later)]))
    for c in first_copies + later:
        c.start()

    column = lax.broadcasted_iota(jnp.int32, (1, D), 1)
    block = (column * 683) >> 16
    order = (own ^ block) * SHARD + column - block * SHARD
    chosen = jnp.where(
        lax.broadcasted_iota(jnp.int32, (D, D), 0) == order, jnp.ones((), F32), jnp.zeros((), F32)
    ).astype(BF)
    normed_own[...] = nn(normed[...], chosen).astype(BF)
    total[...] = jnp.zeros_like(total)
    grad_normed[...] = jnp.zeros_like(grad_normed)
    small[...] = jnp.zeros_like(small)
    for c in first_copies + later:
        c.wait()

    def step(p, carry):
        chip = (own >> 1) ^ p
        at = pl.ds(pl.multiple_of(chip * D, D), D)
        rows = pl.ds(pl.multiple_of(p * D, D), D)
        hidden = nn(normed_own[...], w_in[:, at]) + bias[pl.ds(chip, 1), :]
        area = 0.5 + 0.5 * lax.erf(hidden * 0.7071067811865476)
        slope = area + hidden * (0.3989422804014327 * jnp.exp(-0.5 * hidden * hidden))
        active = (hidden * area).astype(BF)
        total[...] += nn(active, w_out[rows, :])
        grad_hidden = (nt(cot[...], w_out[rows, :]) * slope).astype(BF)
        grad_normed[...] += nt(grad_hidden, w_in[:, at])
        small[pl.ds(9 + chip, 1), :] = jnp.sum(grad_hidden.astype(F32), axis=0, keepdims=True)
        shuffle[...] = tn(active, cot[...])
        for kind, ref in ((parity, keep_wc), (1 - parity, send_wc)):
            for c in range(4):
                part = shuffle[pl.ds(pl.multiple_of(kind * 384 + c * SHARD, 32), SHARD), :]
                ref[p, :, c * D : (c + 1) * D] = part.astype(BF)
        moved = tn(normed_own[...], grad_hidden).astype(BF)
        for j in range(4):
            keep_we[j, :, at] = moved[2 * j * SHARD : (2 * j + 1) * SHARD]
            send_we[j, :, at] = moved[(2 * j + 1) * SHARD : (2 * j + 2) * SHARD]
        return carry

    lax.fori_loop(0, 4, step, 0)
    params = params_ref[...]
    values = after_ref[...]
    result = (values + (total[...] + small_row(params, 8))).astype(BF)
    for f in range(2):
        output[0, f] = result[f * FRAME_ROWS : f * FRAME_ROWS + PLACES]
    unit, scale = normalised(values)
    dn = nt(grad_normed[...].astype(BF), chosen)
    inner, dgain, dshift = norm_back(dn, unit, scale, small_row(params, 2))
    top = cot[...].astype(F32)
    dafter = top + inner
    grad_after[...] = dafter
    branch[...] = dafter.astype(BF)
    small[2:3, :] = dgain
    small[5:6, :] = dshift
    small[8:9, :] = jnp.sum(top, axis=0, keepdims=True)


def spatial_back(branch, packed, w_last, grad_packed, grad_blended):
    grad_blended[...] = nt(branch[...], w_last[...]).astype(BF)
    keep = lax.broadcasted_iota(jnp.int32, (FRAME_ROWS, 2 * FRAME_ROWS), 0) < PLACES

    def heads(i, carry):
        at = pl.multiple_of(i * 128, 128)
        for f in range(2):
            rows = pl.ds(f * FRAME_ROWS, FRAME_ROWS)
            dq, dk, dv = attend_block_back(
                packed[rows, pl.ds(at, 128)],
                packed[rows, pl.ds(at + D, 128)],
                packed[rows, pl.ds(at + 2 * D, 128)],
                grad_blended[rows, pl.ds(at, 128)],
                keep,
            )
            grad_packed[rows, pl.ds(at, 128)] = dq
            grad_packed[rows, pl.ds(at + D, 128)] = dk
            grad_packed[rows, pl.ds(at + 2 * D, 128)] = dv
        return carry

    lax.fori_loop(0, HEADS // 2, heads, 0)


def spatial_back_norm(where, *refs):
    grad_packed, branch, grad_after, after_ref, params_ref, small_in, w_entry, w_exit = refs[:8]
    grad_first, branch_first, small, *pieces = refs[8:]
    params = params_ref[...]
    dn = nt(grad_packed[...], w_entry[...]).astype(BF).astype(F32)
    unit, scale = normalised(after_ref[...])
    inner, dgain, dshift = norm_back(dn, unit, scale, small_row(params, 1))
    first = grad_after[...] + inner
    grad_first[...] = first
    low = first.astype(BF)
    branch_first[...] = low
    back = nt(low, w_exit[...]).astype(BF)
    split_pieces(nn(piece_from_frame(where[1]), back).astype(BF), pieces)
    small[...] = small_in[...]
    small[1:2, :] = dgain
    small[4:5, :] = dshift
    small[6:7, :] = jnp.sum(low.astype(F32), axis=0, keepdims=True)
    small[7:8, :] = jnp.sum(branch[...].astype(F32), axis=0, keepdims=True)


def temporal_back(*refs):
    video, pieces, (packed, small_in, weights), refs = refs[:4], refs[4:8], refs[8:11], refs[11:]
    (grad_packed, small), out, (stack, grads) = refs[:2], refs[2:6], refs[6:]
    stack_pieces(pieces, stack)
    grads[...] = nn(place_from_piece(), stack[...]).astype(BF)
    keep = spot_mask(GROUP, 2 * GROUP)

    def heads(i, carry):
        at = pl.multiple_of(i * 128, 128)
        for t in range(SPOTS // GROUP):
            rows = pl.ds(t * GROUP, GROUP)
            dq, dk, dv = attend_block_back(
                packed[rows, pl.ds(at, 128)],
                packed[rows, pl.ds(at + D, 128)],
                packed[rows, pl.ds(at + 2 * D, 128)],
                grads[rows, pl.ds(at, 128)],
                keep,
            )
            grad_packed[rows, pl.ds(at, 128)] = dq
            grad_packed[rows, pl.ds(at + D, 128)] = dk
            grad_packed[rows, pl.ds(at + 2 * D, 128)] = dv
        return carry

    lax.fori_loop(0, HEADS // 2, heads, 0)
    dn = nt(grad_packed[...], weights[...]).astype(BF)
    moved = nn(piece_from_place(), dn)
    split_pieces(moved.astype(BF), out)
    stack_pieces(video, stack)
    unit, _ = normalised(stack[...].astype(F32))
    small[...] = small_in[...]
    small[0:1, :] = jnp.sum(moved * unit, axis=0, keepdims=True)
    small[3:4, :] = jnp.sum(moved, axis=0, keepdims=True)


def input_back(where, tokens, grad_first, params_ref, *refs):
    pieces, (out, stack) = refs[:4], refs[4:]
    stack_pieces(pieces, stack)
    dn = nn(frame_from_piece(where[1]), stack[...])
    unit, scale = normalised(tokens[...].astype(F32))
    moved = dn * small_row(params_ref[...], 0)
    inner = scale * (
        moved
        - jnp.mean(moved, axis=-1, keepdims=True)
        - unit * jnp.mean(moved * unit, axis=-1, keepdims=True)
    )
    total = grad_first[...] + inner
    for f in range(2):
        out[0, f] = total[f * FRAME_ROWS : f * FRAME_ROWS + PLACES]


def weight_grads(where, *refs, tiles):
    step = pl.program_id(0)
    own = where[0]
    pairs, (keep, send, shuffle) = refs[: 2 * len(tiles)], refs[2 * len(tiles) :]
    first = 0
    for i, count in enumerate(tiles):

        @pl.when((step >= first) & (step < first + count))
        def _(i=i):
            shuffle[...] = tn(pairs[2 * i][...], pairs[2 * i + 1][...])

        first += count
    for j in range(4):
        for parity, ref in ((0, keep), (1, send)):
            rows = pl.ds(pl.multiple_of((own ^ (2 * j + parity)) * SHARD, 8), SHARD)
            ref[j] = shuffle[rows, :].astype(BF)


def by_columns(width, step):
    def run(i, carry):
        step(pl.ds(pl.multiple_of(i * 384, 128), 384))
        return carry

    lax.fori_loop(0, width // 384, run, 0)


def plane_one_sums(*refs, count):
    keeps, gots, (for_x, for_y, held) = refs[:count], refs[count : 2 * count], refs[2 * count :]

    def step(at):
        for i, (keep, got) in enumerate(zip(keeps, gots, strict=True)):
            total = [keep[j, :, at].astype(F32) + got[j, :, at].astype(F32) for j in range(4)]
            for_x[2 * i, :, at] = total[1][:HALF].astype(BF)
            for_x[2 * i + 1, :, at] = total[3][:HALF].astype(BF)
            for_y[2 * i, :, at] = total[2][HALF:].astype(BF)
            for_y[2 * i + 1, :, at] = total[3][HALF:].astype(BF)
            held[i, 0, :, at] = total[0][:HALF]
            held[i, 1, :, at] = total[0][HALF:]
            held[i, 2, :, at] = total[2][:HALF]
            held[i, 3, :, at] = total[1][HALF:]

    by_columns(keeps[0].shape[-1], step)


def plane_two_sums(held, from_x, from_y, next_y, next_x, left):
    def step(at):
        for i in range(held.shape[0]):
            next_y[i, :, at] = (held[i, 2, :, at] + from_x[2 * i + 1, :, at].astype(F32)).astype(BF)
            next_x[i, :, at] = (held[i, 3, :, at] + from_y[2 * i + 1, :, at].astype(F32)).astype(BF)
            left[i, 0, :, at] = held[i, 0, :, at] + from_x[2 * i, :, at].astype(F32)
            left[i, 1, :, at] = held[i, 1, :, at] + from_y[2 * i, :, at].astype(F32)

    by_columns(held.shape[-1], step)


def line_one_sums(where, left, got_y, got_x, out, stays):
    odd = where[1] & 1

    def step(at):
        for i in range(left.shape[0]):
            first = left[i, 0, :, at] + got_y[i, :, at].astype(F32)
            second = left[i, 1, :, at] + got_x[i, :, at].astype(F32)
            out[i, :, at] = jnp.where(odd == 1, first, second).astype(BF)
            stays[i, :, at] = jnp.where(odd == 1, second, first)

    by_columns(left.shape[-1], step)


def pair_sums(one, two, out):
    def step(at):
        for i in range(out.shape[0]):
            out[i, :, at] = (one[i, :, at].astype(F32) + two[i, :, at].astype(F32)).astype(BF)

    by_columns(out.shape[-1], step)


def line_result(where, full, other, *outs, parts):
    odd = where[1] & 1
    for out, (i, first, columns) in zip(outs, parts, strict=True):
        for block in range(columns // D):
            at = slice(first + block * D, first + (block + 1) * D)
            one, two = full[i, :, at].astype(F32), other[i, :, at].astype(F32)
            low = jnp.where(odd == 1, two, one)
            high = jnp.where(odd == 1, one, two)
            if out.shape[1] == D:
                out[block * SHARD : block * SHARD + HALF, :] = low
                out[block * SHARD + HALF : (block + 1) * SHARD, :] = high
            else:
                out[:HALF, block * D : (block + 1) * D] = low
                out[HALF:, block * D : (block + 1) * D] = high


def shape(*dims, dtype=BF):
    return jax.ShapeDtypeStruct(dims, dtype)


def kept(*dims, dtype=BF):
    return pltpu.HBM(dims, dtype)


NO_COST = pl.CostEstimate(flops=1000, bytes_accessed=1000, transcendentals=0)


def limit(mebibytes):
    return pltpu.CompilerParams(vmem_limit_bytes=mebibytes << 20)


def whole_call(kernel, name, outs, *ins, mebibytes=16, scalars=0, scratch=(), **options):
    specs = [pl.BlockSpec(memory_space=pltpu.SMEM)] * scalars + [VMEM] * (len(ins) - scalars)
    single = not isinstance(outs, (list, tuple))
    return pl.pallas_call(
        functools.partial(kernel, **options),
        name=name,
        out_shape=outs,
        in_specs=specs,
        out_specs=VMEM if single else [VMEM] * len(outs),
        scratch_shapes=scratch,
        compiler_params=limit(mebibytes),
        cost_estimate=NO_COST,
    )(*ins)


CORE = [(i, i ^ 1) for i in range(8)]
ACROSS = [(i, i ^ 2) for i in range(8)]
UP = [(i, i ^ 4) for i in range(8)]
NEAR = [(i, i ^ 1) for i in range(4)]
FAR = [(i, i ^ 2) for i in range(4)]


def swap(value, pairs, axis="fsdp"):
    return lax.ppermute(value, axis, pairs)


def shift(pieces):
    moved = [lax.ppermute(pieces[k], "frame", [(i, i ^ k) for i in range(4)]) for k in (1, 2, 3)]
    return [pieces[0], *moved]


def after(value, *earlier):
    return lax.optimization_barrier((value, *earlier))[0]


class Reduction:
    def __init__(self, where, keep, send):
        self.where, self.keep, self.count, self.width = where, keep, len(keep), keep[0].shape[-1]
        self.got = [swap(v, CORE) for v in send]

    def shape(self, *dims, dtype=BF):
        return shape(*dims, HALF, self.width, dtype=dtype)

    def plane_one(self, *earlier):
        got = [after(g, *earlier) for g in self.got] if earlier else self.got
        n = self.count
        for_x, for_y, self.held = whole_call(
            plane_one_sums,
            "plane_one",
            [self.shape(2 * n), self.shape(2 * n), self.shape(n, 4, dtype=F32)],
            *self.keep,
            *got,
            count=n,
            mebibytes=24,
        )
        self.from_x = swap(for_x, ACROSS)
        self.from_y = swap(for_y, UP)
        return for_x, for_y

    def plane_two(self, *earlier):
        n = self.count
        next_y, next_x, self.left = whole_call(
            plane_two_sums,
            "plane_two",
            [self.shape(n), self.shape(n), self.shape(n, 2, dtype=F32)],
            self.held,
            after(self.from_x, *earlier),
            after(self.from_y, *earlier),
        )
        self.got_y = swap(next_y, UP)
        self.got_x = swap(next_x, ACROSS)
        return next_y, next_x

    def line_one(self, *earlier):
        n = self.count
        out, self.stays = whole_call(
            line_one_sums,
            "line_one",
            [self.shape(n), self.shape(n, dtype=F32)],
            self.where,
            self.left,
            after(self.got_y, *earlier),
            after(self.got_x, *earlier),
            scalars=1,
        )
        self.near = swap(out, NEAR, "frame")
        return (out,)

    def line_two(self, *earlier):
        self.pair = whole_call(
            pair_sums, "line_two", self.shape(self.count), self.stays, after(self.near, *earlier)
        )
        self.far = swap(self.pair, FAR, "frame")
        return (self.pair,)

    def line_three(self, *earlier):
        self.full = whole_call(
            pair_sums, "line_three", self.shape(self.count), self.pair, after(self.far, *earlier)
        )
        self.other = swap(self.full, NEAR, "frame")
        return (self.full,)

    def result(self, parts, outs):
        return whole_call(
            line_result, "line_result", outs, self.where, self.full, self.other, scalars=1, parts=parts
        )


def reduce_small(small):
    for pairs in (CORE, ACROSS, UP):
        small = small + swap(small, pairs)
    for pairs in (NEAR, FAR):
        small = small + swap(small, pairs, "frame")
    return small


def body(
    video,
    temporal_entry,
    temporal_exit,
    spatial_entry,
    spatial_exit,
    expand_weight,
    contract_weight,
    layer_gains,
    layer_shifts,
    branch_biases,
    expand_bias,
    cotangent,
):
    own = lax.axis_index("fsdp")
    where = jnp.stack([own, lax.axis_index("frame")]).astype(jnp.int32)
    rows = lambda *parts: jnp.concatenate(parts, axis=0)

    sources = (temporal_entry, temporal_exit, layer_gains, layer_shifts, branch_biases)
    g1a, g1b = pl.pallas_call(
        arrange_parameters,
        name="arrange_parameters",
        out_shape=[shape(HALF + 8, WIDE), shape(HALF, WIDE)],
        in_specs=[pl.BlockSpec(memory_space=pltpu.SMEM), VMEM] + [HBM] * 5,
        out_specs=[VMEM] * 2,
        scratch_shapes=[pltpu.VMEM(v.shape, BF) for v in sources] + [pltpu.SemaphoreType.DMA((5,))],
        compiler_params=limit(8),
        cost_estimate=NO_COST,
    )(
        where,
        expand_bias.reshape(1, 384),
        *(pltpu.with_memory_space_constraint(v, pltpu.HBM) for v in sources),
    )
    x1, y1 = swap(g1a, ACROSS), swap(g1b, UP)

    tokens, cot, *video_pieces = whole_call(
        arrange_tokens,
        "arrange_tokens",
        [shape(ROWS, D), shape(ROWS, D)] + [shape(PIECE, D)] * 4,
        where,
        after(video, g1a),
        cotangent,
        scalars=1,
    )
    video_pieces = shift(video_pieces)

    plane = jnp.concatenate([spatial_entry, spatial_exit], axis=1)
    contract = jnp.concatenate([contract_weight[c * SHARD : (c + 1) * SHARD] for c in range(4)], axis=1)
    x1, y1, plane, contract, *_ = lax.optimization_barrier((x1, y1, plane, contract, tokens))
    to_y = rows(g1a, x1, plane[HALF:])
    to_x = rows(g1b, y1, plane[:HALF])
    r2y, r2x = swap(to_y, UP), swap(to_x, ACROSS)
    c1 = swap(rows(g1a, g1b, x1, y1, r2y[:112], r2x[:96]), CORE)
    to_y = after(rows(plane[:HALF], r2x[96:], contract), *video_pieces[1:])
    to_x = after(rows(plane[HALF:], r2y[112:], expand_weight), *video_pieces[1:])
    r3y, r3x = swap(to_y, UP), swap(to_x, ACROSS)

    *places, normed_place, packed_place, entry_full, exit_full, params, bias_full = pl.pallas_call(
        temporal_forward,
        name="temporal_forward",
        out_shape=[shape(PIECE, D)] * 4
        + [
            kept(SPOTS, D),
            kept(SPOTS, 3 * D),
            kept(D, 3 * D),
            kept(D, D),
            shape(8, WIDE, dtype=F32),
            shape(8, D, dtype=F32),
        ],
        in_specs=[VMEM] * 4 + [HBM] * 7,
        out_specs=[VMEM] * 4 + [KEPT] * 4 + [VMEM] * 2,
        scratch_shapes=[
            pltpu.VMEM((D, WIDE), BF),
            pltpu.VMEM((8, 8, WIDE), BF),
            pltpu.VMEM((ROWS, D), BF),
            pltpu.VMEM((SPOTS, D), BF),
            pltpu.VMEM((SPOTS, 3 * D), BF),
            pltpu.VMEM((SPOTS, D), BF),
            pltpu.SemaphoreType.DMA((24,)),
            pltpu.SemaphoreType.DMA((4,)),
        ],
        compiler_params=limit(24),
        cost_estimate=NO_COST,
    )(after(video_pieces[0], to_y, to_x), *video_pieces[1:], g1a, g1b, x1, y1, r2y, r2x, c1)
    places = shift(places)

    r3y, r3x = after(r3y, *places[1:]), after(r3x, *places[1:])
    c2 = swap(rows(plane, r2x[96:], r2y[112:], r3y[:96], r3x[:96]), CORE)
    to_y = rows(expand_weight, r3x[96:])
    to_x = rows(contract, r3y[96:])
    r4y, r4x = swap(to_y, UP), swap(to_x, ACROSS)
    (
        after_space,
        normed_three,
        space_full,
        last_full,
        blended_time,
        after_time,
        normed_two,
        packed_space,
        blended_space,
    ) = pl.pallas_call(
        spatial_forward,
        name="spatial_forward",
        out_shape=[
            shape(ROWS, D, dtype=F32),
            shape(ROWS, D),
            kept(D, 3 * D),
            kept(D, D),
            kept(ROWS, D),
            kept(ROWS, D, dtype=F32),
            kept(ROWS, D),
            kept(ROWS, 3 * D),
            kept(ROWS, D),
        ],
        in_specs=[VMEM] * 7 + [HBM] * 6,
        out_specs=[VMEM] * 2 + [KEPT] * 7,
        scratch_shapes=[
            pltpu.VMEM((D, WIDE), BF),
            pltpu.VMEM((ROWS, D), BF),
            pltpu.VMEM((ROWS, D), F32),
            pltpu.VMEM((ROWS, D), BF),
            pltpu.VMEM((ROWS, 3 * D), BF),
            pltpu.VMEM((ROWS, D), BF),
            pltpu.VMEM((ROWS, D), BF),
            pltpu.SemaphoreType.DMA((16,)),
            pltpu.SemaphoreType.DMA((7,)),
        ],
        compiler_params=limit(24),
        cost_estimate=NO_COST,
    )(after(tokens, to_y, to_x), params, exit_full, *places, plane, r2y, r2x, r3y, r3x, c2)

    c3 = swap(after(rows(expand_weight, contract, r3x[96:], r3y[96:]), normed_three), CORE)
    c4, c5 = swap(r4y, CORE), swap(r4x, CORE)
    output, grad_after, branch_last, keep_we, send_we, keep_wc, send_wc, small = pl.pallas_call(
        feed_forward,
        name="feed_forward",
        out_shape=[
            shape(*video.shape),
            shape(ROWS, D, dtype=F32),
            shape(ROWS, D),
            shape(4, SHARD, WIDE),
            shape(4, SHARD, WIDE),
            shape(4, SHARD, WIDE),
            shape(4, SHARD, WIDE),
            shape(16, D, dtype=F32),
        ],
        in_specs=[pl.BlockSpec(memory_space=pltpu.SMEM)] + [VMEM] * 5 + [HBM] * 9,
        out_specs=[VMEM] * 8,
        scratch_shapes=[
            pltpu.VMEM((D, WIDE), BF),
            pltpu.VMEM((WIDE, D), BF),
            pltpu.VMEM((ROWS, D), BF),
            pltpu.VMEM((ROWS, D), F32),
            pltpu.VMEM((ROWS, D), F32),
            pltpu.VMEM((D, D), F32),
            pltpu.SemaphoreType.DMA((40,)),
        ],
        compiler_params=limit(28),
        cost_estimate=NO_COST,
    )(
        *(where, normed_three, after_space, cot, params, bias_full),
        *(expand_weight, contract, r3x, r3y, r4y, r4x, c3, c4, c5),
    )
    forward_sum = Reduction(where, [keep_we, keep_wc], [send_we, send_wc])

    grad_packed = pl.pallas_call(
        spatial_back,
        name="spatial_back",
        out_shape=shape(ROWS, 3 * D),
        in_specs=[VMEM] * 3,
        out_specs=VMEM,
        scratch_shapes=[pltpu.VMEM((ROWS, D), BF)],
        compiler_params=limit(16),
        cost_estimate=NO_COST,
    )(branch_last, packed_space, last_full)
    placed = forward_sum.plane_one(grad_packed)
    grad_first, branch_first, small, *grad_pieces = whole_call(
        spatial_back_norm,
        "spatial_back_norm",
        [shape(ROWS, D, dtype=F32), shape(ROWS, D), shape(16, D, dtype=F32)] + [shape(PIECE, D)] * 4,
        where,
        grad_packed,
        branch_last,
        grad_after,
        after_time,
        params,
        after(small, *placed),
        space_full,
        exit_full,
        mebibytes=20,
        scalars=1,
    )
    grad_pieces = shift(grad_pieces)

    whole = lambda *dims: pl.BlockSpec(dims, lambda i, w: (0,) * len(dims))

    def grads(*pairs):
        tiles = tuple(b.shape[1] // D for _, b in pairs)
        specs, first = [], 0
        for (a, b), count in zip(pairs, tiles, strict=True):
            at = lambda i, w, first=first, count=count: (0, jnp.clip(i - first, 0, count - 1))
            specs += [whole(*a.shape), pl.BlockSpec((b.shape[0], D), at)]
            first += count
        return pl.pallas_call(
            functools.partial(weight_grads, tiles=tiles),
            name="weight_grads",
            out_shape=[shape(4, SHARD, D * first)] * 2,
            grid_spec=pltpu.PrefetchScalarGridSpec(
                num_scalar_prefetch=1,
                grid=(first,),
                in_specs=specs,
                out_specs=[pl.BlockSpec((4, SHARD, D), lambda i, w: (0, 0, i))] * 2,
                scratch_shapes=[pltpu.VMEM((D, D), F32)],
            ),
            compiler_params=limit(16),
            cost_estimate=NO_COST,
        )(where, *(v for pair in pairs for v in pair))

    keep_space, send_space = grads(
        (blended_time, branch_first), (normed_two, grad_packed), (blended_space, branch_last)
    )
    output = after(jnp.swapaxes(output, 1, 2), send_space)

    grad_place, small, *normed_back = pl.pallas_call(
        temporal_back,
        name="temporal_back",
        out_shape=[shape(SPOTS, 3 * D), shape(16, D, dtype=F32)] + [shape(PIECE, D)] * 4,
        in_specs=[VMEM] * 11,
        out_specs=[VMEM] * 6,
        scratch_shapes=[pltpu.VMEM((ROWS, D), BF), pltpu.VMEM((SPOTS, D), BF)],
        compiler_params=limit(20),
        cost_estimate=NO_COST,
    )(*video_pieces, after(grad_pieces[0], output), *grad_pieces[1:], packed_place, small, entry_full)

    step = lambda total, pairs, *axis: (total, swap(total, pairs, *axis))
    join = lambda both, *earlier: both[0] + after(both[1], *earlier)
    placed = forward_sum.plane_two(small)
    space_sum = Reduction(where, [keep_space], [after(send_space, *placed)])
    near = swap(after(jnp.stack([normed_back[1], normed_back[3]]), *placed), NEAR, "frame")
    keep_time, send_time = grads((after(normed_place, *placed), grad_place))
    placed = space_sum.plane_one(send_time)
    time_sum = Reduction(where, [keep_time], [after(send_time, near, *placed)])
    placed = forward_sum.line_one(*placed, near)
    far = swap(after(jnp.stack([normed_back[2], near[1]]), *placed), FAR, "frame")
    small = step(join(step(after(small, *placed), CORE)), ACROSS)
    placed = forward_sum.line_two(*placed, far)
    small = join(small, *placed)
    placed = space_sum.plane_two(*placed, small)
    placed = time_sum.plane_one(*placed)
    input_grad = whole_call(
        input_back,
        "input_back",
        shape(*video.shape, dtype=F32),
        where,
        after(tokens, *placed),
        grad_first,
        params,
        *(normed_back[0], near[0], far[0], far[1]),
        scalars=1,
        scratch=[pltpu.VMEM((ROWS, D), BF)],
    )
    placed = space_sum.line_one(*placed, input_grad)
    placed = time_sum.plane_two(*placed)
    small = step(after(small, *placed), UP)
    placed = forward_sum.line_three(*placed)
    small = join(small, *placed)
    placed = time_sum.line_one(*placed, small)
    small = step(after(small, *placed), NEAR, "frame")
    placed = space_sum.line_two(*placed)
    small = join(small, *placed)
    placed = time_sum.line_two(*placed, small)
    small = step(after(small, *placed), FAR, "frame")
    wide = lambda rows, columns: shape(rows, columns, dtype=F32)
    grad_expand, grad_contract = forward_sum.result(
        ((0, 0, WIDE), (1, 0, WIDE)), [wide(SHARD, WIDE), wide(4 * SHARD, D)]
    )
    placed = space_sum.line_three(*placed)
    small = join(small, *placed)
    placed = time_sum.line_three(*placed, grad_contract, small)
    input_grad = jnp.swapaxes(input_grad, 1, 2)
    grad_exit_time, grad_entry_space, grad_exit_space = space_sum.result(
        ((0, 0, D), (0, D, 3 * D), (0, 4 * D, D)),
        [wide(SHARD, D), wide(SHARD, 3 * D), wide(SHARD, D)],
    )
    time_sum.other = after(time_sum.other, grad_exit_space)
    (grad_entry_time,) = time_sum.result(((0, 0, 3 * D),), [wide(SHARD, 3 * D)])

    mine = lax.dynamic_slice_in_dim(small[:9], own * SHARD, SHARD, axis=1)
    return (
        jnp.swapaxes(output, 1, 2),
        jnp.swapaxes(input_grad, 1, 2),
        grad_entry_time,
        grad_exit_time,
        grad_entry_space,
        grad_exit_space,
        grad_expand,
        grad_contract,
        mine[0:3],
        mine[3:6],
        mine[6:9],
        lax.dynamic_slice_in_dim(small[9:13].reshape(WIDE), own * 384, 384),
    )


def solution(mesh):
    placed = (
        P("fsdp", "frame", None, None),
        P("fsdp", None),
        P("fsdp", None),
        P("fsdp", None),
        P("fsdp", None),
        P("fsdp", None),
        P("fsdp", None),
        P(None, "fsdp"),
        P(None, "fsdp"),
        P(None, "fsdp"),
        P("fsdp"),
        P("fsdp", "frame", None, None),
    )
    special = mesh.shape["fsdp"] == 8 and mesh.shape["frame"] == 4
    return jax.shard_map(
        body if special else general_body,
        mesh=mesh,
        in_specs=placed,
        out_specs=(
            P("fsdp", "frame", None, None),
            P("fsdp", "frame", None, None),
            P("fsdp", None),
            P("fsdp", None),
            P("fsdp", None),
            P("fsdp", None),
            P("fsdp", None),
            P("fsdp", None),
            P(None, "fsdp"),
            P(None, "fsdp"),
            P(None, "fsdp"),
            P("fsdp"),
        ),
        check_vma=False,
    )
```

```python
import functools

import jax
import jax.numpy as jnp
from jax import lax
from jax.experimental import pallas as pl
from jax.experimental.pallas import tpu as pltpu
from jax.sharding import PartitionSpec as P

HEADS = 12


norm_eps = 1e-05


def layer_norm(values, norm_gain, norm_shift):
    average = jnp.mean(values, axis=-1, keepdims=True)
    centred = values - average
    variance = jnp.mean(centred * centred, axis=-1, keepdims=True)
    return centred * lax.rsqrt(variance + norm_eps) * norm_gain + norm_shift


def rounded(values):
    return lax.optimization_barrier(values.astype(jnp.bfloat16)).astype(jnp.float32)


def dense(first_op, second_op):
    return jnp.dot(first_op, second_op, preferred_element_type=jnp.float32)


def dense_left(first_op, second_op):
    return lax.dot_general(
        first_op, second_op, (((0,), (0,)), ((), ())), preferred_element_type=jnp.float32
    )


def dense_right(first_op, second_op):
    return lax.dot_general(
        first_op, second_op, (((1,), (1,)), ((), ())), preferred_element_type=jnp.float32
    )


def split_heads(packed):
    outer = packed.shape
    parted = packed.reshape(outer[:-1] + (3, HEADS, outer[-1] // (3 * HEADS)))
    return (parted[..., 0, :, :], parted[..., 1, :, :], parted[..., 2, :, :])


def attend_forward(packed, layout):
    key_layout = layout.replace("l", "m")
    queries, key_rows, values = split_heads(packed)
    factor = queries.shape[-1] ** (-0.5)
    scores = (
        jnp.einsum(
            layout + "hd," + key_layout + "hd->cqhlm",
            queries,
            key_rows,
            preferred_element_type=jnp.float32,
        )
        * factor
    )
    highest = jnp.max(scores, axis=-1, keepdims=True)
    raised = jnp.exp(scores - highest)
    row_totals = jnp.sum(raised, axis=-1, keepdims=True)
    attention = (raised / row_totals).astype(jnp.bfloat16)
    blended = jnp.einsum(
        "cqhlm," + key_layout + "hd->" + layout + "hd",
        attention,
        values,
        preferred_element_type=jnp.float32,
    )
    outer = packed.shape
    return (
        blended.reshape(outer[:-1] + (outer[-1] // 3,)).astype(jnp.bfloat16),
        highest + jnp.log(row_totals),
    )


def attend_backward(packed, logsum, grad_blended, layout):
    key_layout = layout.replace("l", "m")
    queries, key_rows, values = split_heads(packed)
    factor = queries.shape[-1] ** (-0.5)
    outer = grad_blended.shape
    grad_heads = grad_blended.reshape(outer[:-1] + (HEADS, outer[-1] // HEADS))
    scores = (
        jnp.einsum(
            layout + "hd," + key_layout + "hd->cqhlm",
            queries,
            key_rows,
            preferred_element_type=jnp.float32,
        )
        * factor
    )
    attention = jnp.exp(scores - logsum)
    grad_values = jnp.einsum(
        "cqhlm," + layout + "hd->" + key_layout + "hd",
        attention.astype(jnp.bfloat16),
        grad_heads,
        preferred_element_type=jnp.float32,
    )
    grad_attention = jnp.einsum(
        layout + "hd," + key_layout + "hd->cqhlm",
        grad_heads,
        values,
        preferred_element_type=jnp.float32,
    )
    grad_scores = (
        attention * (grad_attention - jnp.sum(grad_attention * attention, axis=-1, keepdims=True))
    ).astype(jnp.bfloat16)
    grad_queries = (
        jnp.einsum(
            "cqhlm," + key_layout + "hd->" + layout + "hd",
            grad_scores,
            key_rows,
            preferred_element_type=jnp.float32,
        )
        * factor
    )
    grad_keys = (
        jnp.einsum(
            "cqhlm," + layout + "hd->" + key_layout + "hd",
            grad_scores,
            queries,
            preferred_element_type=jnp.float32,
        )
        * factor
    )
    stacked = jnp.stack([grad_queries, grad_keys, grad_values], axis=-3)
    return stacked.reshape(packed.shape).astype(jnp.bfloat16)


def general_body(
    video,
    temporal_entry,
    temporal_exit,
    spatial_entry,
    spatial_exit,
    expand_weight,
    contract_weight,
    layer_gains,
    layer_shifts,
    branch_biases,
    expand_bias,
    cotangent,
):
    clips_here, frames_here, places, model_width = video.shape
    rows_shape = (clips_here, frames_here, places)
    entry_time, exit_time, entry_space, exit_space, gains_low, shifts_low, biases_low = (
        lax.all_gather(temporal_entry, "fsdp", axis=0, tiled=True),
        lax.all_gather(temporal_exit, "fsdp", axis=0, tiled=True),
        lax.all_gather(spatial_entry, "fsdp", axis=0, tiled=True),
        lax.all_gather(spatial_exit, "fsdp", axis=0, tiled=True),
        lax.all_gather(layer_gains, "fsdp", axis=1, tiled=True),
        lax.all_gather(layer_shifts, "fsdp", axis=1, tiled=True),
        lax.all_gather(branch_biases, "fsdp", axis=1, tiled=True),
    )
    expand_full, contract_full, expand_bias_full = (
        lax.all_gather(expand_weight, "fsdp", axis=0, tiled=True),
        lax.all_gather(contract_weight, "fsdp", axis=0, tiled=True),
        lax.all_gather(expand_bias, "fsdp", axis=0, tiled=True),
    )
    gains = gains_low.astype(jnp.float32)
    shifts = shifts_low.astype(jnp.float32)
    biases = biases_low.astype(jnp.float32)
    tokens = video.astype(jnp.float32).reshape(-1, model_width)
    normed_one = layer_norm(tokens, gains[0], shifts[0]).astype(jnp.bfloat16)
    packed_frame = dense(normed_one, entry_time).astype(jnp.bfloat16)
    packed_place = lax.all_to_all(
        packed_frame.reshape(rows_shape + (3 * model_width,)),
        "frame",
        split_axis=2,
        concat_axis=1,
        tiled=True,
    )
    blended_place, logsum_time = attend_forward(packed_place, "clq")
    blended_time = lax.all_to_all(
        blended_place, "frame", split_axis=1, concat_axis=2, tiled=True
    ).reshape(-1, model_width)
    after_time = tokens + (dense(blended_time, exit_time) + biases[0])
    normed_two = layer_norm(after_time, gains[1], shifts[1]).astype(jnp.bfloat16)
    packed_space = (
        dense(normed_two, entry_space).astype(jnp.bfloat16).reshape(rows_shape + (3 * model_width,))
    )
    blended_space, logsum_space = attend_forward(packed_space, "cql")
    blended_rows = blended_space.reshape(-1, model_width)
    after_space = after_time + (dense(blended_rows, exit_space) + biases[1])
    normed_three = layer_norm(after_space, gains[2], shifts[2]).astype(jnp.bfloat16)
    hidden = dense(normed_three, expand_full) + expand_bias_full.astype(jnp.float32)
    active = jax.nn.gelu(hidden, approximate=False).astype(jnp.bfloat16)
    layer_output = (
        (after_space + (dense(active, contract_full) + biases[2]))
        .astype(jnp.bfloat16)
        .reshape(video.shape)
    )
    grad_top = cotangent.astype(jnp.float32).reshape(-1, model_width)
    grad_branch = grad_top.astype(jnp.bfloat16)
    grad_bias_last = jnp.sum(grad_branch.astype(jnp.float32), axis=0)
    grad_contract = dense_left(active, grad_branch)
    grad_active = dense_right(grad_branch, contract_full)
    gelu_pull = jax.vjp(lambda inner: jax.nn.gelu(inner, approximate=False), hidden)[1]
    grad_hidden = gelu_pull(grad_active)[0].astype(jnp.bfloat16)
    grad_expand = dense_left(normed_three, grad_hidden)
    grad_expand_bias = jnp.sum(grad_hidden.astype(jnp.float32), axis=0)
    grad_normed = rounded(dense_right(grad_hidden, expand_full))
    norm_pull = jax.vjp(layer_norm, after_space, gains[2], shifts[2])[1]
    grad_inner, grad_gain_last, grad_shift_last = norm_pull(grad_normed)
    grad_after_space = grad_top + grad_inner
    mlp_parts = (
        lax.psum_scatter(grad_expand, "fsdp", scatter_dimension=0, tiled=True),
        lax.psum_scatter(grad_contract, "fsdp", scatter_dimension=0, tiled=True),
        lax.psum_scatter(grad_expand_bias, "fsdp", scatter_dimension=0, tiled=True),
    )
    grad_branch = grad_after_space.astype(jnp.bfloat16)
    grad_bias_space = jnp.sum(grad_branch.astype(jnp.float32), axis=0)
    grad_exit_space = dense_left(blended_rows, grad_branch)
    grad_blended = (
        dense_right(grad_branch, exit_space)
        .astype(jnp.bfloat16)
        .reshape(rows_shape + (model_width,))
    )
    grad_packed = attend_backward(packed_space, logsum_space, grad_blended, "cql").reshape(
        -1, 3 * model_width
    )
    grad_entry_space = dense_left(normed_two, grad_packed)
    grad_normed = rounded(dense_right(grad_packed, entry_space))
    norm_pull = jax.vjp(layer_norm, after_time, gains[1], shifts[1])[1]
    grad_inner, grad_gain_space, grad_shift_space = norm_pull(grad_normed)
    grad_after_time = grad_after_space + grad_inner
    grad_branch = grad_after_time.astype(jnp.bfloat16)
    grad_bias_time = jnp.sum(grad_branch.astype(jnp.float32), axis=0)
    grad_exit_time = dense_left(blended_time, grad_branch)
    grad_blended = (
        dense_right(grad_branch, exit_time)
        .astype(jnp.bfloat16)
        .reshape(rows_shape + (model_width,))
    )
    grad_blended_place = lax.all_to_all(
        grad_blended, "frame", split_axis=2, concat_axis=1, tiled=True
    )
    grad_packed_place = attend_backward(packed_place, logsum_time, grad_blended_place, "clq")
    grad_packed_frame = lax.all_to_all(
        grad_packed_place, "frame", split_axis=1, concat_axis=2, tiled=True
    ).reshape(-1, 3 * model_width)
    grad_entry_time = dense_left(normed_one, grad_packed_frame)
    grad_normed_one = rounded(dense_right(grad_packed_frame, entry_time))
    norm_pull = jax.vjp(layer_norm, tokens, gains[0], shifts[0])[1]
    grad_inner, grad_gain_time, grad_shift_time = norm_pull(grad_normed_one)
    input_grad = (grad_after_time + grad_inner).reshape(video.shape)
    grad_gains = jnp.stack([grad_gain_time, grad_gain_space, grad_gain_last])
    grad_shifts = jnp.stack([grad_shift_time, grad_shift_space, grad_shift_last])
    grad_biases = jnp.stack([grad_bias_time, grad_bias_space, grad_bias_last])
    attention_parts = (
        lax.psum_scatter(grad_entry_time, "fsdp", scatter_dimension=0, tiled=True),
        lax.psum_scatter(grad_exit_time, "fsdp", scatter_dimension=0, tiled=True),
        lax.psum_scatter(grad_entry_space, "fsdp", scatter_dimension=0, tiled=True),
        lax.psum_scatter(grad_exit_space, "fsdp", scatter_dimension=0, tiled=True),
        lax.psum_scatter(grad_gains, "fsdp", scatter_dimension=1, tiled=True),
        lax.psum_scatter(grad_shifts, "fsdp", scatter_dimension=1, tiled=True),
        lax.psum_scatter(grad_biases, "fsdp", scatter_dimension=1, tiled=True),
    )
    shares = (
        lax.psum_scatter(
            attention_parts[0].astype(jnp.bfloat16), "frame", scatter_dimension=0, tiled=True
        ).astype(jnp.float32),
        lax.psum_scatter(
            attention_parts[1].astype(jnp.bfloat16), "frame", scatter_dimension=0, tiled=True
        ).astype(jnp.float32),
        lax.psum_scatter(
            attention_parts[2].astype(jnp.bfloat16), "frame", scatter_dimension=0, tiled=True
        ).astype(jnp.float32),
        lax.psum_scatter(
            attention_parts[3].astype(jnp.bfloat16), "frame", scatter_dimension=0, tiled=True
        ).astype(jnp.float32),
        lax.psum_scatter(
            mlp_parts[0].astype(jnp.bfloat16), "frame", scatter_dimension=0, tiled=True
        ).astype(jnp.float32),
        lax.psum_scatter(
            mlp_parts[1].astype(jnp.bfloat16), "frame", scatter_dimension=0, tiled=True
        ).astype(jnp.float32),
        lax.psum_scatter(
            jnp.moveaxis(attention_parts[4], 0, 1).astype(jnp.bfloat16),
            "frame",
            scatter_dimension=0,
            tiled=True,
        ).astype(jnp.float32),
        lax.psum_scatter(
            jnp.moveaxis(attention_parts[5], 0, 1).astype(jnp.bfloat16),
            "frame",
            scatter_dimension=0,
            tiled=True,
        ).astype(jnp.float32),
        lax.psum_scatter(
            jnp.moveaxis(attention_parts[6], 0, 1).astype(jnp.bfloat16),
            "frame",
            scatter_dimension=0,
            tiled=True,
        ).astype(jnp.float32),
        lax.psum_scatter(
            mlp_parts[2].astype(jnp.bfloat16), "frame", scatter_dimension=0, tiled=True
        ).astype(jnp.float32),
    )
    pieces = (
        lax.all_gather(shares[0].astype(jnp.bfloat16), "frame", axis=0, tiled=True).astype(
            jnp.float32
        ),
        lax.all_gather(shares[1].astype(jnp.bfloat16), "frame", axis=0, tiled=True).astype(
            jnp.float32
        ),
        lax.all_gather(shares[2].astype(jnp.bfloat16), "frame", axis=0, tiled=True).astype(
            jnp.float32
        ),
        lax.all_gather(shares[3].astype(jnp.bfloat16), "frame", axis=0, tiled=True).astype(
            jnp.float32
        ),
        lax.all_gather(shares[4].astype(jnp.bfloat16), "frame", axis=0, tiled=True).astype(
            jnp.float32
        ),
        lax.all_gather(shares[5].astype(jnp.bfloat16), "frame", axis=0, tiled=True).astype(
            jnp.float32
        ),
        lax.all_gather(shares[6].astype(jnp.bfloat16), "frame", axis=0, tiled=True).astype(
            jnp.float32
        ),
        lax.all_gather(shares[7].astype(jnp.bfloat16), "frame", axis=0, tiled=True).astype(
            jnp.float32
        ),
        lax.all_gather(shares[8].astype(jnp.bfloat16), "frame", axis=0, tiled=True).astype(
            jnp.float32
        ),
        lax.all_gather(shares[9].astype(jnp.bfloat16), "frame", axis=0, tiled=True).astype(
            jnp.float32
        ),
    )
    totals = (
        pieces[0],
        pieces[1],
        pieces[2],
        pieces[3],
        pieces[4],
        pieces[5],
        jnp.moveaxis(pieces[6], 0, 1),
        jnp.moveaxis(pieces[7], 0, 1),
        jnp.moveaxis(pieces[8], 0, 1),
        pieces[9],
    )
    return (
        layer_output,
        input_grad,
        totals[0],
        totals[1],
        totals[2],
        totals[3],
        totals[4],
        totals[5],
        totals[6],
        totals[7],
        totals[8],
        totals[9],
    )


BF = jnp.bfloat16
F32 = jnp.float32
D = 768
FRAME_ROWS = 208
PLACES = 196
HERE = 49
PIECE = 104
ROWS = 416
SPOTS = 400
GROUP = 80
SHARD = 96
HALF = 48
WIDE = 3072
NEG = -1e30
HBM = pl.BlockSpec(memory_space=pl.ANY)
KEPT = pl.BlockSpec(memory_space=pltpu.HBM)
VMEM = pl.BlockSpec(memory_space=pltpu.VMEM)


def nn(a, b):
    return jnp.dot(a, b, preferred_element_type=F32)


def nt(a, b):
    return lax.dot_general(a, b, (((1,), (1,)), ((), ())), preferred_element_type=F32)


def tn(a, b):
    return lax.dot_general(a, b, (((0,), (0,)), ((), ())), preferred_element_type=F32)


def normalised(values):
    average = jnp.mean(values, axis=-1, keepdims=True)
    centred = values - average
    variance = jnp.mean(centred * centred, axis=-1, keepdims=True)
    scale = lax.rsqrt(variance + norm_eps)
    return centred * scale, scale


def norm_back(grad, unit, scale, gain):
    moved = grad * gain
    inner = scale * (
        moved
        - jnp.mean(moved, axis=-1, keepdims=True)
        - unit * jnp.mean(moved * unit, axis=-1, keepdims=True)
    )
    return (
        inner,
        jnp.sum(grad * unit, axis=0, keepdims=True),
        jnp.sum(grad, axis=0, keepdims=True),
    )


def picks(target, columns):
    lanes = lax.broadcasted_iota(jnp.int32, (target.shape[0], columns), 1)
    return jnp.where(lanes == target, 1.0, 0.0).astype(BF)


def row_index(rows):
    return lax.broadcasted_iota(jnp.int32, (rows, 1), 0)


def at_least(value, limit):
    return jnp.where(value >= limit, 1, 0)


def place_from_piece():
    r = row_index(SPOTS)
    col = ((r >> 1) & 3) * PIECE + (r & 1) * HERE + (r >> 3)
    return picks(jnp.where(r < 8 * HERE, col, -1), ROWS)


def piece_parts():
    c = row_index(ROWS)
    k = at_least(c, PIECE) + at_least(c, 2 * PIECE) + at_least(c, 3 * PIECE)
    rem = c - PIECE * k
    f = at_least(rem, HERE)
    return k, f, rem - HERE * f, rem < 2 * HERE


def piece_from_place():
    k, f, p, valid = piece_parts()
    return picks(jnp.where(valid, p * 8 + k * 2 + f, -1), SPOTS)


def frame_from_piece(me):
    r = row_index(ROWS)
    f = at_least(r, FRAME_ROWS)
    spot = r - FRAME_ROWS * f
    q = at_least(spot, HERE) + at_least(spot, 2 * HERE) + at_least(spot, 3 * HERE)
    col = (q ^ me) * PIECE + f * HERE + spot - HERE * q
    return picks(jnp.where(spot < PLACES, col, -1), ROWS)


def piece_from_frame(me):
    k, f, p, valid = piece_parts()
    return picks(jnp.where(valid, f * FRAME_ROWS + HERE * (me ^ k) + p, -1), ROWS)


def split_pieces(rows, refs):
    for k, ref in enumerate(refs):
        ref[...] = rows[k * PIECE : (k + 1) * PIECE]


def stack_pieces(refs, stack):
    for k, ref in enumerate(refs):
        stack[k * PIECE : (k + 1) * PIECE, :] = ref[...]


def small_row(params, index, width=D):
    block = index // 8
    return params[index % 8 : index % 8 + 1, block * D : block * D + width]


def two_heads(value, factor=1.0):
    lane = lax.broadcasted_iota(jnp.int32, (1, 128), 1)
    low = jnp.where(lane < 64, factor, 0.0).astype(BF)
    high = jnp.where(lane < 64, 0.0, factor).astype(BF)
    return jnp.concatenate([value * low, value * high], axis=0)


def joined(value):
    rows = value.shape[0] // 2
    lane = lax.broadcasted_iota(jnp.int32, (rows, 128), 1)
    return jnp.where(lane < 64, value[:rows], value[rows:])


def attend_block(q, k, v, keep):
    scores = jnp.where(keep, nt(two_heads(q, 0.125), k), NEG)
    raised = jnp.exp(scores - jnp.max(scores, axis=-1, keepdims=True))
    weight = raised * (1.0 / jnp.sum(raised, axis=-1, keepdims=True))
    return joined(nn(weight.astype(BF), v)).astype(BF)


def attend_block_back(q, k, v, do, keep):
    scores = jnp.where(keep, nt(k, two_heads(q, 0.125)), NEG)
    raised = jnp.exp(scores - jnp.max(scores, axis=0, keepdims=True))
    weight = raised * (1.0 / jnp.sum(raised, axis=0, keepdims=True))
    both = two_heads(do)
    dv = nn(weight.astype(BF), both)
    dweight = nt(v, both)
    delta = jnp.sum(dweight * weight, axis=0, keepdims=True)
    dscore = (weight * (dweight - delta)).astype(BF)
    dq = joined(tn(dscore, k)) * 0.125
    dk = nn(dscore, two_heads(q, 0.125))
    return dq.astype(BF), dk.astype(BF), dv.astype(BF)


def spot_mask(rows, columns):
    r = lax.broadcasted_iota(jnp.int32, (rows, columns), 0)
    c = lax.broadcasted_iota(jnp.int32, (rows, columns), 1)
    wrap = lambda i, n: i - jnp.where(i >= GROUP, GROUP, 0) if n > GROUP else i
    return (wrap(r, rows) >> 3) == (wrap(c, columns) >> 3)


def wide_product(a_ref, w_ref, out_ref, columns, step, w_offset=0):
    def body(i, carry):
        at = pl.multiple_of(i * step, 128)
        out_ref[:, pl.ds(at, step)] = nn(
            a_ref[...], w_ref[:, pl.ds(at + w_offset, step)]
        ).astype(BF)
        return carry

    lax.fori_loop(0, columns // step, body, 0)


ENTRY_PIECES = (
    ((0, 0, 0, 0), (1, 0, 0, 1), (2, 0, 2, 0), (3, 0, 4, 1))
    + ((4, 0, 4, 0), (4, 56, 6, 0), (5, 0, 2, 1), (5, 48, 6, 1))
    + ((6, 0, 1, 0), (6, 56, 1, 1), (6, 104, 3, 0), (6, 160, 5, 1))
    + ((6, 208, 5, 0), (6, 264, 7, 0), (6, 320, 3, 1), (6, 368, 7, 1))
)
PLANE_PIECES = (
    ((0, 0, 0, 0), (0, 48, 0, 1), (2, 96, 2, 0), (1, 112, 4, 1))
    + ((3, 0, 4, 0), (3, 48, 6, 0), (4, 0, 2, 1), (4, 48, 6, 1))
    + ((5, 0, 1, 0), (5, 48, 1, 1), (5, 96, 3, 0), (5, 144, 5, 1))
    + ((5, 192, 5, 0), (5, 240, 7, 0), (5, 288, 3, 1), (5, 336, 7, 1))
)
EXPAND_PIECES = ((0, 0), (6, 0), (2, 96), (6, 192), (4, 0), (7, 0), (4, 96), (7, 96))
CONTRACT_PIECES = ((1, 0), (6, 96), (5, 0), (8, 0), (3, 96), (6, 288), (5, 96), (8, 96))


def piece_copies(refs, table, own, weights, extra, sems):
    copies = []
    for array, at, relative, half in table:
        rows = pl.ds(pl.multiple_of((own ^ relative) * SHARD + half * HALF, 16), HALF)
        pairs = [(refs[array].at[pl.ds(at, HALF)], weights.at[rows])]
        if half == 0 and extra is not None:
            pairs.append((refs[array].at[pl.ds(at + HALF, 8)], extra.at[relative]))
        for source, target in pairs:
            copies.append(pltpu.make_async_copy(source, target, sems.at[len(copies)]))
    return copies


def arrange_parameters(where, bias, *refs):
    sources, (first, second), held, sems = refs[:5], refs[5:7], refs[7:12], refs[12]
    copies = [
        pltpu.make_async_copy(source, target, sems.at[i])
        for i, (source, target) in enumerate(zip(sources, held, strict=True))
    ]
    for c in copies:
        c.start()
    entry, leave, gains, shifts, biases = held
    own = where[0]
    lane = lax.broadcasted_iota(jnp.int32, (SHARD, D), 1)
    spread = jnp.where(lane == own * SHARD + row_index(SHARD), 1.0, 0.0).astype(BF)
    lane = lax.broadcasted_iota(jnp.int32, (384, D), 1)
    wide = jnp.where(lane == (own & 1) * 384 + row_index(384), 1.0, 0.0).astype(BF)
    four = lax.broadcasted_iota(jnp.int32, (4, D), 0)
    bias_rows = jnp.where(four == own // 2, nn(bias[...], wide), 0.0)
    for c in copies:
        c.wait()
    rows = jnp.concatenate(
        [nn(gains[...], spread), nn(shifts[...], spread), nn(biases[...], spread), bias_rows], axis=0
    )
    rows = jnp.concatenate([rows, jnp.zeros((3, D), F32)], axis=0)
    first[0:HALF, : 3 * D] = entry[0:HALF]
    first[0:HALF, 3 * D :] = leave[0:HALF]
    first[HALF:, :D] = rows[0:8].astype(BF)
    first[HALF:, D : 2 * D] = rows[8:16].astype(BF)
    first[HALF:, 2 * D :] = jnp.zeros((8, 2 * D), BF)
    second[:, : 3 * D] = entry[HALF:]
    second[:, 3 * D :] = leave[HALF:]


def arrange_tokens(where, video, cotangent, tokens, cot, *pieces):
    for source, target in ((video, tokens), (cotangent, cot)):
        for f in range(2):
            target[f * FRAME_ROWS : f * FRAME_ROWS + PLACES, :] = source[0, f]
            target[f * FRAME_ROWS + PLACES : (f + 1) * FRAME_ROWS, :] = jnp.zeros(
                (FRAME_ROWS - PLACES, D), BF
            )
    split_pieces(nn(piece_from_frame(where[1]), tokens[...]).astype(BF), pieces)


def temporal_forward(*refs):
    video, pieces, refs = refs[:4], refs[4:11], refs[11:]
    out, refs = refs[:4], refs[4:]
    (normed_out, packed_out, weight_out, leave_out, params_out, bias_out), refs = refs[:6], refs[6:]
    weights, extra, stack, normed_ref, packed_ref, blended, sems, out_sems = refs
    own = lax.axis_index("fsdp")
    copies = piece_copies(pieces, ENTRY_PIECES, own, weights, extra, sems)
    for c in copies:
        c.start()
    stack_pieces(video, stack)
    unit, _ = normalised(stack[...].astype(F32))
    for c in copies:
        c.wait()
    outs = [
        pltpu.make_async_copy(weights.at[:, pl.ds(0, 3 * D)], weight_out, out_sems.at[0]),
        pltpu.make_async_copy(normed_ref, normed_out, out_sems.at[1]),
        pltpu.make_async_copy(packed_ref, packed_out, out_sems.at[2]),
        pltpu.make_async_copy(weights.at[:, pl.ds(3 * D, D)], leave_out, out_sems.at[3]),
    ]
    outs[0].start()
    outs[3].start()
    params = extra[0].astype(F32)
    for k in range(1, 8):
        params = params + extra[k].astype(F32)
    params_out[...] = params
    for r in range(4):
        bias_out[r : r + 1, :] = small_row(params, 9 + r)
    normed = (unit * small_row(params, 0) + small_row(params, 3)).astype(BF)
    normed_ref[...] = nn(place_from_piece(), normed).astype(BF)
    outs[1].start()
    wide_product(normed_ref, weights, packed_ref, 3 * D, D)
    outs[2].start()
    keep = spot_mask(2 * GROUP, GROUP)

    def heads(i, carry):
        at = pl.multiple_of(i * 128, 128)
        for t in range(SPOTS // GROUP):
            rows = pl.ds(t * GROUP, GROUP)
            blended[rows, pl.ds(at, 128)] = attend_block(
                packed_ref[rows, pl.ds(at, 128)],
                packed_ref[rows, pl.ds(at + D, 128)],
                packed_ref[rows, pl.ds(at + 2 * D, 128)],
                keep,
            )
        return carry

    lax.fori_loop(0, HEADS // 2, heads, 0)
    split_pieces(nn(piece_from_place(), blended[...]).astype(BF), out)
    for c in outs:
        c.wait()


def spatial_forward(*refs):
    (tokens, params_ref, w_exit), places, pieces, refs = refs[:3], refs[3:7], refs[7:13], refs[13:]
    after_two, normed_three = refs[:2]
    held, refs = refs[2:9], refs[9:]
    weights, stack, after_ref, normed_ref, packed_ref, blended, blended_time, sems, out_sems = refs
    own = lax.axis_index("fsdp")
    me = lax.axis_index("frame")
    copies = piece_copies(pieces, PLANE_PIECES, own, weights, None, sems)
    for c in copies:
        c.start()
    params = params_ref[...]
    stack_pieces(places, stack)
    blended_time[...] = nn(frame_from_piece(me), stack[...]).astype(BF)
    for c in copies:
        c.wait()
    outs = [
        pltpu.make_async_copy(src, dst, out_sems.at[i])
        for i, (src, dst) in enumerate(
            zip(
                (
                    weights.at[:, pl.ds(0, 3 * D)],
                    weights.at[:, pl.ds(3 * D, D)],
                    blended_time,
                    after_ref,
                    normed_ref,
                    packed_ref,
                    blended,
                ),
                held,
                strict=True,
            )
        )
    ]
    for c in outs[:3]:
        c.start()
    after_time = (
        tokens[...].astype(F32)
        + nn(blended_time[...], w_exit[...])
        + small_row(params, 6)
    )
    after_ref[...] = after_time
    outs[3].start()
    unit, _ = normalised(after_time)
    normed_ref[...] = (unit * small_row(params, 1) + small_row(params, 4)).astype(BF)
    outs[4].start()
    wide_product(normed_ref, weights, packed_ref, 3 * D, D)
    outs[5].start()
    keep = lax.broadcasted_iota(jnp.int32, (2 * FRAME_ROWS, FRAME_ROWS), 1) < PLACES

    def heads(i, carry):
        at = pl.multiple_of(i * 128, 128)
        for f in range(2):
            rows = pl.ds(f * FRAME_ROWS, FRAME_ROWS)
            blended[rows, pl.ds(at, 128)] = attend_block(
                packed_ref[rows, pl.ds(at, 128)],
                packed_ref[rows, pl.ds(at + D, 128)],
                packed_ref[rows, pl.ds(at + 2 * D, 128)],
                keep,
            )
        return carry

    lax.fori_loop(0, HEADS // 2, heads, 0)
    outs[6].start()
    last = after_ref[...] + nn(blended[...], weights[:, 3 * D :]) + small_row(params, 7)
    after_two[...] = last
    unit, _ = normalised(last)
    normed_three[...] = (unit * small_row(params, 2) + small_row(params, 5)).astype(BF)
    for c in outs:
        c.wait()


def feed_forward(where, normed, after_ref, cot, params_ref, bias, *refs):
    pieces, refs = refs[:9], refs[9:]
    (output, grad_after, branch, keep_we, send_we, keep_wc, send_wc, small), refs = refs[:8], refs[8:]
    w_in, w_out, normed_own, total, grad_normed, shuffle, sems = refs
    own = where[0]
    parity = own & 1
    first_copies, later = [], []
    for k, (array, at) in enumerate(EXPAND_PIECES):
        source = pieces[array].at[pl.ds(at, SHARD)]
        first_copies.append(
            pltpu.make_async_copy(source, w_in.at[pl.ds(k * SHARD, SHARD)], sems.at[k])
        )
    for k, (array, at) in enumerate(CONTRACT_PIECES):
        for c in range(4):
            source = pieces[array].at[pl.ds(at, SHARD), pl.ds(c * D, D)]
            spot = (k // 2) * D + (parity ^ (k & 1)) * 384 + c * SHARD
            target = w_out.at[pl.ds(pl.multiple_of(spot, 32), SHARD)]
            later.append(pltpu.make_async_copy(source, target, sems.at[8 + len(later)]))
    for c in first_copies + later:
        c.start()

    column = lax.broadcasted_iota(jnp.int32, (1, D), 1)
    block = (column * 683) >> 16
    order = (own ^ block) * SHARD + column - block * SHARD
    chosen = jnp.where(
        lax.broadcasted_iota(jnp.int32, (D, D), 0) == order, jnp.ones((), F32), jnp.zeros((), F32)
    ).astype(BF)
    normed_own[...] = nn(normed[...], chosen).astype(BF)
    total[...] = jnp.zeros_like(total)
    grad_normed[...] = jnp.zeros_like(grad_normed)
    small[...] = jnp.zeros_like(small)
    for c in first_copies + later:
        c.wait()

    def step(p, carry):
        chip = (own >> 1) ^ p
        at = pl.ds(pl.multiple_of(chip * D, D), D)
        rows = pl.ds(pl.multiple_of(p * D, D), D)
        hidden = nn(normed_own[...], w_in[:, at]) + bias[pl.ds(chip, 1), :]
        area = 0.5 + 0.5 * lax.erf(hidden * 0.7071067811865476)
        slope = area + hidden * (0.3989422804014327 * jnp.exp(-0.5 * hidden * hidden))
        active = (hidden * area).astype(BF)
        total[...] += nn(active, w_out[rows, :])
        grad_hidden = (nt(cot[...], w_out[rows, :]) * slope).astype(BF)
        grad_normed[...] += nt(grad_hidden, w_in[:, at])
        small[pl.ds(9 + chip, 1), :] = jnp.sum(grad_hidden.astype(F32), axis=0, keepdims=True)
        shuffle[...] = tn(active, cot[...])
        for kind, ref in ((parity, keep_wc), (1 - parity, send_wc)):
            for c in range(4):
                part = shuffle[pl.ds(pl.multiple_of(kind * 384 + c * SHARD, 32), SHARD), :]
                ref[p, :, c * D : (c + 1) * D] = part.astype(BF)
        moved = tn(normed_own[...], grad_hidden).astype(BF)
        for j in range(4):
            keep_we[j, :, at] = moved[2 * j * SHARD : (2 * j + 1) * SHARD]
            send_we[j, :, at] = moved[(2 * j + 1) * SHARD : (2 * j + 2) * SHARD]
        return carry

    lax.fori_loop(0, 4, step, 0)
    params = params_ref[...]
    values = after_ref[...]
    result = (values + (total[...] + small_row(params, 8))).astype(BF)
    for f in range(2):
        output[0, f] = result[f * FRAME_ROWS : f * FRAME_ROWS + PLACES]
    unit, scale = normalised(values)
    dn = nt(grad_normed[...].astype(BF), chosen)
    inner, dgain, dshift = norm_back(dn, unit, scale, small_row(params, 2))
    top = cot[...].astype(F32)
    dafter = top + inner
    grad_after[...] = dafter
    branch[...] = dafter.astype(BF)
    small[2:3, :] = dgain
    small[5:6, :] = dshift
    small[8:9, :] = jnp.sum(top, axis=0, keepdims=True)


def spatial_back(branch, packed, w_last, grad_packed, grad_blended):
    grad_blended[...] = nt(branch[...], w_last[...]).astype(BF)
    keep = lax.broadcasted_iota(jnp.int32, (FRAME_ROWS, 2 * FRAME_ROWS), 0) < PLACES

    def heads(i, carry):
        at = pl.multiple_of(i * 128, 128)
        for f in range(2):
            rows = pl.ds(f * FRAME_ROWS, FRAME_ROWS)
            dq, dk, dv = attend_block_back(
                packed[rows, pl.ds(at, 128)],
                packed[rows, pl.ds(at + D, 128)],
                packed[rows, pl.ds(at + 2 * D, 128)],
                grad_blended[rows, pl.ds(at, 128)],
                keep,
            )
            grad_packed[rows, pl.ds(at, 128)] = dq
            grad_packed[rows, pl.ds(at + D, 128)] = dk
            grad_packed[rows, pl.ds(at + 2 * D, 128)] = dv
        return carry

    lax.fori_loop(0, HEADS // 2, heads, 0)


def spatial_back_norm(where, *refs):
    grad_packed, branch, grad_after, after_ref, params_ref, small_in, w_entry, w_exit = refs[:8]
    grad_first, branch_first, small, *pieces = refs[8:]
    params = params_ref[...]
    dn = nt(grad_packed[...], w_entry[...]).astype(BF).astype(F32)
    unit, scale = normalised(after_ref[...])
    inner, dgain, dshift = norm_back(dn, unit, scale, small_row(params, 1))
    first = grad_after[...] + inner
    grad_first[...] = first
    low = first.astype(BF)
    branch_first[...] = low
    back = nt(low, w_exit[...]).astype(BF)
    split_pieces(nn(piece_from_frame(where[1]), back).astype(BF), pieces)
    small[...] = small_in[...]
    small[1:2, :] = dgain
    small[4:5, :] = dshift
    small[6:7, :] = jnp.sum(low.astype(F32), axis=0, keepdims=True)
    small[7:8, :] = jnp.sum(branch[...].astype(F32), axis=0, keepdims=True)


def temporal_back(*refs):
    video, pieces, (packed, small_in, weights), refs = refs[:4], refs[4:8], refs[8:11], refs[11:]
    (grad_packed, small), out, (stack, grads) = refs[:2], refs[2:6], refs[6:]
    stack_pieces(pieces, stack)
    grads[...] = nn(place_from_piece(), stack[...]).astype(BF)
    keep = spot_mask(GROUP, 2 * GROUP)

    def heads(i, carry):
        at = pl.multiple_of(i * 128, 128)
        for t in range(SPOTS // GROUP):
            rows = pl.ds(t * GROUP, GROUP)
            dq, dk, dv = attend_block_back(
                packed[rows, pl.ds(at, 128)],
                packed[rows, pl.ds(at + D, 128)],
                packed[rows, pl.ds(at + 2 * D, 128)],
                grads[rows, pl.ds(at, 128)],
                keep,
            )
            grad_packed[rows, pl.ds(at, 128)] = dq
            grad_packed[rows, pl.ds(at + D, 128)] = dk
            grad_packed[rows, pl.ds(at + 2 * D, 128)] = dv
        return carry

    lax.fori_loop(0, HEADS // 2, heads, 0)
    dn = nt(grad_packed[...], weights[...]).astype(BF)
    moved = nn(piece_from_place(), dn)
    split_pieces(moved.astype(BF), out)
    stack_pieces(video, stack)
    unit, _ = normalised(stack[...].astype(F32))
    small[...] = small_in[...]
    small[0:1, :] = jnp.sum(moved * unit, axis=0, keepdims=True)
    small[3:4, :] = jnp.sum(moved, axis=0, keepdims=True)


def input_back(where, tokens, grad_first, params_ref, *refs):
    pieces, (out, stack) = refs[:4], refs[4:]
    stack_pieces(pieces, stack)
    dn = nn(frame_from_piece(where[1]), stack[...])
    unit, scale = normalised(tokens[...].astype(F32))
    moved = dn * small_row(params_ref[...], 0)
    inner = scale * (
        moved
        - jnp.mean(moved, axis=-1, keepdims=True)
        - unit * jnp.mean(moved * unit, axis=-1, keepdims=True)
    )
    total = grad_first[...] + inner
    for f in range(2):
        out[0, f] = total[f * FRAME_ROWS : f * FRAME_ROWS + PLACES]


def weight_grads(where, *refs, tiles):
    step = pl.program_id(0)
    own = where[0]
    pairs, (keep, send, shuffle) = refs[: 2 * len(tiles)], refs[2 * len(tiles) :]
    first = 0
    for i, count in enumerate(tiles):

        @pl.when((step >= first) & (step < first + count))
        def _(i=i):
            shuffle[...] = tn(pairs[2 * i][...], pairs[2 * i + 1][...])

        first += count
    for j in range(4):
        for parity, ref in ((0, keep), (1, send)):
            rows = pl.ds(pl.multiple_of((own ^ (2 * j + parity)) * SHARD, 8), SHARD)
            ref[j] = shuffle[rows, :].astype(BF)


def by_columns(width, step):
    def run(i, carry):
        step(pl.ds(pl.multiple_of(i * 384, 128), 384))
        return carry

    lax.fori_loop(0, width // 384, run, 0)


def plane_one_sums(*refs, count):
    keeps, gots, (for_x, for_y, held) = refs[:count], refs[count : 2 * count], refs[2 * count :]

    def step(at):
        for i, (keep, got) in enumerate(zip(keeps, gots, strict=True)):
            total = [keep[j, :, at].astype(F32) + got[j, :, at].astype(F32) for j in range(4)]
            for_x[2 * i, :, at] = total[1][:HALF].astype(BF)
            for_x[2 * i + 1, :, at] = total[3][:HALF].astype(BF)
            for_y[2 * i, :, at] = total[2][HALF:].astype(BF)
            for_y[2 * i + 1, :, at] = total[3][HALF:].astype(BF)
            held[i, 0, :, at] = total[0][:HALF]
            held[i, 1, :, at] = total[0][HALF:]
            held[i, 2, :, at] = total[2][:HALF]
            held[i, 3, :, at] = total[1][HALF:]

    by_columns(keeps[0].shape[-1], step)


def plane_two_sums(held, from_x, from_y, next_y, next_x, left):
    def step(at):
        for i in range(held.shape[0]):
            next_y[i, :, at] = (held[i, 2, :, at] + from_x[2 * i + 1, :, at].astype(F32)).astype(BF)
            next_x[i, :, at] = (held[i, 3, :, at] + from_y[2 * i + 1, :, at].astype(F32)).astype(BF)
            left[i, 0, :, at] = held[i, 0, :, at] + from_x[2 * i, :, at].astype(F32)
            left[i, 1, :, at] = held[i, 1, :, at] + from_y[2 * i, :, at].astype(F32)

    by_columns(held.shape[-1], step)


def line_one_sums(where, left, got_y, got_x, out, stays):
    odd = where[1] & 1

    def step(at):
        for i in range(left.shape[0]):
            first = left[i, 0, :, at] + got_y[i, :, at].astype(F32)
            second = left[i, 1, :, at] + got_x[i, :, at].astype(F32)
            out[i, :, at] = jnp.where(odd == 1, first, second).astype(BF)
            stays[i, :, at] = jnp.where(odd == 1, second, first)

    by_columns(left.shape[-1], step)


def pair_sums(one, two, out):
    def step(at):
        for i in range(out.shape[0]):
            out[i, :, at] = (one[i, :, at].astype(F32) + two[i, :, at].astype(F32)).astype(BF)

    by_columns(out.shape[-1], step)


def line_result(where, full, other, *outs, parts):
    odd = where[1] & 1
    for out, (i, first, columns) in zip(outs, parts, strict=True):
        for block in range(columns // D):
            at = slice(first + block * D, first + (block + 1) * D)
            one, two = full[i, :, at].astype(F32), other[i, :, at].astype(F32)
            low = jnp.where(odd == 1, two, one)
            high = jnp.where(odd == 1, one, two)
            if out.shape[1] == D:
                out[block * SHARD : block * SHARD + HALF, :] = low
                out[block * SHARD + HALF : (block + 1) * SHARD, :] = high
            else:
                out[:HALF, block * D : (block + 1) * D] = low
                out[HALF:, block * D : (block + 1) * D] = high


def chain_start(left, got_y, got_x, *outs):
    def step(at):
        for i, out in enumerate(outs):
            out[0, :HALF, at] = (left[i, 0, :, at] + got_y[i, :, at].astype(F32)).astype(BF)
            out[0, HALF:, at] = (left[i, 1, :, at] + got_x[i, :, at].astype(F32)).astype(BF)

    by_columns(left.shape[-1], step)


def chain_result(where, *refs):
    inner = (where[1] == 1) | (where[1] == 2)
    count = len(refs) // 3
    for total, got, out in zip(refs[:count], refs[count : 2 * count], refs[2 * count :], strict=True):
        for block in range(total.shape[-1] // D):
            at = slice(block * D, (block + 1) * D)
            value = jnp.where(inner, total[0, :, at].astype(F32), got[0, :, at].astype(F32))
            if out.shape[1] == D:
                out[block * SHARD : (block + 1) * SHARD, :] = value
            else:
                out[:, at] = value


def put_small(target, at, value):
    target[at : at + 8, :D] = value[:8]
    target[at : at + 8, D : 2 * D] = value[8:]
    target[at : at + 8, 2 * D :] = jnp.zeros((8, target.shape[1] - 2 * D), BF)


def add_small(kept, source, at):
    got = source[at : at + 8, : 2 * D].astype(F32)
    return kept[...].astype(F32) + jnp.concatenate([got[:, :D], got[:, D:]], axis=0)


def plane_one_both(keep, got, small, small_got, for_x, for_y, held, kept):
    def step(at):
        total = [keep[j, :, at].astype(F32) + got[j, :, at].astype(F32) for j in range(4)]
        for_x[:HALF, at] = total[1][:HALF].astype(BF)
        for_x[HALF:SHARD, at] = total[3][:HALF].astype(BF)
        for_y[:HALF, at] = total[2][HALF:].astype(BF)
        for_y[HALF:, at] = total[3][HALF:].astype(BF)
        held[0, :, at] = total[0][:HALF]
        held[1, :, at] = total[0][HALF:]
        held[2, :, at] = total[2][:HALF]
        held[3, :, at] = total[1][HALF:]

    by_columns(keep.shape[-1], step)
    value = (small[...] + small_got[...]).astype(BF)
    kept[...] = value
    put_small(for_x, SHARD, value)


def plane_two_both(held, from_x, from_y, kept, next_y, next_x, left, kept_next):
    def step(at):
        next_y[:HALF, at] = (held[2, :, at] + from_x[HALF:SHARD, at].astype(F32)).astype(BF)
        next_x[:, at] = (held[3, :, at] + from_y[HALF:, at].astype(F32)).astype(BF)
        left[0, :, at] = held[0, :, at] + from_x[:HALF, at].astype(F32)
        left[1, :, at] = held[1, :, at] + from_y[:HALF, at].astype(F32)

    by_columns(held.shape[-1], step)
    value = add_small(kept, from_x, SHARD).astype(BF)
    kept_next[...] = value
    put_small(next_y, HALF, value)


def line_one_both(where, left, got_y, got_x, kept, out, stays, kept_next):
    odd = where[1] & 1

    def step(at):
        first = left[0, :, at] + got_y[:HALF, at].astype(F32)
        second = left[1, :, at] + got_x[:, at].astype(F32)
        out[:HALF, at] = jnp.where(odd == 1, first, second).astype(BF)
        stays[:, at] = jnp.where(odd == 1, second, first)

    by_columns(left.shape[-1], step)
    value = add_small(kept, got_y, HALF).astype(BF)
    kept_next[...] = value
    put_small(out, HALF, value)


def line_two_both(stays, near, kept, pair, kept_next):
    def step(at):
        pair[:HALF, at] = (stays[:, at] + near[:HALF, at].astype(F32)).astype(BF)

    by_columns(stays.shape[-1], step)
    value = add_small(kept, near, HALF).astype(BF)
    kept_next[...] = value
    put_small(pair, HALF, value)


def line_three_both(pair, far, kept, full, small):
    def step(at):
        full[0, :, at] = (pair[:HALF, at].astype(F32) + far[:HALF, at].astype(F32)).astype(BF)

    by_columns(full.shape[-1], step)
    small[...] = add_small(kept, far, HALF)


def shape(*dims, dtype=BF):
    return jax.ShapeDtypeStruct(dims, dtype)


def kept(*dims, dtype=BF):
    return pltpu.HBM(dims, dtype)


NO_COST = pl.CostEstimate(flops=1000, bytes_accessed=1000, transcendentals=0)


def limit(mebibytes):
    return pltpu.CompilerParams(vmem_limit_bytes=mebibytes << 20)


def whole_call(kernel, name, outs, *ins, mebibytes=16, scalars=0, scratch=(), **options):
    specs = [pl.BlockSpec(memory_space=pltpu.SMEM)] * scalars + [VMEM] * (len(ins) - scalars)
    single = not isinstance(outs, (list, tuple))
    return pl.pallas_call(
        functools.partial(kernel, **options),
        name=name,
        out_shape=outs,
        in_specs=specs,
        out_specs=VMEM if single else [VMEM] * len(outs),
        scratch_shapes=scratch,
        compiler_params=limit(mebibytes),
        cost_estimate=NO_COST,
    )(*ins)


CORE = [(i, i ^ 1) for i in range(8)]
ACROSS = [(i, i ^ 2) for i in range(8)]
UP = [(i, i ^ 4) for i in range(8)]
NEAR = [(i, i ^ 1) for i in range(4)]
FAR = [(i, i ^ 2) for i in range(4)]


def swap(value, pairs, axis="fsdp"):
    return lax.ppermute(value, axis, pairs)


def shift(pieces):
    moved = [lax.ppermute(pieces[k], "frame", [(i, i ^ k) for i in range(4)]) for k in (1, 2, 3)]
    return [pieces[0], *moved]


def after(value, *earlier):
    return lax.optimization_barrier((value, *earlier))[0]


class Reduction:
    def __init__(self, where, keep, send):
        self.where, self.keep, self.count, self.width = where, keep, len(keep), keep[0].shape[-1]
        self.got = [swap(v, CORE) for v in send]

    def shape(self, *dims, dtype=BF):
        return shape(*dims, HALF, self.width, dtype=dtype)

    def plane_one(self, *earlier):
        got = [after(g, *earlier) for g in self.got] if earlier else self.got
        n = self.count
        for_x, for_y, self.held = whole_call(
            plane_one_sums,
            "plane_one",
            [self.shape(2 * n), self.shape(2 * n), self.shape(n, 4, dtype=F32)],
            *self.keep,
            *got,
            count=n,
            mebibytes=24,
        )
        self.from_x = swap(for_x, ACROSS)
        self.from_y = swap(for_y, UP)
        return for_x, for_y

    def plane_two(self, *earlier):
        n = self.count
        next_y, next_x, self.left = whole_call(
            plane_two_sums,
            "plane_two",
            [self.shape(n), self.shape(n), self.shape(n, 2, dtype=F32)],
            self.held,
            after(self.from_x, *earlier),
            after(self.from_y, *earlier),
        )
        self.got_y = swap(next_y, UP)
        self.got_x = swap(next_x, ACROSS)
        return next_y, next_x

    def line_one(self, *earlier):
        n = self.count
        out, self.stays = whole_call(
            line_one_sums,
            "line_one",
            [self.shape(n), self.shape(n, dtype=F32)],
            self.where,
            self.left,
            after(self.got_y, *earlier),
            after(self.got_x, *earlier),
            scalars=1,
        )
        self.near = swap(out, NEAR, "frame")
        return (out,)

    def line_two(self, *earlier):
        self.pair = whole_call(
            pair_sums, "line_two", self.shape(self.count), self.stays, after(self.near, *earlier)
        )
        self.far = swap(self.pair, FAR, "frame")
        return (self.pair,)

    def line_three(self, *earlier):
        self.full = whole_call(
            pair_sums, "line_three", self.shape(self.count), self.pair, after(self.far, *earlier)
        )
        self.other = swap(self.full, NEAR, "frame")
        return (self.full,)

    def result(self, parts, outs):
        return whole_call(
            line_result, "line_result", outs, self.where, self.full, self.other, scalars=1, parts=parts
        )


class ReductionChain(Reduction):
    def chain_one(self, *earlier):
        self.mine = whole_call(
            chain_start,
            "chain_start",
            [shape(1, SHARD, self.width)] * self.count,
            self.left,
            after(self.got_y, *earlier),
            after(self.got_x, *earlier),
        )
        self.inward = [swap(v, [(0, 1), (3, 2)], "frame") for v in self.mine]
        self.pair, self.across = [None] * self.count, [None] * self.count
        self.total, self.outward = [None] * self.count, [None] * self.count
        return tuple(self.mine)

    def chain_two(self, i, *earlier):
        out = shape(1, SHARD, self.width)
        self.pair[i] = whole_call(
            pair_sums, "chain_two", out, self.mine[i], after(self.inward[i], *earlier)
        )
        self.across[i] = swap(self.pair[i], [(1, 2), (2, 1)], "frame")
        return (self.pair[i],)

    def chain_three(self, i, *earlier):
        out = shape(1, SHARD, self.width)
        self.total[i] = whole_call(
            pair_sums, "chain_three", out, self.pair[i], after(self.across[i], *earlier)
        )
        self.outward[i] = swap(self.total[i], [(1, 0), (2, 3)], "frame")
        return (self.total[i],)

    def chain_result(self, i, out, *earlier):
        got = after(self.outward[i], *earlier)
        return whole_call(
            chain_result, "chain_result", [out], self.where, self.total[i], got, scalars=1
        )[0]


class ReductionBoth(Reduction):
    def __init__(self, where, keep, send, small):
        super().__init__(where, [keep], [send])
        self.small, self.small_got = small, swap(small, CORE)

    def flat(self, rows, dtype=BF):
        return shape(rows, self.width, dtype=dtype)

    def plane_one(self, *earlier):
        kept = shape(16, D)
        for_x, for_y, self.held, self.kept = whole_call(
            plane_one_both,
            "plane_one_both",
            [self.flat(SHARD + 8), self.flat(SHARD), self.shape(4, dtype=F32), kept],
            self.keep[0],
            after(self.got[0], *earlier),
            self.small,
            self.small_got,
            mebibytes=24,
        )
        self.from_x, self.from_y = swap(for_x, ACROSS), swap(for_y, UP)
        return for_x, for_y

    def plane_two(self, *earlier):
        next_y, next_x, self.left, self.kept = whole_call(
            plane_two_both,
            "plane_two_both",
            [self.flat(HALF + 8), self.flat(HALF), self.shape(2, dtype=F32), shape(16, D)],
            self.held,
            after(self.from_x, *earlier),
            after(self.from_y, *earlier),
            self.kept,
        )
        self.got_y, self.got_x = swap(next_y, UP), swap(next_x, ACROSS)
        return next_y, next_x

    def line_one(self, *earlier):
        out, self.stays, self.kept = whole_call(
            line_one_both,
            "line_one_both",
            [self.flat(HALF + 8), self.flat(HALF, F32), shape(16, D)],
            self.where,
            self.left,
            after(self.got_y, *earlier),
            after(self.got_x, *earlier),
            self.kept,
            scalars=1,
        )
        self.near = swap(out, NEAR, "frame")
        return (out,)

    def line_two(self, *earlier):
        self.pair, self.kept = whole_call(
            line_two_both,
            "line_two_both",
            [self.flat(HALF + 8), shape(16, D)],
            self.stays,
            after(self.near, *earlier),
            self.kept,
        )
        self.far = swap(self.pair, FAR, "frame")
        return (self.pair,)

    def line_three(self, *earlier):
        self.full, self.small = whole_call(
            line_three_both,
            "line_three_both",
            [self.shape(1), shape(16, D, dtype=F32)],
            self.pair,
            after(self.far, *earlier),
            self.kept,
        )
        self.other = swap(self.full, NEAR, "frame")
        return (self.full,)


def body(
    video,
    temporal_entry,
    temporal_exit,
    spatial_entry,
    spatial_exit,
    expand_weight,
    contract_weight,
    layer_gains,
    layer_shifts,
    branch_biases,
    expand_bias,
    cotangent,
):
    own = lax.axis_index("fsdp")
    where = jnp.stack([own, lax.axis_index("frame")]).astype(jnp.int32)
    rows = lambda *parts: jnp.concatenate(parts, axis=0)

    sources = (temporal_entry, temporal_exit, layer_gains, layer_shifts, branch_biases)
    g1a, g1b = pl.pallas_call(
        arrange_parameters,
        name="arrange_parameters",
        out_shape=[shape(HALF + 8, WIDE), shape(HALF, WIDE)],
        in_specs=[pl.BlockSpec(memory_space=pltpu.SMEM), VMEM] + [HBM] * 5,
        out_specs=[VMEM] * 2,
        scratch_shapes=[pltpu.VMEM(v.shape, BF) for v in sources] + [pltpu.SemaphoreType.DMA((5,))],
        compiler_params=limit(8),
        cost_estimate=NO_COST,
    )(
        where,
        expand_bias.reshape(1, 384),
        *(pltpu.with_memory_space_constraint(v, pltpu.HBM) for v in sources),
    )
    x1, y1 = swap(g1a, ACROSS), swap(g1b, UP)

    tokens, cot, *video_pieces = whole_call(
        arrange_tokens,
        "arrange_tokens",
        [shape(ROWS, D), shape(ROWS, D)] + [shape(PIECE, D)] * 4,
        where,
        after(video, g1a),
        cotangent,
        scalars=1,
    )
    video_pieces = shift(video_pieces)

    plane = jnp.concatenate([spatial_entry, spatial_exit], axis=1)
    contract = jnp.concatenate([contract_weight[c * SHARD : (c + 1) * SHARD] for c in range(4)], axis=1)
    x1, y1, plane, contract, *_ = lax.optimization_barrier((x1, y1, plane, contract, tokens))
    to_y = rows(g1a, x1, plane[HALF:])
    to_x = rows(g1b, y1, plane[:HALF])
    r2y, r2x = swap(to_y, UP), swap(to_x, ACROSS)
    c1 = swap(rows(g1a, g1b, x1, y1, r2y[:112], r2x[:96]), CORE)
    to_y = after(rows(plane[:HALF], r2x[96:], contract), *video_pieces[1:])
    to_x = after(rows(plane[HALF:], r2y[112:], expand_weight), *video_pieces[1:])
    r3y, r3x = swap(to_y, UP), swap(to_x, ACROSS)

    *places, normed_place, packed_place, entry_full, exit_full, params, bias_full = pl.pallas_call(
        temporal_forward,
        name="temporal_forward",
        out_shape=[shape(PIECE, D)] * 4
        + [
            kept(SPOTS, D),
            kept(SPOTS, 3 * D),
            kept(D, 3 * D),
            kept(D, D),
            shape(8, WIDE, dtype=F32),
            shape(8, D, dtype=F32),
        ],
        in_specs=[VMEM] * 4 + [HBM] * 7,
        out_specs=[VMEM] * 4 + [KEPT] * 4 + [VMEM] * 2,
        scratch_shapes=[
            pltpu.VMEM((D, WIDE), BF),
            pltpu.VMEM((8, 8, WIDE), BF),
            pltpu.VMEM((ROWS, D), BF),
            pltpu.VMEM((SPOTS, D), BF),
            pltpu.VMEM((SPOTS, 3 * D), BF),
            pltpu.VMEM((SPOTS, D), BF),
            pltpu.SemaphoreType.DMA((24,)),
            pltpu.SemaphoreType.DMA((4,)),
        ],
        compiler_params=limit(24),
        cost_estimate=NO_COST,
    )(after(video_pieces[0], to_y, to_x), *video_pieces[1:], g1a, g1b, x1, y1, r2y, r2x, c1)
    places = shift(places)

    r3y, r3x = after(r3y, *places[1:]), after(r3x, *places[1:])
    c2 = swap(rows(plane, r2x[96:], r2y[112:], r3y[:96], r3x[:96]), CORE)
    to_y = rows(expand_weight, r3x[96:])
    to_x = rows(contract, r3y[96:])
    r4y, r4x = swap(to_y, UP), swap(to_x, ACROSS)
    (
        after_space,
        normed_three,
        space_full,
        last_full,
        blended_time,
        after_time,
        normed_two,
        packed_space,
        blended_space,
    ) = pl.pallas_call(
        spatial_forward,
        name="spatial_forward",
        out_shape=[
            shape(ROWS, D, dtype=F32),
            shape(ROWS, D),
            kept(D, 3 * D),
            kept(D, D),
            kept(ROWS, D),
            kept(ROWS, D, dtype=F32),
            kept(ROWS, D),
            kept(ROWS, 3 * D),
            kept(ROWS, D),
        ],
        in_specs=[VMEM] * 7 + [HBM] * 6,
        out_specs=[VMEM] * 2 + [KEPT] * 7,
        scratch_shapes=[
            pltpu.VMEM((D, WIDE), BF),
            pltpu.VMEM((ROWS, D), BF),
            pltpu.VMEM((ROWS, D), F32),
            pltpu.VMEM((ROWS, D), BF),
            pltpu.VMEM((ROWS, 3 * D), BF),
            pltpu.VMEM((ROWS, D), BF),
            pltpu.VMEM((ROWS, D), BF),
            pltpu.SemaphoreType.DMA((16,)),
            pltpu.SemaphoreType.DMA((7,)),
        ],
        compiler_params=limit(24),
        cost_estimate=NO_COST,
    )(after(tokens, to_y, to_x), params, exit_full, *places, plane, r2y, r2x, r3y, r3x, c2)

    c3 = swap(after(rows(expand_weight, contract, r3x[96:], r3y[96:]), normed_three), CORE)
    c4, c5 = swap(r4y, CORE), swap(r4x, CORE)
    output, grad_after, branch_last, keep_we, send_we, keep_wc, send_wc, small = pl.pallas_call(
        feed_forward,
        name="feed_forward",
        out_shape=[
            shape(*video.shape),
            shape(ROWS, D, dtype=F32),
            shape(ROWS, D),
            shape(4, SHARD, WIDE),
            shape(4, SHARD, WIDE),
            shape(4, SHARD, WIDE),
            shape(4, SHARD, WIDE),
            shape(16, D, dtype=F32),
        ],
        in_specs=[pl.BlockSpec(memory_space=pltpu.SMEM)] + [VMEM] * 5 + [HBM] * 9,
        out_specs=[VMEM] * 8,
        scratch_shapes=[
            pltpu.VMEM((D, WIDE), BF),
            pltpu.VMEM((WIDE, D), BF),
            pltpu.VMEM((ROWS, D), BF),
            pltpu.VMEM((ROWS, D), F32),
            pltpu.VMEM((ROWS, D), F32),
            pltpu.VMEM((D, D), F32),
            pltpu.SemaphoreType.DMA((40,)),
        ],
        compiler_params=limit(28),
        cost_estimate=NO_COST,
    )(
        *(where, normed_three, after_space, cot, params, bias_full),
        *(expand_weight, contract, r3x, r3y, r4y, r4x, c3, c4, c5),
    )
    forward_sum = ReductionChain(where, [keep_we, keep_wc], [send_we, send_wc])

    grad_packed = pl.pallas_call(
        spatial_back,
        name="spatial_back",
        out_shape=shape(ROWS, 3 * D),
        in_specs=[VMEM] * 3,
        out_specs=VMEM,
        scratch_shapes=[pltpu.VMEM((ROWS, D), BF)],
        compiler_params=limit(16),
        cost_estimate=NO_COST,
    )(branch_last, packed_space, last_full)
    placed = forward_sum.plane_one(grad_packed)
    grad_first, branch_first, small, *grad_pieces = whole_call(
        spatial_back_norm,
        "spatial_back_norm",
        [shape(ROWS, D, dtype=F32), shape(ROWS, D), shape(16, D, dtype=F32)] + [shape(PIECE, D)] * 4,
        where,
        grad_packed,
        branch_last,
        grad_after,
        after_time,
        params,
        after(small, *placed),
        space_full,
        exit_full,
        mebibytes=20,
        scalars=1,
    )
    grad_pieces = shift(grad_pieces)

    whole = lambda *dims: pl.BlockSpec(dims, lambda i, w: (0,) * len(dims))

    def grads(*pairs):
        tiles = tuple(b.shape[1] // D for _, b in pairs)
        specs, first = [], 0
        for (a, b), count in zip(pairs, tiles, strict=True):
            at = lambda i, w, first=first, count=count: (0, jnp.clip(i - first, 0, count - 1))
            specs += [whole(*a.shape), pl.BlockSpec((b.shape[0], D), at)]
            first += count
        return pl.pallas_call(
            functools.partial(weight_grads, tiles=tiles),
            name="weight_grads",
            out_shape=[shape(4, SHARD, D * first)] * 2,
            grid_spec=pltpu.PrefetchScalarGridSpec(
                num_scalar_prefetch=1,
                grid=(first,),
                in_specs=specs,
                out_specs=[pl.BlockSpec((4, SHARD, D), lambda i, w: (0, 0, i))] * 2,
                scratch_shapes=[pltpu.VMEM((D, D), F32)],
            ),
            compiler_params=limit(16),
            cost_estimate=NO_COST,
        )(where, *(v for pair in pairs for v in pair))

    keep_space, send_space = grads(
        (blended_time, branch_first), (normed_two, grad_packed), (blended_space, branch_last)
    )
    output = after(jnp.swapaxes(output, 1, 2), send_space)

    grad_place, small, *normed_back = pl.pallas_call(
        temporal_back,
        name="temporal_back",
        out_shape=[shape(SPOTS, 3 * D), shape(16, D, dtype=F32)] + [shape(PIECE, D)] * 4,
        in_specs=[VMEM] * 11,
        out_specs=[VMEM] * 6,
        scratch_shapes=[pltpu.VMEM((ROWS, D), BF), pltpu.VMEM((SPOTS, D), BF)],
        compiler_params=limit(20),
        cost_estimate=NO_COST,
    )(*video_pieces, after(grad_pieces[0], output), *grad_pieces[1:], packed_place, small, entry_full)

    placed = forward_sum.plane_two(small)
    space_sum = ReductionBoth(where, keep_space, after(send_space, *placed), after(small, *placed))
    normed_back = shift([after(v, *placed) for v in normed_back])
    keep_time, send_time = grads((after(normed_place, *placed), grad_place))
    placed = space_sum.plane_one(send_time)
    placed = forward_sum.chain_one(*placed, *normed_back[1:])
    time_sum = Reduction(where, [keep_time], [after(send_time, *placed)])
    input_grad = whole_call(
        input_back,
        "input_back",
        shape(*video.shape, dtype=F32),
        where,
        after(tokens, *placed),
        grad_first,
        params,
        *normed_back,
        scalars=1,
        scratch=[pltpu.VMEM((ROWS, D), BF)],
    )
    placed = forward_sum.chain_two(0, *placed, input_grad)
    placed = space_sum.plane_two(*placed)
    placed = forward_sum.chain_two(1, *placed)
    placed = forward_sum.chain_three(0, *placed)
    placed = space_sum.line_one(*placed)
    placed = time_sum.plane_one(*placed)
    placed = forward_sum.chain_three(1, *placed)
    wide = lambda rows, columns: shape(rows, columns, dtype=F32)
    grad_expand = forward_sum.chain_result(0, wide(SHARD, WIDE), *placed)
    placed = time_sum.plane_two(*placed, grad_expand)
    placed = space_sum.line_two(*placed)
    placed = time_sum.line_one(*placed)
    placed = time_sum.line_two(*placed)
    grad_contract = forward_sum.chain_result(1, wide(4 * SHARD, D), *placed)
    placed = space_sum.line_three(*placed)
    small = space_sum.small
    placed = time_sum.line_three(*placed, grad_contract)
    input_grad = jnp.swapaxes(input_grad, 1, 2)
    grad_exit_time, grad_entry_space, grad_exit_space = space_sum.result(
        ((0, 0, D), (0, D, 3 * D), (0, 4 * D, D)),
        [wide(SHARD, D), wide(SHARD, 3 * D), wide(SHARD, D)],
    )
    time_sum.other = after(time_sum.other, grad_exit_space)
    (grad_entry_time,) = time_sum.result(((0, 0, 3 * D),), [wide(SHARD, 3 * D)])

    mine = lax.dynamic_slice_in_dim(small[:9], own * SHARD, SHARD, axis=1)
    return (
        jnp.swapaxes(output, 1, 2),
        jnp.swapaxes(input_grad, 1, 2),
        grad_entry_time,
        grad_exit_time,
        grad_entry_space,
        grad_exit_space,
        grad_expand,
        grad_contract,
        mine[0:3],
        mine[3:6],
        mine[6:9],
        lax.dynamic_slice_in_dim(small[9:13].reshape(WIDE), own * 384, 384),
    )


def solution(mesh):
    placed = (
        P("fsdp", "frame", None, None),
        P("fsdp", None),
        P("fsdp", None),
        P("fsdp", None),
        P("fsdp", None),
        P("fsdp", None),
        P("fsdp", None),
        P(None, "fsdp"),
        P(None, "fsdp"),
        P(None, "fsdp"),
        P("fsdp"),
        P("fsdp", "frame", None, None),
    )
    special = mesh.shape["fsdp"] == 8 and mesh.shape["frame"] == 4
    return jax.shard_map(
        body if special else general_body,
        mesh=mesh,
        in_specs=placed,
        out_specs=(
            P("fsdp", "frame", None, None),
            P("fsdp", "frame", None, None),
            P("fsdp", None),
            P("fsdp", None),
            P("fsdp", None),
            P("fsdp", None),
            P("fsdp", None),
            P("fsdp", None),
            P(None, "fsdp"),
            P(None, "fsdp"),
            P(None, "fsdp"),
            P("fsdp"),
        ),
        check_vma=False,
    )
```

```python
import functools

import jax
import jax.numpy as jnp
from jax import lax
from jax.experimental import pallas as pl
from jax.experimental.pallas import tpu as pltpu
from jax.sharding import PartitionSpec as P

HEADS = 12


norm_eps = 1e-05


def layer_norm(values, norm_gain, norm_shift):
    average = jnp.mean(values, axis=-1, keepdims=True)
    centred = values - average
    variance = jnp.mean(centred * centred, axis=-1, keepdims=True)
    return centred * lax.rsqrt(variance + norm_eps) * norm_gain + norm_shift


def rounded(values):
    return lax.optimization_barrier(values.astype(jnp.bfloat16)).astype(jnp.float32)


def dense(first_op, second_op):
    return jnp.dot(first_op, second_op, preferred_element_type=jnp.float32)


def dense_left(first_op, second_op):
    return lax.dot_general(
        first_op, second_op, (((0,), (0,)), ((), ())), preferred_element_type=jnp.float32
    )


def dense_right(first_op, second_op):
    return lax.dot_general(
        first_op, second_op, (((1,), (1,)), ((), ())), preferred_element_type=jnp.float32
    )


def split_heads(packed):
    outer = packed.shape
    parted = packed.reshape(outer[:-1] + (3, HEADS, outer[-1] // (3 * HEADS)))
    return (parted[..., 0, :, :], parted[..., 1, :, :], parted[..., 2, :, :])


def attend_forward(packed, layout):
    key_layout = layout.replace("l", "m")
    queries, key_rows, values = split_heads(packed)
    factor = queries.shape[-1] ** (-0.5)
    scores = (
        jnp.einsum(
            layout + "hd," + key_layout + "hd->cqhlm",
            queries,
            key_rows,
            preferred_element_type=jnp.float32,
        )
        * factor
    )
    highest = jnp.max(scores, axis=-1, keepdims=True)
    raised = jnp.exp(scores - highest)
    row_totals = jnp.sum(raised, axis=-1, keepdims=True)
    attention = (raised / row_totals).astype(jnp.bfloat16)
    blended = jnp.einsum(
        "cqhlm," + key_layout + "hd->" + layout + "hd",
        attention,
        values,
        preferred_element_type=jnp.float32,
    )
    outer = packed.shape
    return (
        blended.reshape(outer[:-1] + (outer[-1] // 3,)).astype(jnp.bfloat16),
        highest + jnp.log(row_totals),
    )


def attend_backward(packed, logsum, grad_blended, layout):
    key_layout = layout.replace("l", "m")
    queries, key_rows, values = split_heads(packed)
    factor = queries.shape[-1] ** (-0.5)
    outer = grad_blended.shape
    grad_heads = grad_blended.reshape(outer[:-1] + (HEADS, outer[-1] // HEADS))
    scores = (
        jnp.einsum(
            layout + "hd," + key_layout + "hd->cqhlm",
            queries,
            key_rows,
            preferred_element_type=jnp.float32,
        )
        * factor
    )
    attention = jnp.exp(scores - logsum)
    grad_values = jnp.einsum(
        "cqhlm," + layout + "hd->" + key_layout + "hd",
        attention.astype(jnp.bfloat16),
        grad_heads,
        preferred_element_type=jnp.float32,
    )
    grad_attention = jnp.einsum(
        layout + "hd," + key_layout + "hd->cqhlm",
        grad_heads,
        values,
        preferred_element_type=jnp.float32,
    )
    grad_scores = (
        attention * (grad_attention - jnp.sum(grad_attention * attention, axis=-1, keepdims=True))
    ).astype(jnp.bfloat16)
    grad_queries = (
        jnp.einsum(
            "cqhlm," + key_layout + "hd->" + layout + "hd",
            grad_scores,
            key_rows,
            preferred_element_type=jnp.float32,
        )
        * factor
    )
    grad_keys = (
        jnp.einsum(
            "cqhlm," + layout + "hd->" + key_layout + "hd",
            grad_scores,
            queries,
            preferred_element_type=jnp.float32,
        )
        * factor
    )
    stacked = jnp.stack([grad_queries, grad_keys, grad_values], axis=-3)
    return stacked.reshape(packed.shape).astype(jnp.bfloat16)


def general_body(
    video,
    temporal_entry,
    temporal_exit,
    spatial_entry,
    spatial_exit,
    expand_weight,
    contract_weight,
    layer_gains,
    layer_shifts,
    branch_biases,
    expand_bias,
    cotangent,
):
    clips_here, frames_here, places, model_width = video.shape
    rows_shape = (clips_here, frames_here, places)
    entry_time, exit_time, entry_space, exit_space, gains_low, shifts_low, biases_low = (
        lax.all_gather(temporal_entry, "fsdp", axis=0, tiled=True),
        lax.all_gather(temporal_exit, "fsdp", axis=0, tiled=True),
        lax.all_gather(spatial_entry, "fsdp", axis=0, tiled=True),
        lax.all_gather(spatial_exit, "fsdp", axis=0, tiled=True),
        lax.all_gather(layer_gains, "fsdp", axis=1, tiled=True),
        lax.all_gather(layer_shifts, "fsdp", axis=1, tiled=True),
        lax.all_gather(branch_biases, "fsdp", axis=1, tiled=True),
    )
    expand_full, contract_full, expand_bias_full = (
        lax.all_gather(expand_weight, "fsdp", axis=0, tiled=True),
        lax.all_gather(contract_weight, "fsdp", axis=0, tiled=True),
        lax.all_gather(expand_bias, "fsdp", axis=0, tiled=True),
    )
    gains = gains_low.astype(jnp.float32)
    shifts = shifts_low.astype(jnp.float32)
    biases = biases_low.astype(jnp.float32)
    tokens = video.astype(jnp.float32).reshape(-1, model_width)
    normed_one = layer_norm(tokens, gains[0], shifts[0]).astype(jnp.bfloat16)
    packed_frame = dense(normed_one, entry_time).astype(jnp.bfloat16)
    packed_place = lax.all_to_all(
        packed_frame.reshape(rows_shape + (3 * model_width,)),
        "frame",
        split_axis=2,
        concat_axis=1,
        tiled=True,
    )
    blended_place, logsum_time = attend_forward(packed_place, "clq")
    blended_time = lax.all_to_all(
        blended_place, "frame", split_axis=1, concat_axis=2, tiled=True
    ).reshape(-1, model_width)
    after_time = tokens + (dense(blended_time, exit_time) + biases[0])
    normed_two = layer_norm(after_time, gains[1], shifts[1]).astype(jnp.bfloat16)
    packed_space = (
        dense(normed_two, entry_space).astype(jnp.bfloat16).reshape(rows_shape + (3 * model_width,))
    )
    blended_space, logsum_space = attend_forward(packed_space, "cql")
    blended_rows = blended_space.reshape(-1, model_width)
    after_space = after_time + (dense(blended_rows, exit_space) + biases[1])
    normed_three = layer_norm(after_space, gains[2], shifts[2]).astype(jnp.bfloat16)
    hidden = dense(normed_three, expand_full) + expand_bias_full.astype(jnp.float32)
    active = jax.nn.gelu(hidden, approximate=False).astype(jnp.bfloat16)
    layer_output = (
        (after_space + (dense(active, contract_full) + biases[2]))
        .astype(jnp.bfloat16)
        .reshape(video.shape)
    )
    grad_top = cotangent.astype(jnp.float32).reshape(-1, model_width)
    grad_branch = grad_top.astype(jnp.bfloat16)
    grad_bias_last = jnp.sum(grad_branch.astype(jnp.float32), axis=0)
    grad_contract = dense_left(active, grad_branch)
    grad_active = dense_right(grad_branch, contract_full)
    gelu_pull = jax.vjp(lambda inner: jax.nn.gelu(inner, approximate=False), hidden)[1]
    grad_hidden = gelu_pull(grad_active)[0].astype(jnp.bfloat16)
    grad_expand = dense_left(normed_three, grad_hidden)
    grad_expand_bias = jnp.sum(grad_hidden.astype(jnp.float32), axis=0)
    grad_normed = rounded(dense_right(grad_hidden, expand_full))
    norm_pull = jax.vjp(layer_norm, after_space, gains[2], shifts[2])[1]
    grad_inner, grad_gain_last, grad_shift_last = norm_pull(grad_normed)
    grad_after_space = grad_top + grad_inner
    mlp_parts = (
        lax.psum_scatter(grad_expand, "fsdp", scatter_dimension=0, tiled=True),
        lax.psum_scatter(grad_contract, "fsdp", scatter_dimension=0, tiled=True),
        lax.psum_scatter(grad_expand_bias, "fsdp", scatter_dimension=0, tiled=True),
    )
    grad_branch = grad_after_space.astype(jnp.bfloat16)
    grad_bias_space = jnp.sum(grad_branch.astype(jnp.float32), axis=0)
    grad_exit_space = dense_left(blended_rows, grad_branch)
    grad_blended = (
        dense_right(grad_branch, exit_space)
        .astype(jnp.bfloat16)
        .reshape(rows_shape + (model_width,))
    )
    grad_packed = attend_backward(packed_space, logsum_space, grad_blended, "cql").reshape(
        -1, 3 * model_width
    )
    grad_entry_space = dense_left(normed_two, grad_packed)
    grad_normed = rounded(dense_right(grad_packed, entry_space))
    norm_pull = jax.vjp(layer_norm, after_time, gains[1], shifts[1])[1]
    grad_inner, grad_gain_space, grad_shift_space = norm_pull(grad_normed)
    grad_after_time = grad_after_space + grad_inner
    grad_branch = grad_after_time.astype(jnp.bfloat16)
    grad_bias_time = jnp.sum(grad_branch.astype(jnp.float32), axis=0)
    grad_exit_time = dense_left(blended_time, grad_branch)
    grad_blended = (
        dense_right(grad_branch, exit_time)
        .astype(jnp.bfloat16)
        .reshape(rows_shape + (model_width,))
    )
    grad_blended_place = lax.all_to_all(
        grad_blended, "frame", split_axis=2, concat_axis=1, tiled=True
    )
    grad_packed_place = attend_backward(packed_place, logsum_time, grad_blended_place, "clq")
    grad_packed_frame = lax.all_to_all(
        grad_packed_place, "frame", split_axis=1, concat_axis=2, tiled=True
    ).reshape(-1, 3 * model_width)
    grad_entry_time = dense_left(normed_one, grad_packed_frame)
    grad_normed_one = rounded(dense_right(grad_packed_frame, entry_time))
    norm_pull = jax.vjp(layer_norm, tokens, gains[0], shifts[0])[1]
    grad_inner, grad_gain_time, grad_shift_time = norm_pull(grad_normed_one)
    input_grad = (grad_after_time + grad_inner).reshape(video.shape)
    grad_gains = jnp.stack([grad_gain_time, grad_gain_space, grad_gain_last])
    grad_shifts = jnp.stack([grad_shift_time, grad_shift_space, grad_shift_last])
    grad_biases = jnp.stack([grad_bias_time, grad_bias_space, grad_bias_last])
    attention_parts = (
        lax.psum_scatter(grad_entry_time, "fsdp", scatter_dimension=0, tiled=True),
        lax.psum_scatter(grad_exit_time, "fsdp", scatter_dimension=0, tiled=True),
        lax.psum_scatter(grad_entry_space, "fsdp", scatter_dimension=0, tiled=True),
        lax.psum_scatter(grad_exit_space, "fsdp", scatter_dimension=0, tiled=True),
        lax.psum_scatter(grad_gains, "fsdp", scatter_dimension=1, tiled=True),
        lax.psum_scatter(grad_shifts, "fsdp", scatter_dimension=1, tiled=True),
        lax.psum_scatter(grad_biases, "fsdp", scatter_dimension=1, tiled=True),
    )
    shares = (
        lax.psum_scatter(
            attention_parts[0].astype(jnp.bfloat16), "frame", scatter_dimension=0, tiled=True
        ).astype(jnp.float32),
        lax.psum_scatter(
            attention_parts[1].astype(jnp.bfloat16), "frame", scatter_dimension=0, tiled=True
        ).astype(jnp.float32),
        lax.psum_scatter(
            attention_parts[2].astype(jnp.bfloat16), "frame", scatter_dimension=0, tiled=True
        ).astype(jnp.float32),
        lax.psum_scatter(
            attention_parts[3].astype(jnp.bfloat16), "frame", scatter_dimension=0, tiled=True
        ).astype(jnp.float32),
        lax.psum_scatter(
            mlp_parts[0].astype(jnp.bfloat16), "frame", scatter_dimension=0, tiled=True
        ).astype(jnp.float32),
        lax.psum_scatter(
            mlp_parts[1].astype(jnp.bfloat16), "frame", scatter_dimension=0, tiled=True
        ).astype(jnp.float32),
        lax.psum_scatter(
            jnp.moveaxis(attention_parts[4], 0, 1).astype(jnp.bfloat16),
            "frame",
            scatter_dimension=0,
            tiled=True,
        ).astype(jnp.float32),
        lax.psum_scatter(
            jnp.moveaxis(attention_parts[5], 0, 1).astype(jnp.bfloat16),
            "frame",
            scatter_dimension=0,
            tiled=True,
        ).astype(jnp.float32),
        lax.psum_scatter(
            jnp.moveaxis(attention_parts[6], 0, 1).astype(jnp.bfloat16),
            "frame",
            scatter_dimension=0,
            tiled=True,
        ).astype(jnp.float32),
        lax.psum_scatter(
            mlp_parts[2].astype(jnp.bfloat16), "frame", scatter_dimension=0, tiled=True
        ).astype(jnp.float32),
    )
    pieces = (
        lax.all_gather(shares[0].astype(jnp.bfloat16), "frame", axis=0, tiled=True).astype(
            jnp.float32
        ),
        lax.all_gather(shares[1].astype(jnp.bfloat16), "frame", axis=0, tiled=True).astype(
            jnp.float32
        ),
        lax.all_gather(shares[2].astype(jnp.bfloat16), "frame", axis=0, tiled=True).astype(
            jnp.float32
        ),
        lax.all_gather(shares[3].astype(jnp.bfloat16), "frame", axis=0, tiled=True).astype(
            jnp.float32
        ),
        lax.all_gather(shares[4].astype(jnp.bfloat16), "frame", axis=0, tiled=True).astype(
            jnp.float32
        ),
        lax.all_gather(shares[5].astype(jnp.bfloat16), "frame", axis=0, tiled=True).astype(
            jnp.float32
        ),
        lax.all_gather(shares[6].astype(jnp.bfloat16), "frame", axis=0, tiled=True).astype(
            jnp.float32
        ),
        lax.all_gather(shares[7].astype(jnp.bfloat16), "frame", axis=0, tiled=True).astype(
            jnp.float32
        ),
        lax.all_gather(shares[8].astype(jnp.bfloat16), "frame", axis=0, tiled=True).astype(
            jnp.float32
        ),
        lax.all_gather(shares[9].astype(jnp.bfloat16), "frame", axis=0, tiled=True).astype(
            jnp.float32
        ),
    )
    totals = (
        pieces[0],
        pieces[1],
        pieces[2],
        pieces[3],
        pieces[4],
        pieces[5],
        jnp.moveaxis(pieces[6], 0, 1),
        jnp.moveaxis(pieces[7], 0, 1),
        jnp.moveaxis(pieces[8], 0, 1),
        pieces[9],
    )
    return (
        layer_output,
        input_grad,
        totals[0],
        totals[1],
        totals[2],
        totals[3],
        totals[4],
        totals[5],
        totals[6],
        totals[7],
        totals[8],
        totals[9],
    )


BF = jnp.bfloat16
F32 = jnp.float32
D = 768
FRAME_ROWS = 208
PLACES = 196
HERE = 49
PIECE = 104
ROWS = 416
SPOTS = 400
GROUP = 80
SHARD = 96
HALF = 48
WIDE = 3072
NEG = -1e30
HBM = pl.BlockSpec(memory_space=pl.ANY)
KEPT = pl.BlockSpec(memory_space=pltpu.HBM)
VMEM = pl.BlockSpec(memory_space=pltpu.VMEM)


def nn(a, b):
    return jnp.dot(a, b, preferred_element_type=F32)


def nt(a, b):
    return lax.dot_general(a, b, (((1,), (1,)), ((), ())), preferred_element_type=F32)


def tn(a, b):
    return lax.dot_general(a, b, (((0,), (0,)), ((), ())), preferred_element_type=F32)


def normalised(values):
    average = jnp.mean(values, axis=-1, keepdims=True)
    centred = values - average
    variance = jnp.mean(centred * centred, axis=-1, keepdims=True)
    scale = lax.rsqrt(variance + norm_eps)
    return centred * scale, scale


def norm_back(grad, unit, scale, gain):
    moved = grad * gain
    inner = scale * (
        moved
        - jnp.mean(moved, axis=-1, keepdims=True)
        - unit * jnp.mean(moved * unit, axis=-1, keepdims=True)
    )
    return (
        inner,
        jnp.sum(grad * unit, axis=0, keepdims=True),
        jnp.sum(grad, axis=0, keepdims=True),
    )


def picks(target, columns):
    lanes = lax.broadcasted_iota(jnp.int32, (target.shape[0], columns), 1)
    return jnp.where(lanes == target, 1.0, 0.0).astype(BF)


def row_index(rows):
    return lax.broadcasted_iota(jnp.int32, (rows, 1), 0)


def at_least(value, limit):
    return jnp.where(value >= limit, 1, 0)


def place_from_piece():
    r = row_index(SPOTS)
    col = ((r >> 1) & 3) * PIECE + (r & 1) * HERE + (r >> 3)
    return picks(jnp.where(r < 8 * HERE, col, -1), ROWS)


def piece_parts():
    c = row_index(ROWS)
    k = at_least(c, PIECE) + at_least(c, 2 * PIECE) + at_least(c, 3 * PIECE)
    rem = c - PIECE * k
    f = at_least(rem, HERE)
    return k, f, rem - HERE * f, rem < 2 * HERE


def piece_from_place():
    k, f, p, valid = piece_parts()
    return picks(jnp.where(valid, p * 8 + k * 2 + f, -1), SPOTS)


def frame_from_piece(me):
    r = row_index(ROWS)
    f = at_least(r, FRAME_ROWS)
    spot = r - FRAME_ROWS * f
    q = at_least(spot, HERE) + at_least(spot, 2 * HERE) + at_least(spot, 3 * HERE)
    col = (q ^ me) * PIECE + f * HERE + spot - HERE * q
    return picks(jnp.where(spot < PLACES, col, -1), ROWS)


def piece_from_frame(me):
    k, f, p, valid = piece_parts()
    return picks(jnp.where(valid, f * FRAME_ROWS + HERE * (me ^ k) + p, -1), ROWS)


def split_pieces(rows, refs):
    for k, ref in enumerate(refs):
        ref[...] = rows[k * PIECE : (k + 1) * PIECE]


def stack_pieces(refs, stack):
    for k, ref in enumerate(refs):
        stack[k * PIECE : (k + 1) * PIECE, :] = ref[...]


def small_row(params, index, width=D):
    block = index // 8
    return params[index % 8 : index % 8 + 1, block * D : block * D + width]


def two_heads(value, factor=1.0):
    lane = lax.broadcasted_iota(jnp.int32, (1, 128), 1)
    low = jnp.where(lane < 64, factor, 0.0).astype(BF)
    high = jnp.where(lane < 64, 0.0, factor).astype(BF)
    return jnp.concatenate([value * low, value * high], axis=0)


def joined(value):
    rows = value.shape[0] // 2
    lane = lax.broadcasted_iota(jnp.int32, (rows, 128), 1)
    return jnp.where(lane < 64, value[:rows], value[rows:])


def attend_block(q, k, v, keep):
    scores = jnp.where(keep, nt(two_heads(q, 0.125), k), NEG)
    raised = jnp.exp(scores - jnp.max(scores, axis=-1, keepdims=True))
    weight = raised * (1.0 / jnp.sum(raised, axis=-1, keepdims=True))
    return joined(nn(weight.astype(BF), v)).astype(BF)


def attend_block_back(q, k, v, do, keep):
    scores = jnp.where(keep, nt(k, two_heads(q, 0.125)), NEG)
    raised = jnp.exp(scores - jnp.max(scores, axis=0, keepdims=True))
    weight = raised * (1.0 / jnp.sum(raised, axis=0, keepdims=True))
    both = two_heads(do)
    dv = nn(weight.astype(BF), both)
    dweight = nt(v, both)
    delta = jnp.sum(dweight * weight, axis=0, keepdims=True)
    dscore = (weight * (dweight - delta)).astype(BF)
    dq = joined(tn(dscore, k)) * 0.125
    dk = nn(dscore, two_heads(q, 0.125))
    return dq.astype(BF), dk.astype(BF), dv.astype(BF)


def spot_mask(rows, columns):
    r = lax.broadcasted_iota(jnp.int32, (rows, columns), 0)
    c = lax.broadcasted_iota(jnp.int32, (rows, columns), 1)
    wrap = lambda i, n: i - jnp.where(i >= GROUP, GROUP, 0) if n > GROUP else i
    return (wrap(r, rows) >> 3) == (wrap(c, columns) >> 3)


def wide_product(a_ref, w_ref, out_ref, columns, step, w_offset=0):
    def body(i, carry):
        at = pl.multiple_of(i * step, 128)
        out_ref[:, pl.ds(at, step)] = nn(
            a_ref[...], w_ref[:, pl.ds(at + w_offset, step)]
        ).astype(BF)
        return carry

    lax.fori_loop(0, columns // step, body, 0)


ENTRY_PIECES = (
    ((0, 0, 0, 0), (1, 0, 0, 1), (2, 0, 2, 0), (3, 0, 4, 1))
    + ((4, 0, 4, 0), (4, 56, 6, 0), (5, 0, 2, 1), (5, 48, 6, 1))
    + ((6, 0, 1, 0), (6, 56, 1, 1), (6, 104, 3, 0), (6, 160, 5, 1))
    + ((6, 208, 5, 0), (6, 264, 7, 0), (6, 320, 3, 1), (6, 368, 7, 1))
)
PLANE_PIECES = (
    ((0, 0, 0, 0), (0, 48, 0, 1), (2, 96, 2, 0), (1, 112, 4, 1))
    + ((3, 0, 4, 0), (3, 48, 6, 0), (4, 0, 2, 1), (4, 48, 6, 1))
    + ((5, 0, 1, 0), (5, 48, 1, 1), (5, 96, 3, 0), (5, 144, 5, 1))
    + ((5, 192, 5, 0), (5, 240, 7, 0), (5, 288, 3, 1), (5, 336, 7, 1))
)
EXPAND_PIECES = ((0, 0), (6, 0), (2, 96), (6, 192), (4, 0), (7, 0), (4, 96), (7, 96))
CONTRACT_PIECES = ((1, 0), (6, 96), (5, 0), (8, 0), (3, 96), (6, 288), (5, 96), (8, 96))


def piece_copies(refs, table, own, weights, extra, sems):
    copies = []
    for array, at, relative, half in table:
        rows = pl.ds(pl.multiple_of((own ^ relative) * SHARD + half * HALF, 16), HALF)
        pairs = [(refs[array].at[pl.ds(at, HALF)], weights.at[rows])]
        if half == 0 and extra is not None:
            pairs.append((refs[array].at[pl.ds(at + HALF, 8)], extra.at[relative]))
        for source, target in pairs:
            copies.append(pltpu.make_async_copy(source, target, sems.at[len(copies)]))
    return copies


def arrange_parameters(where, bias, *refs):
    sources, (first, second), held, sems = refs[:5], refs[5:7], refs[7:12], refs[12]
    copies = [
        pltpu.make_async_copy(source, target, sems.at[i])
        for i, (source, target) in enumerate(zip(sources, held, strict=True))
    ]
    for c in copies:
        c.start()
    entry, leave, gains, shifts, biases = held
    own = where[0]
    lane = lax.broadcasted_iota(jnp.int32, (SHARD, D), 1)
    spread = jnp.where(lane == own * SHARD + row_index(SHARD), 1.0, 0.0).astype(BF)
    lane = lax.broadcasted_iota(jnp.int32, (384, D), 1)
    wide = jnp.where(lane == (own & 1) * 384 + row_index(384), 1.0, 0.0).astype(BF)
    four = lax.broadcasted_iota(jnp.int32, (4, D), 0)
    bias_rows = jnp.where(four == own // 2, nn(bias[...], wide), 0.0)
    for c in copies:
        c.wait()
    rows = jnp.concatenate(
        [nn(gains[...], spread), nn(shifts[...], spread), nn(biases[...], spread), bias_rows], axis=0
    )
    rows = jnp.concatenate([rows, jnp.zeros((3, D), F32)], axis=0)
    first[0:HALF, : 3 * D] = entry[0:HALF]
    first[0:HALF, 3 * D :] = leave[0:HALF]
    first[HALF:, :D] = rows[0:8].astype(BF)
    first[HALF:, D : 2 * D] = rows[8:16].astype(BF)
    first[HALF:, 2 * D :] = jnp.zeros((8, 2 * D), BF)
    second[:, : 3 * D] = entry[HALF:]
    second[:, 3 * D :] = leave[HALF:]


def pad_frames(source, target):
    for f in range(2):
        target[f * FRAME_ROWS : f * FRAME_ROWS + PLACES, :] = source[0, f]
        target[f * FRAME_ROWS + PLACES : (f + 1) * FRAME_ROWS, :] = jnp.zeros(
            (FRAME_ROWS - PLACES, D), BF
        )


def arrange_tokens(where, video, tokens, *pieces):
    pad_frames(video, tokens)
    split_pieces(nn(piece_from_frame(where[1]), tokens[...]).astype(BF), pieces)


def temporal_forward(*refs):
    video, pieces, refs = refs[:4], refs[4:11], refs[11:]
    out, refs = refs[:4], refs[4:]
    (normed_out, packed_out, weight_out, leave_out, params_out, bias_out), refs = refs[:6], refs[6:]
    weights, extra, stack, normed_ref, packed_ref, blended, sems, out_sems = refs
    own = lax.axis_index("fsdp")
    copies = piece_copies(pieces, ENTRY_PIECES, own, weights, extra, sems)
    for c in copies:
        c.start()
    stack_pieces(video, stack)
    unit, _ = normalised(stack[...].astype(F32))
    for c in copies:
        c.wait()
    outs = [
        pltpu.make_async_copy(weights.at[:, pl.ds(0, 3 * D)], weight_out, out_sems.at[0]),
        pltpu.make_async_copy(normed_ref, normed_out, out_sems.at[1]),
        pltpu.make_async_copy(packed_ref, packed_out, out_sems.at[2]),
        pltpu.make_async_copy(weights.at[:, pl.ds(3 * D, D)], leave_out, out_sems.at[3]),
    ]
    outs[0].start()
    outs[3].start()
    params = extra[0].astype(F32)
    for k in range(1, 8):
        params = params + extra[k].astype(F32)
    params_out[...] = params
    for r in range(4):
        bias_out[r : r + 1, :] = small_row(params, 9 + r)
    normed = (unit * small_row(params, 0) + small_row(params, 3)).astype(BF)
    normed_ref[...] = nn(place_from_piece(), normed).astype(BF)
    outs[1].start()
    wide_product(normed_ref, weights, packed_ref, 3 * D, D)
    outs[2].start()
    keep = spot_mask(2 * GROUP, GROUP)

    def heads(i, carry):
        at = pl.multiple_of(i * 128, 128)
        for t in range(SPOTS // GROUP):
            rows = pl.ds(t * GROUP, GROUP)
            blended[rows, pl.ds(at, 128)] = attend_block(
                packed_ref[rows, pl.ds(at, 128)],
                packed_ref[rows, pl.ds(at + D, 128)],
                packed_ref[rows, pl.ds(at + 2 * D, 128)],
                keep,
            )
        return carry

    lax.fori_loop(0, HEADS // 2, heads, 0)
    split_pieces(nn(piece_from_place(), blended[...]).astype(BF), out)
    for c in outs:
        c.wait()


def spatial_forward(*refs):
    (tokens, params_ref, w_exit), places, pieces, refs = refs[:3], refs[3:7], refs[7:13], refs[13:]
    after_two, normed_three = refs[:2]
    held, refs = refs[2:9], refs[9:]
    weights, stack, after_ref, normed_ref, packed_ref, blended, blended_time, sems, out_sems = refs
    own = lax.axis_index("fsdp")
    me = lax.axis_index("frame")
    copies = piece_copies(pieces, PLANE_PIECES, own, weights, None, sems)
    for c in copies:
        c.start()
    params = params_ref[...]
    stack_pieces(places, stack)
    blended_time[...] = nn(frame_from_piece(me), stack[...]).astype(BF)
    for c in copies:
        c.wait()
    outs = [
        pltpu.make_async_copy(src, dst, out_sems.at[i])
        for i, (src, dst) in enumerate(
            zip(
                (
                    weights.at[:, pl.ds(0, 3 * D)],
                    weights.at[:, pl.ds(3 * D, D)],
                    blended_time,
                    after_ref,
                    normed_ref,
                    packed_ref,
                    blended,
                ),
                held,
                strict=True,
            )
        )
    ]
    for c in outs[:3]:
        c.start()
    after_time = (
        tokens[...].astype(F32)
        + nn(blended_time[...], w_exit[...])
        + small_row(params, 6)
    )
    after_ref[...] = after_time
    outs[3].start()
    unit, _ = normalised(after_time)
    normed_ref[...] = (unit * small_row(params, 1) + small_row(params, 4)).astype(BF)
    outs[4].start()
    wide_product(normed_ref, weights, packed_ref, 3 * D, D)
    outs[5].start()
    keep = lax.broadcasted_iota(jnp.int32, (2 * FRAME_ROWS, FRAME_ROWS), 1) < PLACES

    def heads(i, carry):
        at = pl.multiple_of(i * 128, 128)
        for f in range(2):
            rows = pl.ds(f * FRAME_ROWS, FRAME_ROWS)
            blended[rows, pl.ds(at, 128)] = attend_block(
                packed_ref[rows, pl.ds(at, 128)],
                packed_ref[rows, pl.ds(at + D, 128)],
                packed_ref[rows, pl.ds(at + 2 * D, 128)],
                keep,
            )
        return carry

    lax.fori_loop(0, HEADS // 2, heads, 0)
    outs[6].start()
    last = after_ref[...] + nn(blended[...], weights[:, 3 * D :]) + small_row(params, 7)
    after_two[...] = last
    unit, _ = normalised(last)
    normed_three[...] = (unit * small_row(params, 2) + small_row(params, 5)).astype(BF)
    for c in outs:
        c.wait()


def feed_forward(where, normed, after_ref, cot, params_ref, bias, *refs):
    pieces, refs = refs[:9], refs[9:]
    (output, grad_after, branch, keep_we, send_we, keep_wc, send_wc, small), refs = refs[:8], refs[8:]
    w_in, w_out, normed_own, total, grad_normed, shuffle, sems = refs
    own = where[0]
    parity = own & 1
    first_copies, later = [], []
    for k, (array, at) in enumerate(EXPAND_PIECES):
        source = pieces[array].at[pl.ds(at, SHARD)]
        first_copies.append(
            pltpu.make_async_copy(source, w_in.at[pl.ds(k * SHARD, SHARD)], sems.at[k])
        )
    for k, (array, at) in enumerate(CONTRACT_PIECES):
        for c in range(4):
            source = pieces[array].at[pl.ds(at, SHARD), pl.ds(c * D, D)]
            spot = (k // 2) * D + (parity ^ (k & 1)) * 384 + c * SHARD
            target = w_out.at[pl.ds(pl.multiple_of(spot, 32), SHARD)]
            later.append(pltpu.make_async_copy(source, target, sems.at[8 + len(later)]))
    for c in first_copies + later:
        c.start()

    column = lax.broadcasted_iota(jnp.int32, (1, D), 1)
    block = (column * 683) >> 16
    order = (own ^ block) * SHARD + column - block * SHARD
    chosen = jnp.where(
        lax.broadcasted_iota(jnp.int32, (D, D), 0) == order, jnp.ones((), F32), jnp.zeros((), F32)
    ).astype(BF)
    normed_own[...] = nn(normed[...], chosen).astype(BF)
    total[...] = jnp.zeros_like(total)
    grad_normed[...] = jnp.zeros_like(grad_normed)
    small[...] = jnp.zeros_like(small)
    for c in first_copies + later:
        c.wait()

    def step(p, carry):
        chip = (own >> 1) ^ p
        at = pl.ds(pl.multiple_of(chip * D, D), D)
        rows = pl.ds(pl.multiple_of(p * D, D), D)
        hidden = nn(normed_own[...], w_in[:, at]) + bias[pl.ds(chip, 1), :]
        area = 0.5 + 0.5 * lax.erf(hidden * 0.7071067811865476)
        slope = area + hidden * (0.3989422804014327 * jnp.exp(-0.5 * hidden * hidden))
        active = (hidden * area).astype(BF)
        total[...] += nn(active, w_out[rows, :])
        grad_hidden = (nt(cot[...], w_out[rows, :]) * slope).astype(BF)
        grad_normed[...] += nt(grad_hidden, w_in[:, at])
        small[pl.ds(9 + chip, 1), :] = jnp.sum(grad_hidden.astype(F32), axis=0, keepdims=True)
        shuffle[...] = tn(active, cot[...]).astype(BF)
        for kind, ref in ((parity, keep_wc), (1 - parity, send_wc)):
            for c in range(4):
                rows = pl.ds(pl.multiple_of(kind * 384 + c * SHARD, 32), SHARD)
                ref[p, :, c * D : (c + 1) * D] = shuffle[rows, :]
        moved = tn(normed_own[...], grad_hidden).astype(BF)
        for j in range(4):
            keep_we[j, :, at] = moved[2 * j * SHARD : (2 * j + 1) * SHARD]
            send_we[j, :, at] = moved[(2 * j + 1) * SHARD : (2 * j + 2) * SHARD]
        return carry

    lax.fori_loop(0, 4, step, 0)
    params = params_ref[...]
    values = after_ref[...]
    result = (values + (total[...] + small_row(params, 8))).astype(BF)
    for f in range(2):
        output[0, f] = result[f * FRAME_ROWS : f * FRAME_ROWS + PLACES]
    unit, scale = normalised(values)
    dn = nt(grad_normed[...].astype(BF), chosen)
    inner, dgain, dshift = norm_back(dn, unit, scale, small_row(params, 2))
    top = cot[...].astype(F32)
    dafter = top + inner
    grad_after[...] = dafter
    branch[...] = dafter.astype(BF)
    small[2:3, :] = dgain
    small[5:6, :] = dshift
    small[8:9, :] = jnp.sum(top, axis=0, keepdims=True)


def spatial_back(branch, packed, w_last, grad_packed, grad_blended):
    grad_blended[...] = nt(branch[...], w_last[...]).astype(BF)
    keep = lax.broadcasted_iota(jnp.int32, (FRAME_ROWS, 2 * FRAME_ROWS), 0) < PLACES

    def heads(i, carry):
        at = pl.multiple_of(i * 128, 128)
        for f in range(2):
            rows = pl.ds(f * FRAME_ROWS, FRAME_ROWS)
            dq, dk, dv = attend_block_back(
                packed[rows, pl.ds(at, 128)],
                packed[rows, pl.ds(at + D, 128)],
                packed[rows, pl.ds(at + 2 * D, 128)],
                grad_blended[rows, pl.ds(at, 128)],
                keep,
            )
            grad_packed[rows, pl.ds(at, 128)] = dq
            grad_packed[rows, pl.ds(at + D, 128)] = dk
            grad_packed[rows, pl.ds(at + 2 * D, 128)] = dv
        return carry

    lax.fori_loop(0, HEADS // 2, heads, 0)


def spatial_back_norm(where, *refs):
    grad_packed, branch, grad_after, after_ref, params_ref, small_in, w_entry, w_exit = refs[:8]
    grad_first, branch_first, small, *pieces = refs[8:]
    params = params_ref[...]
    dn = nt(grad_packed[...], w_entry[...]).astype(BF).astype(F32)
    unit, scale = normalised(after_ref[...])
    inner, dgain, dshift = norm_back(dn, unit, scale, small_row(params, 1))
    first = grad_after[...] + inner
    grad_first[...] = first
    low = first.astype(BF)
    branch_first[...] = low
    back = nt(low, w_exit[...]).astype(BF)
    split_pieces(nn(piece_from_frame(where[1]), back).astype(BF), pieces)
    small[...] = small_in[...]
    small[1:2, :] = dgain
    small[4:5, :] = dshift
    small[6:7, :] = jnp.sum(low.astype(F32), axis=0, keepdims=True)
    small[7:8, :] = jnp.sum(branch[...].astype(F32), axis=0, keepdims=True)


def temporal_back(*refs):
    video, pieces, (packed, small_in, weights), refs = refs[:4], refs[4:8], refs[8:11], refs[11:]
    (grad_packed, small), out, (stack, grads) = refs[:2], refs[2:6], refs[6:]
    stack_pieces(pieces, stack)
    grads[...] = nn(place_from_piece(), stack[...]).astype(BF)
    keep = spot_mask(GROUP, 2 * GROUP)

    def heads(i, carry):
        at = pl.multiple_of(i * 128, 128)
        for t in range(SPOTS // GROUP):
            rows = pl.ds(t * GROUP, GROUP)
            dq, dk, dv = attend_block_back(
                packed[rows, pl.ds(at, 128)],
                packed[rows, pl.ds(at + D, 128)],
                packed[rows, pl.ds(at + 2 * D, 128)],
                grads[rows, pl.ds(at, 128)],
                keep,
            )
            grad_packed[rows, pl.ds(at, 128)] = dq
            grad_packed[rows, pl.ds(at + D, 128)] = dk
            grad_packed[rows, pl.ds(at + 2 * D, 128)] = dv
        return carry

    lax.fori_loop(0, HEADS // 2, heads, 0)
    dn = nt(grad_packed[...], weights[...]).astype(BF)
    moved = nn(piece_from_place(), dn)
    split_pieces(moved.astype(BF), out)
    stack_pieces(video, stack)
    unit, _ = normalised(stack[...].astype(F32))
    small[...] = small_in[...]
    small[0:1, :] = jnp.sum(moved * unit, axis=0, keepdims=True)
    small[3:4, :] = jnp.sum(moved, axis=0, keepdims=True)


def input_back(where, tokens, grad_first, params_ref, *refs):
    pieces, (out, stack) = refs[:4], refs[4:]
    stack_pieces(pieces, stack)
    dn = nn(frame_from_piece(where[1]), stack[...])
    unit, scale = normalised(tokens[...].astype(F32))
    moved = dn * small_row(params_ref[...], 0)
    inner = scale * (
        moved
        - jnp.mean(moved, axis=-1, keepdims=True)
        - unit * jnp.mean(moved * unit, axis=-1, keepdims=True)
    )
    total = grad_first[...] + inner
    for f in range(2):
        out[0, f] = total[f * FRAME_ROWS : f * FRAME_ROWS + PLACES]


def weight_grads(where, *refs, tiles):
    step = pl.program_id(0)
    own = where[0]
    pairs, (keep, send, shuffle) = refs[: 2 * len(tiles)], refs[2 * len(tiles) :]
    first = 0
    for i, count in enumerate(tiles):

        @pl.when((step >= first) & (step < first + count))
        def _(i=i):
            shuffle[...] = tn(pairs[2 * i][...], pairs[2 * i + 1][...]).astype(BF)

        first += count
    for j in range(4):
        for parity, ref in ((0, keep), (1, send)):
            rows = pl.ds(pl.multiple_of((own ^ (2 * j + parity)) * SHARD, 32), SHARD)
            ref[j] = shuffle[rows, :]


def by_columns(width, step):
    def run(i, carry):
        step(pl.ds(pl.multiple_of(i * 384, 128), 384))
        return carry

    lax.fori_loop(0, width // 384, run, 0)


def plane_one_sums(*refs, count):
    keeps, gots, (for_x, for_y, held) = refs[:count], refs[count : 2 * count], refs[2 * count :]

    def step(at):
        for i, (keep, got) in enumerate(zip(keeps, gots, strict=True)):
            total = [keep[j, :, at].astype(F32) + got[j, :, at].astype(F32) for j in range(4)]
            for_x[2 * i, :, at] = total[1][:HALF].astype(BF)
            for_x[2 * i + 1, :, at] = total[3][:HALF].astype(BF)
            for_y[2 * i, :, at] = total[2][HALF:].astype(BF)
            for_y[2 * i + 1, :, at] = total[3][HALF:].astype(BF)
            held[i, 0, :, at] = total[0][:HALF]
            held[i, 1, :, at] = total[0][HALF:]
            held[i, 2, :, at] = total[2][:HALF]
            held[i, 3, :, at] = total[1][HALF:]

    by_columns(keeps[0].shape[-1], step)


def plane_two_sums(held, from_x, from_y, next_y, next_x, left):
    def step(at):
        for i in range(held.shape[0]):
            next_y[i, :, at] = (held[i, 2, :, at] + from_x[2 * i + 1, :, at].astype(F32)).astype(BF)
            next_x[i, :, at] = (held[i, 3, :, at] + from_y[2 * i + 1, :, at].astype(F32)).astype(BF)
            left[i, 0, :, at] = held[i, 0, :, at] + from_x[2 * i, :, at].astype(F32)
            left[i, 1, :, at] = held[i, 1, :, at] + from_y[2 * i, :, at].astype(F32)

    by_columns(held.shape[-1], step)


def line_one_sums(where, left, got_y, got_x, out, stays):
    odd = where[1] & 1

    def step(at):
        for i in range(left.shape[0]):
            first = left[i, 0, :, at] + got_y[i, :, at].astype(F32)
            second = left[i, 1, :, at] + got_x[i, :, at].astype(F32)
            out[i, :, at] = jnp.where(odd == 1, first, second).astype(BF)
            stays[i, :, at] = jnp.where(odd == 1, second, first)

    by_columns(left.shape[-1], step)


def pair_sums(one, two, out):
    def step(at):
        for i in range(out.shape[0]):
            out[i, :, at] = (one[i, :, at].astype(F32) + two[i, :, at].astype(F32)).astype(BF)

    by_columns(out.shape[-1], step)


def line_result(where, full, other, *outs, parts):
    odd = where[1] & 1
    for out, (i, first, columns) in zip(outs, parts, strict=True):
        for block in range(columns // D):
            at = slice(first + block * D, first + (block + 1) * D)
            one, two = full[i, :, at].astype(F32), other[i, :, at].astype(F32)
            low = jnp.where(odd == 1, two, one)
            high = jnp.where(odd == 1, one, two)
            if out.shape[1] == D:
                out[block * SHARD : block * SHARD + HALF, :] = low
                out[block * SHARD + HALF : (block + 1) * SHARD, :] = high
            else:
                out[:HALF, block * D : (block + 1) * D] = low
                out[HALF:, block * D : (block + 1) * D] = high


def chain_start(left, got_y, got_x, *outs):
    def step(at):
        for i, out in enumerate(outs):
            out[0, :HALF, at] = (left[i, 0, :, at] + got_y[i, :, at].astype(F32)).astype(BF)
            out[0, HALF:, at] = (left[i, 1, :, at] + got_x[i, :, at].astype(F32)).astype(BF)

    by_columns(left.shape[-1], step)


def chain_result(where, *refs):
    inner = (where[1] == 1) | (where[1] == 2)
    count = len(refs) // 3
    for total, got, out in zip(refs[:count], refs[count : 2 * count], refs[2 * count :], strict=True):
        for block in range(total.shape[-1] // D):
            at = slice(block * D, (block + 1) * D)
            value = jnp.where(inner, total[0, :, at].astype(F32), got[0, :, at].astype(F32))
            if out.shape[1] == D:
                out[block * SHARD : (block + 1) * SHARD, :] = value
            else:
                out[:, at] = value


def put_small(target, at, value):
    target[at : at + 8, :D] = value[:8]
    target[at : at + 8, D : 2 * D] = value[8:]
    target[at : at + 8, 2 * D :] = jnp.zeros((8, target.shape[1] - 2 * D), BF)


def add_small(kept, source, at):
    got = source[at : at + 8, : 2 * D].astype(F32)
    return kept[...].astype(F32) + jnp.concatenate([got[:, :D], got[:, D:]], axis=0)


def plane_one_both(keep, got, small, small_got, for_x, for_y, held, kept):
    def step(at):
        total = [keep[j, :, at].astype(F32) + got[j, :, at].astype(F32) for j in range(4)]
        for_x[:HALF, at] = total[1][:HALF].astype(BF)
        for_x[HALF:SHARD, at] = total[3][:HALF].astype(BF)
        for_y[:HALF, at] = total[2][HALF:].astype(BF)
        for_y[HALF:, at] = total[3][HALF:].astype(BF)
        held[0, :, at] = total[0][:HALF]
        held[1, :, at] = total[0][HALF:]
        held[2, :, at] = total[2][:HALF]
        held[3, :, at] = total[1][HALF:]

    by_columns(keep.shape[-1], step)
    value = (small[...] + small_got[...]).astype(BF)
    kept[...] = value
    put_small(for_x, SHARD, value)


def plane_two_both(held, from_x, from_y, kept, next_y, next_x, left, kept_next):
    def step(at):
        next_y[:HALF, at] = (held[2, :, at] + from_x[HALF:SHARD, at].astype(F32)).astype(BF)
        next_x[:, at] = (held[3, :, at] + from_y[HALF:, at].astype(F32)).astype(BF)
        left[0, :, at] = held[0, :, at] + from_x[:HALF, at].astype(F32)
        left[1, :, at] = held[1, :, at] + from_y[:HALF, at].astype(F32)

    by_columns(held.shape[-1], step)
    value = add_small(kept, from_x, SHARD).astype(BF)
    kept_next[...] = value
    put_small(next_y, HALF, value)


def line_one_both(where, left, got_y, got_x, kept, out, stays, kept_next):
    odd = where[1] & 1

    def step(at):
        first = left[0, :, at] + got_y[:HALF, at].astype(F32)
        second = left[1, :, at] + got_x[:, at].astype(F32)
        out[:HALF, at] = jnp.where(odd == 1, first, second).astype(BF)
        stays[:, at] = jnp.where(odd == 1, second, first)

    by_columns(left.shape[-1], step)
    value = add_small(kept, got_y, HALF).astype(BF)
    kept_next[...] = value
    put_small(out, HALF, value)


def line_two_both(stays, near, kept, pair, kept_next):
    def step(at):
        pair[:HALF, at] = (stays[:, at] + near[:HALF, at].astype(F32)).astype(BF)

    by_columns(stays.shape[-1], step)
    value = add_small(kept, near, HALF).astype(BF)
    kept_next[...] = value
    put_small(pair, HALF, value)


def line_three_both(pair, far, kept, full, small):
    def step(at):
        full[0, :, at] = (pair[:HALF, at].astype(F32) + far[:HALF, at].astype(F32)).astype(BF)

    by_columns(full.shape[-1], step)
    small[...] = add_small(kept, far, HALF)


def shape(*dims, dtype=BF):
    return jax.ShapeDtypeStruct(dims, dtype)


def kept(*dims, dtype=BF):
    return pltpu.HBM(dims, dtype)


NO_COST = pl.CostEstimate(flops=1000, bytes_accessed=1000, transcendentals=0)


def limit(mebibytes):
    return pltpu.CompilerParams(vmem_limit_bytes=mebibytes << 20)


def whole_call(kernel, name, outs, *ins, mebibytes=16, scalars=0, scratch=(), **options):
    specs = [pl.BlockSpec(memory_space=pltpu.SMEM)] * scalars + [VMEM] * (len(ins) - scalars)
    single = not isinstance(outs, (list, tuple))
    return pl.pallas_call(
        functools.partial(kernel, **options),
        name=name,
        out_shape=outs,
        in_specs=specs,
        out_specs=VMEM if single else [VMEM] * len(outs),
        scratch_shapes=scratch,
        compiler_params=limit(mebibytes),
        cost_estimate=NO_COST,
    )(*ins)


CORE = [(i, i ^ 1) for i in range(8)]
ACROSS = [(i, i ^ 2) for i in range(8)]
UP = [(i, i ^ 4) for i in range(8)]
NEAR = [(i, i ^ 1) for i in range(4)]
FAR = [(i, i ^ 2) for i in range(4)]


def swap(value, pairs, axis="fsdp"):
    return lax.ppermute(value, axis, pairs)


def shift(pieces):
    moved = [lax.ppermute(pieces[k], "frame", [(i, i ^ k) for i in range(4)]) for k in (1, 2, 3)]
    return [pieces[0], *moved]


def after(value, *earlier):
    return lax.optimization_barrier((value, *earlier))[0]


class Reduction:
    def __init__(self, where, keep, send):
        self.where, self.keep, self.count, self.width = where, keep, len(keep), keep[0].shape[-1]
        self.got = [swap(v, CORE) for v in send]

    def shape(self, *dims, dtype=BF):
        return shape(*dims, HALF, self.width, dtype=dtype)

    def plane_one(self, *earlier):
        got = [after(g, *earlier) for g in self.got] if earlier else self.got
        n = self.count
        for_x, for_y, self.held = whole_call(
            plane_one_sums,
            "plane_one",
            [self.shape(2 * n), self.shape(2 * n), self.shape(n, 4, dtype=F32)],
            *self.keep,
            *got,
            count=n,
            mebibytes=24,
        )
        self.from_x = swap(for_x, ACROSS)
        self.from_y = swap(for_y, UP)
        return for_x, for_y

    def plane_two(self, *earlier):
        n = self.count
        next_y, next_x, self.left = whole_call(
            plane_two_sums,
            "plane_two",
            [self.shape(n), self.shape(n), self.shape(n, 2, dtype=F32)],
            self.held,
            after(self.from_x, *earlier),
            after(self.from_y, *earlier),
        )
        self.got_y = swap(next_y, UP)
        self.got_x = swap(next_x, ACROSS)
        return next_y, next_x

    def line_one(self, *earlier):
        n = self.count
        out, self.stays = whole_call(
            line_one_sums,
            "line_one",
            [self.shape(n), self.shape(n, dtype=F32)],
            self.where,
            self.left,
            after(self.got_y, *earlier),
            after(self.got_x, *earlier),
            scalars=1,
        )
        self.near = swap(out, NEAR, "frame")
        return (out,)

    def line_two(self, *earlier):
        self.pair = whole_call(
            pair_sums, "line_two", self.shape(self.count), self.stays, after(self.near, *earlier)
        )
        self.far = swap(self.pair, FAR, "frame")
        return (self.pair,)

    def line_three(self, *earlier):
        self.full = whole_call(
            pair_sums, "line_three", self.shape(self.count), self.pair, after(self.far, *earlier)
        )
        self.other = swap(self.full, NEAR, "frame")
        return (self.full,)

    def result(self, parts, outs):
        return whole_call(
            line_result, "line_result", outs, self.where, self.full, self.other, scalars=1, parts=parts
        )


class ReductionChain(Reduction):
    def chain_one(self, *earlier):
        self.mine = whole_call(
            chain_start,
            "chain_start",
            [shape(1, SHARD, self.width)] * self.count,
            self.left,
            after(self.got_y, *earlier),
            after(self.got_x, *earlier),
        )
        self.inward = [swap(v, [(0, 1), (3, 2)], "frame") for v in self.mine]
        self.pair, self.across = [None] * self.count, [None] * self.count
        self.total, self.outward = [None] * self.count, [None] * self.count
        return tuple(self.mine)

    def chain_two(self, i, *earlier):
        out = shape(1, SHARD, self.width)
        self.pair[i] = whole_call(
            pair_sums, "chain_two", out, self.mine[i], after(self.inward[i], *earlier)
        )
        self.across[i] = swap(self.pair[i], [(1, 2), (2, 1)], "frame")
        return (self.pair[i],)

    def chain_three(self, i, *earlier):
        out = shape(1, SHARD, self.width)
        self.total[i] = whole_call(
            pair_sums, "chain_three", out, self.pair[i], after(self.across[i], *earlier)
        )
        self.outward[i] = swap(self.total[i], [(1, 0), (2, 3)], "frame")
        return (self.total[i],)

    def chain_result(self, i, out, *earlier):
        got = after(self.outward[i], *earlier)
        return whole_call(
            chain_result, "chain_result", [out], self.where, self.total[i], got, scalars=1
        )[0]


class ReductionBoth(Reduction):
    def join(self, small):
        self.small, self.small_got = small, swap(small, CORE)

    def flat(self, rows, dtype=BF):
        return shape(rows, self.width, dtype=dtype)

    def plane_one(self, *earlier):
        kept = shape(16, D)
        for_x, for_y, self.held, self.kept = whole_call(
            plane_one_both,
            "plane_one_both",
            [self.flat(SHARD + 8), self.flat(SHARD), self.shape(4, dtype=F32), kept],
            self.keep[0],
            after(self.got[0], *earlier),
            self.small,
            self.small_got,
            mebibytes=24,
        )
        self.from_x, self.from_y = swap(for_x, ACROSS), swap(for_y, UP)
        return for_x, for_y

    def plane_two(self, *earlier):
        next_y, next_x, self.left, self.kept = whole_call(
            plane_two_both,
            "plane_two_both",
            [self.flat(HALF + 8), self.flat(HALF), self.shape(2, dtype=F32), shape(16, D)],
            self.held,
            after(self.from_x, *earlier),
            after(self.from_y, *earlier),
            self.kept,
        )
        self.got_y, self.got_x = swap(next_y, UP), swap(next_x, ACROSS)
        return next_y, next_x

    def line_one(self, *earlier):
        out, self.stays, self.kept = whole_call(
            line_one_both,
            "line_one_both",
            [self.flat(HALF + 8), self.flat(HALF, F32), shape(16, D)],
            self.where,
            self.left,
            after(self.got_y, *earlier),
            after(self.got_x, *earlier),
            self.kept,
            scalars=1,
        )
        self.near = swap(out, NEAR, "frame")
        return (out,)

    def line_two(self, *earlier):
        self.pair, self.kept = whole_call(
            line_two_both,
            "line_two_both",
            [self.flat(HALF + 8), shape(16, D)],
            self.stays,
            after(self.near, *earlier),
            self.kept,
        )
        self.far = swap(self.pair, FAR, "frame")
        return (self.pair,)

    def line_three(self, *earlier):
        self.full, self.small = whole_call(
            line_three_both,
            "line_three_both",
            [self.shape(1), shape(16, D, dtype=F32)],
            self.pair,
            after(self.far, *earlier),
            self.kept,
        )
        self.other = swap(self.full, NEAR, "frame")
        return (self.full,)


def body(
    video,
    temporal_entry,
    temporal_exit,
    spatial_entry,
    spatial_exit,
    expand_weight,
    contract_weight,
    layer_gains,
    layer_shifts,
    branch_biases,
    expand_bias,
    cotangent,
):
    own = lax.axis_index("fsdp")
    where = jnp.stack([own, lax.axis_index("frame")]).astype(jnp.int32)
    rows = lambda *parts: jnp.concatenate(parts, axis=0)

    sources = (temporal_entry, temporal_exit, layer_gains, layer_shifts, branch_biases)
    g1a, g1b = pl.pallas_call(
        arrange_parameters,
        name="arrange_parameters",
        out_shape=[shape(HALF + 8, WIDE), shape(HALF, WIDE)],
        in_specs=[pl.BlockSpec(memory_space=pltpu.SMEM), VMEM] + [HBM] * 5,
        out_specs=[VMEM] * 2,
        scratch_shapes=[pltpu.VMEM(v.shape, BF) for v in sources] + [pltpu.SemaphoreType.DMA((5,))],
        compiler_params=limit(8),
        cost_estimate=NO_COST,
    )(
        where,
        expand_bias.reshape(1, 384),
        *(pltpu.with_memory_space_constraint(v, pltpu.HBM) for v in sources),
    )
    x1, y1 = swap(g1a, ACROSS), swap(g1b, UP)

    tokens, *video_pieces = whole_call(
        arrange_tokens,
        "arrange_tokens",
        [shape(ROWS, D)] + [shape(PIECE, D)] * 4,
        where,
        after(video, g1a),
        scalars=1,
    )
    video_pieces = shift(video_pieces)

    plane = jnp.concatenate([spatial_entry, spatial_exit], axis=1)
    contract = jnp.concatenate([contract_weight[c * SHARD : (c + 1) * SHARD] for c in range(4)], axis=1)
    x1, y1, plane, contract, *_ = lax.optimization_barrier((x1, y1, plane, contract, tokens))
    to_y = rows(g1a, x1, plane[HALF:])
    to_x = rows(g1b, y1, plane[:HALF])
    r2y, r2x = swap(to_y, UP), swap(to_x, ACROSS)
    c1 = swap(rows(g1a, g1b, x1, y1, r2y[:112], r2x[:96]), CORE)
    cot = whole_call(pad_frames, "arrange_cotangent", shape(ROWS, D), after(cotangent, r2y))
    to_y = after(rows(plane[:HALF], r2x[96:], contract), *video_pieces[1:])
    to_x = after(rows(plane[HALF:], r2y[112:], expand_weight), *video_pieces[1:])
    r3y, r3x = swap(to_y, UP), swap(to_x, ACROSS)

    *places, normed_place, packed_place, entry_full, exit_full, params, bias_full = pl.pallas_call(
        temporal_forward,
        name="temporal_forward",
        out_shape=[shape(PIECE, D)] * 4
        + [
            kept(SPOTS, D),
            kept(SPOTS, 3 * D),
            kept(D, 3 * D),
            kept(D, D),
            shape(8, WIDE, dtype=F32),
            shape(8, D, dtype=F32),
        ],
        in_specs=[VMEM] * 4 + [HBM] * 7,
        out_specs=[VMEM] * 4 + [KEPT] * 4 + [VMEM] * 2,
        scratch_shapes=[
            pltpu.VMEM((D, WIDE), BF),
            pltpu.VMEM((8, 8, WIDE), BF),
            pltpu.VMEM((ROWS, D), BF),
            pltpu.VMEM((SPOTS, D), BF),
            pltpu.VMEM((SPOTS, 3 * D), BF),
            pltpu.VMEM((SPOTS, D), BF),
            pltpu.SemaphoreType.DMA((24,)),
            pltpu.SemaphoreType.DMA((4,)),
        ],
        compiler_params=limit(24),
        cost_estimate=NO_COST,
    )(after(video_pieces[0], to_y, to_x), *video_pieces[1:], g1a, g1b, x1, y1, r2y, r2x, c1)
    places = shift(places)

    r3y, r3x = after(r3y, *places[1:]), after(r3x, *places[1:])
    c2 = swap(rows(plane, r2x[96:], r2y[112:], r3y[:96], r3x[:96]), CORE)
    to_y = rows(expand_weight, r3x[96:])
    to_x = rows(contract, r3y[96:])
    r4y, r4x = swap(to_y, UP), swap(to_x, ACROSS)
    (
        after_space,
        normed_three,
        space_full,
        last_full,
        blended_time,
        after_time,
        normed_two,
        packed_space,
        blended_space,
    ) = pl.pallas_call(
        spatial_forward,
        name="spatial_forward",
        out_shape=[
            shape(ROWS, D, dtype=F32),
            shape(ROWS, D),
            kept(D, 3 * D),
            kept(D, D),
            kept(ROWS, D),
            kept(ROWS, D, dtype=F32),
            kept(ROWS, D),
            kept(ROWS, 3 * D),
            kept(ROWS, D),
        ],
        in_specs=[VMEM] * 7 + [HBM] * 6,
        out_specs=[VMEM] * 2 + [KEPT] * 7,
        scratch_shapes=[
            pltpu.VMEM((D, WIDE), BF),
            pltpu.VMEM((ROWS, D), BF),
            pltpu.VMEM((ROWS, D), F32),
            pltpu.VMEM((ROWS, D), BF),
            pltpu.VMEM((ROWS, 3 * D), BF),
            pltpu.VMEM((ROWS, D), BF),
            pltpu.VMEM((ROWS, D), BF),
            pltpu.SemaphoreType.DMA((16,)),
            pltpu.SemaphoreType.DMA((7,)),
        ],
        compiler_params=limit(24),
        cost_estimate=NO_COST,
    )(after(tokens, to_y, to_x, cot), params, exit_full, *places, plane, r2y, r2x, r3y, r3x, c2)

    c3 = swap(after(rows(expand_weight, contract, r3x[96:], r3y[96:]), normed_three), CORE)
    c4, c5 = swap(r4y, CORE), swap(r4x, CORE)
    output, grad_after, branch_last, keep_we, send_we, keep_wc, send_wc, small = pl.pallas_call(
        feed_forward,
        name="feed_forward",
        out_shape=[
            shape(*video.shape),
            shape(ROWS, D, dtype=F32),
            shape(ROWS, D),
            shape(4, SHARD, WIDE),
            shape(4, SHARD, WIDE),
            shape(4, SHARD, WIDE),
            shape(4, SHARD, WIDE),
            shape(16, D, dtype=F32),
        ],
        in_specs=[pl.BlockSpec(memory_space=pltpu.SMEM)] + [VMEM] * 5 + [HBM] * 9,
        out_specs=[VMEM] * 8,
        scratch_shapes=[
            pltpu.VMEM((D, WIDE), BF),
            pltpu.VMEM((WIDE, D), BF),
            pltpu.VMEM((ROWS, D), BF),
            pltpu.VMEM((ROWS, D), F32),
            pltpu.VMEM((ROWS, D), F32),
            pltpu.VMEM((D, D), BF),
            pltpu.SemaphoreType.DMA((40,)),
        ],
        compiler_params=limit(28),
        cost_estimate=NO_COST,
    )(
        *(where, normed_three, after_space, cot, params, bias_full),
        *(expand_weight, contract, r3x, r3y, r4y, r4x, c3, c4, c5),
    )
    forward_sum = ReductionChain(where, [keep_we, keep_wc], [send_we, send_wc])

    grad_packed = pl.pallas_call(
        spatial_back,
        name="spatial_back",
        out_shape=shape(ROWS, 3 * D),
        in_specs=[VMEM] * 3,
        out_specs=VMEM,
        scratch_shapes=[pltpu.VMEM((ROWS, D), BF)],
        compiler_params=limit(16),
        cost_estimate=NO_COST,
    )(branch_last, packed_space, last_full)
    placed = forward_sum.plane_one(grad_packed)
    grad_first, branch_first, small, *grad_pieces = whole_call(
        spatial_back_norm,
        "spatial_back_norm",
        [shape(ROWS, D, dtype=F32), shape(ROWS, D), shape(16, D, dtype=F32)] + [shape(PIECE, D)] * 4,
        where,
        grad_packed,
        branch_last,
        grad_after,
        after_time,
        params,
        after(small, *placed),
        space_full,
        exit_full,
        mebibytes=20,
        scalars=1,
    )
    grad_pieces = shift(grad_pieces)

    whole = lambda *dims: pl.BlockSpec(dims, lambda i, w: (0,) * len(dims))

    def grads(*pairs):
        tiles = tuple(b.shape[1] // D for _, b in pairs)
        specs, first = [], 0
        for (a, b), count in zip(pairs, tiles, strict=True):
            at = lambda i, w, first=first, count=count: (0, jnp.clip(i - first, 0, count - 1))
            specs += [whole(*a.shape), pl.BlockSpec((b.shape[0], D), at)]
            first += count
        return pl.pallas_call(
            functools.partial(weight_grads, tiles=tiles),
            name="weight_grads",
            out_shape=[shape(4, SHARD, D * first)] * 2,
            grid_spec=pltpu.PrefetchScalarGridSpec(
                num_scalar_prefetch=1,
                grid=(first,),
                in_specs=specs,
                out_specs=[pl.BlockSpec((4, SHARD, D), lambda i, w: (0, 0, i))] * 2,
                scratch_shapes=[pltpu.VMEM((D, D), BF)],
            ),
            compiler_params=limit(16),
            cost_estimate=NO_COST,
        )(where, *(v for pair in pairs for v in pair))

    keep_space, send_space = grads(
        (blended_time, branch_first), (normed_two, grad_packed), (blended_space, branch_last)
    )
    output = after(jnp.swapaxes(output, 1, 2), send_space)

    grad_place, small, *normed_back = pl.pallas_call(
        temporal_back,
        name="temporal_back",
        out_shape=[shape(SPOTS, 3 * D), shape(16, D, dtype=F32)] + [shape(PIECE, D)] * 4,
        in_specs=[VMEM] * 11,
        out_specs=[VMEM] * 6,
        scratch_shapes=[pltpu.VMEM((ROWS, D), BF), pltpu.VMEM((SPOTS, D), BF)],
        compiler_params=limit(20),
        cost_estimate=NO_COST,
    )(*video_pieces, after(grad_pieces[0], output), *grad_pieces[1:], packed_place, small, entry_full)

    placed = forward_sum.plane_two(small)
    space_sum = ReductionBoth(where, [keep_space], [after(send_space, *placed)])
    space_sum.join(after(small, *placed))
    normed_back = shift([after(v, *placed) for v in normed_back])
    keep_time, send_time = grads((after(normed_place, *placed), grad_place))
    placed = space_sum.plane_one(send_time)
    placed = forward_sum.chain_one(*placed, *normed_back[1:])
    time_sum = Reduction(where, [keep_time], [after(send_time, *placed)])
    input_grad = whole_call(
        input_back,
        "input_back",
        shape(*video.shape, dtype=F32),
        where,
        after(tokens, *placed),
        grad_first,
        params,
        *normed_back,
        scalars=1,
        scratch=[pltpu.VMEM((ROWS, D), BF)],
    )
    placed = forward_sum.chain_two(0, *placed, input_grad)
    placed = space_sum.plane_two(*placed)
    placed = forward_sum.chain_two(1, *placed)
    placed = forward_sum.chain_three(0, *placed)
    placed = space_sum.line_one(*placed)
    placed = time_sum.plane_one(*placed)
    placed = forward_sum.chain_three(1, *placed)
    wide = lambda rows, columns: shape(rows, columns, dtype=F32)
    grad_expand = forward_sum.chain_result(0, wide(SHARD, WIDE), *placed)
    placed = time_sum.plane_two(*placed, grad_expand)
    placed = space_sum.line_two(*placed)
    placed = time_sum.line_one(*placed)
    placed = time_sum.line_two(*placed)
    grad_contract = forward_sum.chain_result(1, wide(4 * SHARD, D), *placed)
    placed = space_sum.line_three(*placed)
    small = space_sum.small
    placed = time_sum.line_three(*placed, grad_contract)
    input_grad = jnp.swapaxes(input_grad, 1, 2)
    grad_exit_time, grad_entry_space, grad_exit_space = space_sum.result(
        ((0, 0, D), (0, D, 3 * D), (0, 4 * D, D)),
        [wide(SHARD, D), wide(SHARD, 3 * D), wide(SHARD, D)],
    )
    time_sum.other = after(time_sum.other, grad_exit_space)
    (grad_entry_time,) = time_sum.result(((0, 0, 3 * D),), [wide(SHARD, 3 * D)])

    mine = lax.dynamic_slice_in_dim(small[:9], own * SHARD, SHARD, axis=1)
    return (
        jnp.swapaxes(output, 1, 2),
        jnp.swapaxes(input_grad, 1, 2),
        grad_entry_time,
        grad_exit_time,
        grad_entry_space,
        grad_exit_space,
        grad_expand,
        grad_contract,
        mine[0:3],
        mine[3:6],
        mine[6:9],
        lax.dynamic_slice_in_dim(small[9:13].reshape(WIDE), own * 384, 384),
    )


def solution(mesh):
    placed = (
        P("fsdp", "frame", None, None),
        P("fsdp", None),
        P("fsdp", None),
        P("fsdp", None),
        P("fsdp", None),
        P("fsdp", None),
        P("fsdp", None),
        P(None, "fsdp"),
        P(None, "fsdp"),
        P(None, "fsdp"),
        P("fsdp"),
        P("fsdp", "frame", None, None),
    )
    special = mesh.shape["fsdp"] == 8 and mesh.shape["frame"] == 4
    return jax.shard_map(
        body if special else general_body,
        mesh=mesh,
        in_specs=placed,
        out_specs=(
            P("fsdp", "frame", None, None),
            P("fsdp", "frame", None, None),
            P("fsdp", None),
            P("fsdp", None),
            P("fsdp", None),
            P("fsdp", None),
            P("fsdp", None),
            P("fsdp", None),
            P(None, "fsdp"),
            P(None, "fsdp"),
            P(None, "fsdp"),
            P("fsdp"),
        ),
        check_vma=False,
    )
```

```python
import functools

import jax
import jax.numpy as jnp
from jax import lax
from jax.experimental import pallas as pl
from jax.experimental.pallas import tpu as pltpu
from jax.sharding import PartitionSpec as P

HEADS = 12


norm_eps = 1e-05


def layer_norm(values, norm_gain, norm_shift):
    average = jnp.mean(values, axis=-1, keepdims=True)
    centred = values - average
    variance = jnp.mean(centred * centred, axis=-1, keepdims=True)
    return centred * lax.rsqrt(variance + norm_eps) * norm_gain + norm_shift


def rounded(values):
    return lax.optimization_barrier(values.astype(jnp.bfloat16)).astype(jnp.float32)


def dense(first_op, second_op):
    return jnp.dot(first_op, second_op, preferred_element_type=jnp.float32)


def dense_left(first_op, second_op):
    return lax.dot_general(
        first_op, second_op, (((0,), (0,)), ((), ())), preferred_element_type=jnp.float32
    )


def dense_right(first_op, second_op):
    return lax.dot_general(
        first_op, second_op, (((1,), (1,)), ((), ())), preferred_element_type=jnp.float32
    )


def split_heads(packed):
    outer = packed.shape
    parted = packed.reshape(outer[:-1] + (3, HEADS, outer[-1] // (3 * HEADS)))
    return (parted[..., 0, :, :], parted[..., 1, :, :], parted[..., 2, :, :])


def attend_forward(packed, layout):
    key_layout = layout.replace("l", "m")
    queries, key_rows, values = split_heads(packed)
    factor = queries.shape[-1] ** (-0.5)
    scores = (
        jnp.einsum(
            layout + "hd," + key_layout + "hd->cqhlm",
            queries,
            key_rows,
            preferred_element_type=jnp.float32,
        )
        * factor
    )
    highest = jnp.max(scores, axis=-1, keepdims=True)
    raised = jnp.exp(scores - highest)
    row_totals = jnp.sum(raised, axis=-1, keepdims=True)
    attention = (raised / row_totals).astype(jnp.bfloat16)
    blended = jnp.einsum(
        "cqhlm," + key_layout + "hd->" + layout + "hd",
        attention,
        values,
        preferred_element_type=jnp.float32,
    )
    outer = packed.shape
    return (
        blended.reshape(outer[:-1] + (outer[-1] // 3,)).astype(jnp.bfloat16),
        highest + jnp.log(row_totals),
    )


def attend_backward(packed, logsum, grad_blended, layout):
    key_layout = layout.replace("l", "m")
    queries, key_rows, values = split_heads(packed)
    factor = queries.shape[-1] ** (-0.5)
    outer = grad_blended.shape
    grad_heads = grad_blended.reshape(outer[:-1] + (HEADS, outer[-1] // HEADS))
    scores = (
        jnp.einsum(
            layout + "hd," + key_layout + "hd->cqhlm",
            queries,
            key_rows,
            preferred_element_type=jnp.float32,
        )
        * factor
    )
    attention = jnp.exp(scores - logsum)
    grad_values = jnp.einsum(
        "cqhlm," + layout + "hd->" + key_layout + "hd",
        attention.astype(jnp.bfloat16),
        grad_heads,
        preferred_element_type=jnp.float32,
    )
    grad_attention = jnp.einsum(
        layout + "hd," + key_layout + "hd->cqhlm",
        grad_heads,
        values,
        preferred_element_type=jnp.float32,
    )
    grad_scores = (
        attention * (grad_attention - jnp.sum(grad_attention * attention, axis=-1, keepdims=True))
    ).astype(jnp.bfloat16)
    grad_queries = (
        jnp.einsum(
            "cqhlm," + key_layout + "hd->" + layout + "hd",
            grad_scores,
            key_rows,
            preferred_element_type=jnp.float32,
        )
        * factor
    )
    grad_keys = (
        jnp.einsum(
            "cqhlm," + layout + "hd->" + key_layout + "hd",
            grad_scores,
            queries,
            preferred_element_type=jnp.float32,
        )
        * factor
    )
    stacked = jnp.stack([grad_queries, grad_keys, grad_values], axis=-3)
    return stacked.reshape(packed.shape).astype(jnp.bfloat16)


def general_body(
    video,
    temporal_entry,
    temporal_exit,
    spatial_entry,
    spatial_exit,
    expand_weight,
    contract_weight,
    layer_gains,
    layer_shifts,
    branch_biases,
    expand_bias,
    cotangent,
):
    clips_here, frames_here, places, model_width = video.shape
    rows_shape = (clips_here, frames_here, places)
    entry_time, exit_time, entry_space, exit_space, gains_low, shifts_low, biases_low = (
        lax.all_gather(temporal_entry, "fsdp", axis=0, tiled=True),
        lax.all_gather(temporal_exit, "fsdp", axis=0, tiled=True),
        lax.all_gather(spatial_entry, "fsdp", axis=0, tiled=True),
        lax.all_gather(spatial_exit, "fsdp", axis=0, tiled=True),
        lax.all_gather(layer_gains, "fsdp", axis=1, tiled=True),
        lax.all_gather(layer_shifts, "fsdp", axis=1, tiled=True),
        lax.all_gather(branch_biases, "fsdp", axis=1, tiled=True),
    )
    expand_full, contract_full, expand_bias_full = (
        lax.all_gather(expand_weight, "fsdp", axis=0, tiled=True),
        lax.all_gather(contract_weight, "fsdp", axis=0, tiled=True),
        lax.all_gather(expand_bias, "fsdp", axis=0, tiled=True),
    )
    gains = gains_low.astype(jnp.float32)
    shifts = shifts_low.astype(jnp.float32)
    biases = biases_low.astype(jnp.float32)
    tokens = video.astype(jnp.float32).reshape(-1, model_width)
    normed_one = layer_norm(tokens, gains[0], shifts[0]).astype(jnp.bfloat16)
    packed_frame = dense(normed_one, entry_time).astype(jnp.bfloat16)
    packed_place = lax.all_to_all(
        packed_frame.reshape(rows_shape + (3 * model_width,)),
        "frame",
        split_axis=2,
        concat_axis=1,
        tiled=True,
    )
    blended_place, logsum_time = attend_forward(packed_place, "clq")
    blended_time = lax.all_to_all(
        blended_place, "frame", split_axis=1, concat_axis=2, tiled=True
    ).reshape(-1, model_width)
    after_time = tokens + (dense(blended_time, exit_time) + biases[0])
    normed_two = layer_norm(after_time, gains[1], shifts[1]).astype(jnp.bfloat16)
    packed_space = (
        dense(normed_two, entry_space).astype(jnp.bfloat16).reshape(rows_shape + (3 * model_width,))
    )
    blended_space, logsum_space = attend_forward(packed_space, "cql")
    blended_rows = blended_space.reshape(-1, model_width)
    after_space = after_time + (dense(blended_rows, exit_space) + biases[1])
    normed_three = layer_norm(after_space, gains[2], shifts[2]).astype(jnp.bfloat16)
    hidden = dense(normed_three, expand_full) + expand_bias_full.astype(jnp.float32)
    active = jax.nn.gelu(hidden, approximate=False).astype(jnp.bfloat16)
    layer_output = (
        (after_space + (dense(active, contract_full) + biases[2]))
        .astype(jnp.bfloat16)
        .reshape(video.shape)
    )
    grad_top = cotangent.astype(jnp.float32).reshape(-1, model_width)
    grad_branch = grad_top.astype(jnp.bfloat16)
    grad_bias_last = jnp.sum(grad_branch.astype(jnp.float32), axis=0)
    grad_contract = dense_left(active, grad_branch)
    grad_active = dense_right(grad_branch, contract_full)
    gelu_pull = jax.vjp(lambda inner: jax.nn.gelu(inner, approximate=False), hidden)[1]
    grad_hidden = gelu_pull(grad_active)[0].astype(jnp.bfloat16)
    grad_expand = dense_left(normed_three, grad_hidden)
    grad_expand_bias = jnp.sum(grad_hidden.astype(jnp.float32), axis=0)
    grad_normed = rounded(dense_right(grad_hidden, expand_full))
    norm_pull = jax.vjp(layer_norm, after_space, gains[2], shifts[2])[1]
    grad_inner, grad_gain_last, grad_shift_last = norm_pull(grad_normed)
    grad_after_space = grad_top + grad_inner
    mlp_parts = (
        lax.psum_scatter(grad_expand, "fsdp", scatter_dimension=0, tiled=True),
        lax.psum_scatter(grad_contract, "fsdp", scatter_dimension=0, tiled=True),
        lax.psum_scatter(grad_expand_bias, "fsdp", scatter_dimension=0, tiled=True),
    )
    grad_branch = grad_after_space.astype(jnp.bfloat16)
    grad_bias_space = jnp.sum(grad_branch.astype(jnp.float32), axis=0)
    grad_exit_space = dense_left(blended_rows, grad_branch)
    grad_blended = (
        dense_right(grad_branch, exit_space)
        .astype(jnp.bfloat16)
        .reshape(rows_shape + (model_width,))
    )
    grad_packed = attend_backward(packed_space, logsum_space, grad_blended, "cql").reshape(
        -1, 3 * model_width
    )
    grad_entry_space = dense_left(normed_two, grad_packed)
    grad_normed = rounded(dense_right(grad_packed, entry_space))
    norm_pull = jax.vjp(layer_norm, after_time, gains[1], shifts[1])[1]
    grad_inner, grad_gain_space, grad_shift_space = norm_pull(grad_normed)
    grad_after_time = grad_after_space + grad_inner
    grad_branch = grad_after_time.astype(jnp.bfloat16)
    grad_bias_time = jnp.sum(grad_branch.astype(jnp.float32), axis=0)
    grad_exit_time = dense_left(blended_time, grad_branch)
    grad_blended = (
        dense_right(grad_branch, exit_time)
        .astype(jnp.bfloat16)
        .reshape(rows_shape + (model_width,))
    )
    grad_blended_place = lax.all_to_all(
        grad_blended, "frame", split_axis=2, concat_axis=1, tiled=True
    )
    grad_packed_place = attend_backward(packed_place, logsum_time, grad_blended_place, "clq")
    grad_packed_frame = lax.all_to_all(
        grad_packed_place, "frame", split_axis=1, concat_axis=2, tiled=True
    ).reshape(-1, 3 * model_width)
    grad_entry_time = dense_left(normed_one, grad_packed_frame)
    grad_normed_one = rounded(dense_right(grad_packed_frame, entry_time))
    norm_pull = jax.vjp(layer_norm, tokens, gains[0], shifts[0])[1]
    grad_inner, grad_gain_time, grad_shift_time = norm_pull(grad_normed_one)
    input_grad = (grad_after_time + grad_inner).reshape(video.shape)
    grad_gains = jnp.stack([grad_gain_time, grad_gain_space, grad_gain_last])
    grad_shifts = jnp.stack([grad_shift_time, grad_shift_space, grad_shift_last])
    grad_biases = jnp.stack([grad_bias_time, grad_bias_space, grad_bias_last])
    attention_parts = (
        lax.psum_scatter(grad_entry_time, "fsdp", scatter_dimension=0, tiled=True),
        lax.psum_scatter(grad_exit_time, "fsdp", scatter_dimension=0, tiled=True),
        lax.psum_scatter(grad_entry_space, "fsdp", scatter_dimension=0, tiled=True),
        lax.psum_scatter(grad_exit_space, "fsdp", scatter_dimension=0, tiled=True),
        lax.psum_scatter(grad_gains, "fsdp", scatter_dimension=1, tiled=True),
        lax.psum_scatter(grad_shifts, "fsdp", scatter_dimension=1, tiled=True),
        lax.psum_scatter(grad_biases, "fsdp", scatter_dimension=1, tiled=True),
    )
    shares = (
        lax.psum_scatter(
            attention_parts[0].astype(jnp.bfloat16), "frame", scatter_dimension=0, tiled=True
        ).astype(jnp.float32),
        lax.psum_scatter(
            attention_parts[1].astype(jnp.bfloat16), "frame", scatter_dimension=0, tiled=True
        ).astype(jnp.float32),
        lax.psum_scatter(
            attention_parts[2].astype(jnp.bfloat16), "frame", scatter_dimension=0, tiled=True
        ).astype(jnp.float32),
        lax.psum_scatter(
            attention_parts[3].astype(jnp.bfloat16), "frame", scatter_dimension=0, tiled=True
        ).astype(jnp.float32),
        lax.psum_scatter(
            mlp_parts[0].astype(jnp.bfloat16), "frame", scatter_dimension=0, tiled=True
        ).astype(jnp.float32),
        lax.psum_scatter(
            mlp_parts[1].astype(jnp.bfloat16), "frame", scatter_dimension=0, tiled=True
        ).astype(jnp.float32),
        lax.psum_scatter(
            jnp.moveaxis(attention_parts[4], 0, 1).astype(jnp.bfloat16),
            "frame",
            scatter_dimension=0,
            tiled=True,
        ).astype(jnp.float32),
        lax.psum_scatter(
            jnp.moveaxis(attention_parts[5], 0, 1).astype(jnp.bfloat16),
            "frame",
            scatter_dimension=0,
            tiled=True,
        ).astype(jnp.float32),
        lax.psum_scatter(
            jnp.moveaxis(attention_parts[6], 0, 1).astype(jnp.bfloat16),
            "frame",
            scatter_dimension=0,
            tiled=True,
        ).astype(jnp.float32),
        lax.psum_scatter(
            mlp_parts[2].astype(jnp.bfloat16), "frame", scatter_dimension=0, tiled=True
        ).astype(jnp.float32),
    )
    pieces = (
        lax.all_gather(shares[0].astype(jnp.bfloat16), "frame", axis=0, tiled=True).astype(
            jnp.float32
        ),
        lax.all_gather(shares[1].astype(jnp.bfloat16), "frame", axis=0, tiled=True).astype(
            jnp.float32
        ),
        lax.all_gather(shares[2].astype(jnp.bfloat16), "frame", axis=0, tiled=True).astype(
            jnp.float32
        ),
        lax.all_gather(shares[3].astype(jnp.bfloat16), "frame", axis=0, tiled=True).astype(
            jnp.float32
        ),
        lax.all_gather(shares[4].astype(jnp.bfloat16), "frame", axis=0, tiled=True).astype(
            jnp.float32
        ),
        lax.all_gather(shares[5].astype(jnp.bfloat16), "frame", axis=0, tiled=True).astype(
            jnp.float32
        ),
        lax.all_gather(shares[6].astype(jnp.bfloat16), "frame", axis=0, tiled=True).astype(
            jnp.float32
        ),
        lax.all_gather(shares[7].astype(jnp.bfloat16), "frame", axis=0, tiled=True).astype(
            jnp.float32
        ),
        lax.all_gather(shares[8].astype(jnp.bfloat16), "frame", axis=0, tiled=True).astype(
            jnp.float32
        ),
        lax.all_gather(shares[9].astype(jnp.bfloat16), "frame", axis=0, tiled=True).astype(
            jnp.float32
        ),
    )
    totals = (
        pieces[0],
        pieces[1],
        pieces[2],
        pieces[3],
        pieces[4],
        pieces[5],
        jnp.moveaxis(pieces[6], 0, 1),
        jnp.moveaxis(pieces[7], 0, 1),
        jnp.moveaxis(pieces[8], 0, 1),
        pieces[9],
    )
    return (
        layer_output,
        input_grad,
        totals[0],
        totals[1],
        totals[2],
        totals[3],
        totals[4],
        totals[5],
        totals[6],
        totals[7],
        totals[8],
        totals[9],
    )


BF = jnp.bfloat16
F32 = jnp.float32
D = 768
FRAME_ROWS = 208
PLACES = 196
HERE = 49
PIECE = 104
ROWS = 416
SPOTS = 400
GROUP = 80
SHARD = 96
HALF = 48
WIDE = 3072
NEG = -1e30
HBM = pl.BlockSpec(memory_space=pl.ANY)
KEPT = pl.BlockSpec(memory_space=pltpu.HBM)
VMEM = pl.BlockSpec(memory_space=pltpu.VMEM)


def nn(a, b):
    return jnp.dot(a, b, preferred_element_type=F32)


def nt(a, b):
    return lax.dot_general(a, b, (((1,), (1,)), ((), ())), preferred_element_type=F32)


def tn(a, b):
    return lax.dot_general(a, b, (((0,), (0,)), ((), ())), preferred_element_type=F32)


def normalised(values):
    average = jnp.mean(values, axis=-1, keepdims=True)
    centred = values - average
    variance = jnp.mean(centred * centred, axis=-1, keepdims=True)
    scale = lax.rsqrt(variance + norm_eps)
    return centred * scale, scale


def norm_back(grad, unit, scale, gain):
    moved = grad * gain
    inner = scale * (
        moved
        - jnp.mean(moved, axis=-1, keepdims=True)
        - unit * jnp.mean(moved * unit, axis=-1, keepdims=True)
    )
    return (
        inner,
        jnp.sum(grad * unit, axis=0, keepdims=True),
        jnp.sum(grad, axis=0, keepdims=True),
    )


def picks(target, columns):
    lanes = lax.broadcasted_iota(jnp.int32, (target.shape[0], columns), 1)
    return jnp.where(lanes == target, 1.0, 0.0).astype(BF)


def row_index(rows):
    return lax.broadcasted_iota(jnp.int32, (rows, 1), 0)


def at_least(value, limit):
    return jnp.where(value >= limit, 1, 0)


def place_from_piece():
    r = row_index(SPOTS)
    col = ((r >> 1) & 3) * PIECE + (r & 1) * HERE + (r >> 3)
    return picks(jnp.where(r < 8 * HERE, col, -1), ROWS)


def piece_parts():
    c = row_index(ROWS)
    k = at_least(c, PIECE) + at_least(c, 2 * PIECE) + at_least(c, 3 * PIECE)
    rem = c - PIECE * k
    f = at_least(rem, HERE)
    return k, f, rem - HERE * f, rem < 2 * HERE


def piece_from_place():
    k, f, p, valid = piece_parts()
    return picks(jnp.where(valid, p * 8 + k * 2 + f, -1), SPOTS)


def frame_from_piece(me):
    r = row_index(ROWS)
    f = at_least(r, FRAME_ROWS)
    spot = r - FRAME_ROWS * f
    q = at_least(spot, HERE) + at_least(spot, 2 * HERE) + at_least(spot, 3 * HERE)
    col = (q ^ me) * PIECE + f * HERE + spot - HERE * q
    return picks(jnp.where(spot < PLACES, col, -1), ROWS)


def piece_from_frame(me):
    k, f, p, valid = piece_parts()
    return picks(jnp.where(valid, f * FRAME_ROWS + HERE * (me ^ k) + p, -1), ROWS)


def split_pieces(rows, refs):
    for k, ref in enumerate(refs):
        ref[...] = rows[k * PIECE : (k + 1) * PIECE]


def stack_pieces(refs, stack):
    for k, ref in enumerate(refs):
        stack[k * PIECE : (k + 1) * PIECE, :] = ref[...]


def small_row(params, index, width=D):
    block = index // 8
    return params[index % 8 : index % 8 + 1, block * D : block * D + width]


def two_heads(value, factor=1.0):
    lane = lax.broadcasted_iota(jnp.int32, (1, 128), 1)
    low = jnp.where(lane < 64, factor, 0.0).astype(BF)
    high = jnp.where(lane < 64, 0.0, factor).astype(BF)
    return jnp.concatenate([value * low, value * high], axis=0)


def joined(value):
    rows = value.shape[0] // 2
    lane = lax.broadcasted_iota(jnp.int32, (rows, 128), 1)
    return jnp.where(lane < 64, value[:rows], value[rows:])


def attend_block(q, k, v, keep):
    scores = jnp.where(keep, nt(two_heads(q, 0.125), k), NEG)
    raised = jnp.exp(scores - jnp.max(scores, axis=-1, keepdims=True))
    weight = raised * (1.0 / jnp.sum(raised, axis=-1, keepdims=True))
    return joined(nn(weight.astype(BF), v)).astype(BF)


def attend_block_back(q, k, v, do, keep):
    scores = jnp.where(keep, nt(k, two_heads(q, 0.125)), NEG)
    raised = jnp.exp(scores - jnp.max(scores, axis=0, keepdims=True))
    weight = raised * (1.0 / jnp.sum(raised, axis=0, keepdims=True))
    both = two_heads(do)
    dv = nn(weight.astype(BF), both)
    dweight = nt(v, both)
    delta = jnp.sum(dweight * weight, axis=0, keepdims=True)
    dscore = (weight * (dweight - delta)).astype(BF)
    dq = joined(tn(dscore, k)) * 0.125
    dk = nn(dscore, two_heads(q, 0.125))
    return dq.astype(BF), dk.astype(BF), dv.astype(BF)


def spot_mask(rows, columns):
    r = lax.broadcasted_iota(jnp.int32, (rows, columns), 0)
    c = lax.broadcasted_iota(jnp.int32, (rows, columns), 1)
    wrap = lambda i, n: i - jnp.where(i >= GROUP, GROUP, 0) if n > GROUP else i
    return (wrap(r, rows) >> 3) == (wrap(c, columns) >> 3)


def wide_product(a_ref, w_ref, out_ref, columns, step, w_offset=0):
    def body(i, carry):
        at = pl.multiple_of(i * step, 128)
        out_ref[:, pl.ds(at, step)] = nn(
            a_ref[...], w_ref[:, pl.ds(at + w_offset, step)]
        ).astype(BF)
        return carry

    lax.fori_loop(0, columns // step, body, 0)


ENTRY_PIECES = (
    ((0, 0, 0, 0), (1, 0, 0, 1), (2, 0, 2, 0), (3, 0, 4, 1))
    + ((4, 0, 4, 0), (4, 56, 6, 0), (5, 0, 2, 1), (5, 48, 6, 1))
    + ((6, 0, 1, 0), (6, 56, 1, 1), (6, 104, 3, 0), (6, 160, 5, 1))
    + ((6, 208, 5, 0), (6, 264, 7, 0), (6, 320, 3, 1), (6, 368, 7, 1))
)
PLANE_PIECES = (
    ((0, 0, 0, 0), (0, 48, 0, 1), (2, 96, 2, 0), (1, 112, 4, 1))
    + ((3, 0, 4, 0), (3, 48, 6, 0), (4, 0, 2, 1), (4, 48, 6, 1))
    + ((5, 0, 1, 0), (5, 48, 1, 1), (5, 96, 3, 0), (5, 144, 5, 1))
    + ((5, 192, 5, 0), (5, 240, 7, 0), (5, 288, 3, 1), (5, 336, 7, 1))
)
EXPAND_PIECES = ((0, 0), (6, 0), (2, 96), (6, 192), (4, 0), (7, 0), (4, 96), (7, 96))
CONTRACT_PIECES = ((1, 0), (6, 96), (5, 0), (8, 0), (3, 96), (6, 288), (5, 96), (8, 96))


def piece_copies(refs, table, own, weights, extra, sems):
    copies = []
    for array, at, relative, half in table:
        rows = pl.ds(pl.multiple_of((own ^ relative) * SHARD + half * HALF, 16), HALF)
        pairs = [(refs[array].at[pl.ds(at, HALF)], weights.at[rows])]
        if half == 0 and extra is not None:
            pairs.append((refs[array].at[pl.ds(at + HALF, 8)], extra.at[relative]))
        for source, target in pairs:
            copies.append(pltpu.make_async_copy(source, target, sems.at[len(copies)]))
    return copies


def arrange_parameters(where, *refs):
    sources, (first, second), held, sems = refs[:6], refs[6:8], refs[8:14], refs[14]
    copies = [
        pltpu.make_async_copy(source, target, sems.at[i])
        for i, (source, target) in enumerate(zip(sources, held, strict=True))
    ]
    for c in copies:
        c.start()
    entry, leave, gains, shifts, biases, bias = held
    own = where[0]
    lane = lax.broadcasted_iota(jnp.int32, (SHARD, D), 1)
    spread = jnp.where(lane == own * SHARD + row_index(SHARD), 1.0, 0.0).astype(BF)
    lane = lax.broadcasted_iota(jnp.int32, (384, D), 1)
    wide = jnp.where(lane == (own & 1) * 384 + row_index(384), 1.0, 0.0).astype(BF)
    four = lax.broadcasted_iota(jnp.int32, (4, D), 0)
    for c in copies:
        c.wait()
    bias_rows = jnp.where(four == own // 2, nn(bias[...].reshape(1, 384), wide), 0.0)
    rows = jnp.concatenate(
        [nn(gains[...], spread), nn(shifts[...], spread), nn(biases[...], spread), bias_rows], axis=0
    )
    rows = jnp.concatenate([rows, jnp.zeros((3, D), F32)], axis=0)
    first[0:HALF, : 3 * D] = entry[0:HALF]
    first[0:HALF, 3 * D :] = leave[0:HALF]
    first[HALF:, :D] = rows[0:8].astype(BF)
    first[HALF:, D : 2 * D] = rows[8:16].astype(BF)
    first[HALF:, 2 * D :] = jnp.zeros((8, 2 * D), BF)
    second[:, : 3 * D] = entry[HALF:]
    second[:, 3 * D :] = leave[HALF:]


def pad_frames(source, target):
    for f in range(2):
        target[f * FRAME_ROWS : f * FRAME_ROWS + PLACES, :] = source[0, f]
        target[f * FRAME_ROWS + PLACES : (f + 1) * FRAME_ROWS, :] = jnp.zeros(
            (FRAME_ROWS - PLACES, D), BF
        )


def arrange_tokens(where, video, tokens, *pieces):
    pad_frames(video, tokens)
    split_pieces(nn(piece_from_frame(where[1]), tokens[...]).astype(BF), pieces)


def temporal_forward(*refs):
    video, pieces, refs = refs[:4], refs[4:11], refs[11:]
    out, refs = refs[:4], refs[4:]
    (normed_out, packed_out, weight_out, leave_out, params_out, bias_out), refs = refs[:6], refs[6:]
    weights, extra, stack, normed_ref, packed_ref, blended, sems, out_sems = refs
    own = lax.axis_index("fsdp")
    copies = piece_copies(pieces, ENTRY_PIECES, own, weights, extra, sems)
    for c in copies:
        c.start()
    stack_pieces(video, stack)
    unit, _ = normalised(stack[...].astype(F32))
    for c in copies:
        c.wait()
    outs = [
        pltpu.make_async_copy(weights.at[:, pl.ds(0, 3 * D)], weight_out, out_sems.at[0]),
        pltpu.make_async_copy(normed_ref, normed_out, out_sems.at[1]),
        pltpu.make_async_copy(packed_ref, packed_out, out_sems.at[2]),
        pltpu.make_async_copy(weights.at[:, pl.ds(3 * D, D)], leave_out, out_sems.at[3]),
    ]
    outs[0].start()
    outs[3].start()
    params = extra[0].astype(F32)
    for k in range(1, 8):
        params = params + extra[k].astype(F32)
    params_out[...] = params
    for r in range(4):
        bias_out[r : r + 1, :] = small_row(params, 9 + r)
    normed = (unit * small_row(params, 0) + small_row(params, 3)).astype(BF)
    normed_ref[...] = nn(place_from_piece(), normed).astype(BF)
    outs[1].start()
    wide_product(normed_ref, weights, packed_ref, 3 * D, D)
    outs[2].start()
    keep = spot_mask(2 * GROUP, GROUP)

    def heads(i, carry):
        at = pl.multiple_of(i * 128, 128)
        for t in range(SPOTS // GROUP):
            rows = pl.ds(t * GROUP, GROUP)
            blended[rows, pl.ds(at, 128)] = attend_block(
                packed_ref[rows, pl.ds(at, 128)],
                packed_ref[rows, pl.ds(at + D, 128)],
                packed_ref[rows, pl.ds(at + 2 * D, 128)],
                keep,
            )
        return carry

    lax.fori_loop(0, HEADS // 2, heads, 0)
    split_pieces(nn(piece_from_place(), blended[...]).astype(BF), out)
    for c in outs:
        c.wait()


def spatial_forward(*refs):
    (tokens, params_ref, w_exit), places, pieces, refs = refs[:3], refs[3:7], refs[7:13], refs[13:]
    after_two, normed_three = refs[:2]
    held, refs = refs[2:9], refs[9:]
    weights, stack, after_ref, normed_ref, packed_ref, blended, blended_time, sems, out_sems = refs
    own = lax.axis_index("fsdp")
    me = lax.axis_index("frame")
    copies = piece_copies(pieces, PLANE_PIECES, own, weights, None, sems)
    for c in copies:
        c.start()
    params = params_ref[...]
    stack_pieces(places, stack)
    blended_time[...] = nn(frame_from_piece(me), stack[...]).astype(BF)
    for c in copies:
        c.wait()
    outs = [
        pltpu.make_async_copy(src, dst, out_sems.at[i])
        for i, (src, dst) in enumerate(
            zip(
                (
                    weights.at[:, pl.ds(0, 3 * D)],
                    weights.at[:, pl.ds(3 * D, D)],
                    blended_time,
                    after_ref,
                    normed_ref,
                    packed_ref,
                    blended,
                ),
                held,
                strict=True,
            )
        )
    ]
    for c in outs[:3]:
        c.start()
    after_time = (
        tokens[...].astype(F32)
        + nn(blended_time[...], w_exit[...])
        + small_row(params, 6)
    )
    after_ref[...] = after_time
    outs[3].start()
    unit, _ = normalised(after_time)
    normed_ref[...] = (unit * small_row(params, 1) + small_row(params, 4)).astype(BF)
    outs[4].start()
    wide_product(normed_ref, weights, packed_ref, 3 * D, D)
    outs[5].start()
    keep = lax.broadcasted_iota(jnp.int32, (2 * FRAME_ROWS, FRAME_ROWS), 1) < PLACES

    def heads(i, carry):
        at = pl.multiple_of(i * 128, 128)
        for f in range(2):
            rows = pl.ds(f * FRAME_ROWS, FRAME_ROWS)
            blended[rows, pl.ds(at, 128)] = attend_block(
                packed_ref[rows, pl.ds(at, 128)],
                packed_ref[rows, pl.ds(at + D, 128)],
                packed_ref[rows, pl.ds(at + 2 * D, 128)],
                keep,
            )
        return carry

    lax.fori_loop(0, HEADS // 2, heads, 0)
    outs[6].start()
    last = after_ref[...] + nn(blended[...], weights[:, 3 * D :]) + small_row(params, 7)
    after_two[...] = last
    unit, _ = normalised(last)
    normed_three[...] = (unit * small_row(params, 2) + small_row(params, 5)).astype(BF)
    for c in outs:
        c.wait()


def feed_forward(where, normed, after_ref, cot, params_ref, bias, *refs):
    pieces, refs = refs[:9], refs[9:]
    (output, grad_after, branch, keep_we, send_we, keep_wc, send_wc, small), refs = refs[:8], refs[8:]
    w_in, w_out, normed_own, total, grad_normed, shuffle, sems = refs
    own = where[0]
    parity = own & 1
    first_copies, later = [], []
    for k, (array, at) in enumerate(EXPAND_PIECES):
        source = pieces[array].at[pl.ds(at, SHARD)]
        first_copies.append(
            pltpu.make_async_copy(source, w_in.at[pl.ds(k * SHARD, SHARD)], sems.at[k])
        )
    for k, (array, at) in enumerate(CONTRACT_PIECES):
        for c in range(4):
            source = pieces[array].at[pl.ds(at, SHARD), pl.ds(c * D, D)]
            spot = (k // 2) * D + (parity ^ (k & 1)) * 384 + c * SHARD
            target = w_out.at[pl.ds(pl.multiple_of(spot, 32), SHARD)]
            later.append(pltpu.make_async_copy(source, target, sems.at[8 + len(later)]))
    for c in first_copies + later:
        c.start()

    column = lax.broadcasted_iota(jnp.int32, (1, D), 1)
    block = (column * 683) >> 16
    order = (own ^ block) * SHARD + column - block * SHARD
    chosen = jnp.where(
        lax.broadcasted_iota(jnp.int32, (D, D), 0) == order, jnp.ones((), F32), jnp.zeros((), F32)
    ).astype(BF)
    normed_own[...] = nn(normed[...], chosen).astype(BF)
    total[...] = jnp.zeros_like(total)
    grad_normed[...] = jnp.zeros_like(grad_normed)
    small[...] = jnp.zeros_like(small)
    for c in first_copies + later:
        c.wait()

    def step(p, carry):
        chip = (own >> 1) ^ p
        at = pl.ds(pl.multiple_of(chip * D, D), D)
        rows = pl.ds(pl.multiple_of(p * D, D), D)
        hidden = nn(normed_own[...], w_in[:, at]) + bias[pl.ds(chip, 1), :]
        area = 0.5 + 0.5 * lax.erf(hidden * 0.7071067811865476)
        slope = area + hidden * (0.3989422804014327 * jnp.exp(-0.5 * hidden * hidden))
        active = (hidden * area).astype(BF)
        total[...] += nn(active, w_out[rows, :])
        grad_hidden = (nt(cot[...], w_out[rows, :]) * slope).astype(BF)
        grad_normed[...] += nt(grad_hidden, w_in[:, at])
        small[pl.ds(9 + chip, 1), :] = jnp.sum(grad_hidden.astype(F32), axis=0, keepdims=True)
        shuffle[...] = tn(active, cot[...]).astype(BF)
        for kind, ref in ((parity, keep_wc), (1 - parity, send_wc)):
            for c in range(4):
                rows = pl.ds(pl.multiple_of(kind * 384 + c * SHARD, 32), SHARD)
                ref[p, :, c * D : (c + 1) * D] = shuffle[rows, :]
        moved = tn(normed_own[...], grad_hidden).astype(BF)
        for j in range(4):
            keep_we[j, :, at] = moved[2 * j * SHARD : (2 * j + 1) * SHARD]
            send_we[j, :, at] = moved[(2 * j + 1) * SHARD : (2 * j + 2) * SHARD]
        return carry

    lax.fori_loop(0, 4, step, 0)
    params = params_ref[...]
    values = after_ref[...]
    result = (values + (total[...] + small_row(params, 8))).astype(BF)
    for f in range(2):
        output[0, f] = result[f * FRAME_ROWS : f * FRAME_ROWS + PLACES]
    unit, scale = normalised(values)
    dn = nt(grad_normed[...].astype(BF), chosen)
    inner, dgain, dshift = norm_back(dn, unit, scale, small_row(params, 2))
    top = cot[...].astype(F32)
    dafter = top + inner
    grad_after[...] = dafter
    branch[...] = dafter.astype(BF)
    small[2:3, :] = dgain
    small[5:6, :] = dshift
    small[8:9, :] = jnp.sum(top, axis=0, keepdims=True)


def spatial_back(branch, packed, w_last, grad_packed, grad_blended):
    grad_blended[...] = nt(branch[...], w_last[...]).astype(BF)
    keep = lax.broadcasted_iota(jnp.int32, (FRAME_ROWS, 2 * FRAME_ROWS), 0) < PLACES

    def heads(i, carry):
        at = pl.multiple_of(i * 128, 128)
        for f in range(2):
            rows = pl.ds(f * FRAME_ROWS, FRAME_ROWS)
            dq, dk, dv = attend_block_back(
                packed[rows, pl.ds(at, 128)],
                packed[rows, pl.ds(at + D, 128)],
                packed[rows, pl.ds(at + 2 * D, 128)],
                grad_blended[rows, pl.ds(at, 128)],
                keep,
            )
            grad_packed[rows, pl.ds(at, 128)] = dq
            grad_packed[rows, pl.ds(at + D, 128)] = dk
            grad_packed[rows, pl.ds(at + 2 * D, 128)] = dv
        return carry

    lax.fori_loop(0, HEADS // 2, heads, 0)


def spatial_back_norm(where, *refs):
    grad_packed, branch, grad_after, after_ref, params_ref, small_in, w_entry, w_exit = refs[:8]
    grad_first, branch_first, small, *pieces = refs[8:]
    params = params_ref[...]
    dn = nt(grad_packed[...], w_entry[...]).astype(BF).astype(F32)
    unit, scale = normalised(after_ref[...])
    inner, dgain, dshift = norm_back(dn, unit, scale, small_row(params, 1))
    first = grad_after[...] + inner
    grad_first[...] = first
    low = first.astype(BF)
    branch_first[...] = low
    back = nt(low, w_exit[...]).astype(BF)
    split_pieces(nn(piece_from_frame(where[1]), back).astype(BF), pieces)
    small[...] = small_in[...]
    small[1:2, :] = dgain
    small[4:5, :] = dshift
    small[6:7, :] = jnp.sum(low.astype(F32), axis=0, keepdims=True)
    small[7:8, :] = jnp.sum(branch[...].astype(F32), axis=0, keepdims=True)


def temporal_back(*refs):
    video, pieces, (packed, small_in, weights), refs = refs[:4], refs[4:8], refs[8:11], refs[11:]
    (grad_packed, small), out, (stack, grads) = refs[:2], refs[2:6], refs[6:]
    stack_pieces(pieces, stack)
    grads[...] = nn(place_from_piece(), stack[...]).astype(BF)
    keep = spot_mask(GROUP, 2 * GROUP)

    def heads(i, carry):
        at = pl.multiple_of(i * 128, 128)
        for t in range(SPOTS // GROUP):
            rows = pl.ds(t * GROUP, GROUP)
            dq, dk, dv = attend_block_back(
                packed[rows, pl.ds(at, 128)],
                packed[rows, pl.ds(at + D, 128)],
                packed[rows, pl.ds(at + 2 * D, 128)],
                grads[rows, pl.ds(at, 128)],
                keep,
            )
            grad_packed[rows, pl.ds(at, 128)] = dq
            grad_packed[rows, pl.ds(at + D, 128)] = dk
            grad_packed[rows, pl.ds(at + 2 * D, 128)] = dv
        return carry

    lax.fori_loop(0, HEADS // 2, heads, 0)
    dn = nt(grad_packed[...], weights[...]).astype(BF)
    moved = nn(piece_from_place(), dn)
    split_pieces(moved.astype(BF), out)
    stack_pieces(video, stack)
    unit, _ = normalised(stack[...].astype(F32))
    small[...] = small_in[...]
    small[0:1, :] = jnp.sum(moved * unit, axis=0, keepdims=True)
    small[3:4, :] = jnp.sum(moved, axis=0, keepdims=True)


def input_back(where, tokens, grad_first, params_ref, *refs):
    pieces, (out, stack) = refs[:4], refs[4:]
    stack_pieces(pieces, stack)
    dn = nn(frame_from_piece(where[1]), stack[...])
    unit, scale = normalised(tokens[...].astype(F32))
    moved = dn * small_row(params_ref[...], 0)
    inner = scale * (
        moved
        - jnp.mean(moved, axis=-1, keepdims=True)
        - unit * jnp.mean(moved * unit, axis=-1, keepdims=True)
    )
    total = grad_first[...] + inner
    for f in range(2):
        out[0, f] = total[f * FRAME_ROWS : f * FRAME_ROWS + PLACES]


def weight_grads(where, *refs, tiles):
    step = pl.program_id(0)
    own = where[0]
    pairs, (keep, send, shuffle) = refs[: 2 * len(tiles)], refs[2 * len(tiles) :]
    first = 0
    for i, count in enumerate(tiles):

        @pl.when((step >= first) & (step < first + count))
        def _(i=i):
            shuffle[...] = tn(pairs[2 * i][...], pairs[2 * i + 1][...]).astype(BF)

        first += count
    for j in range(4):
        for parity, ref in ((0, keep), (1, send)):
            rows = pl.ds(pl.multiple_of((own ^ (2 * j + parity)) * SHARD, 32), SHARD)
            ref[j] = shuffle[rows, :]


def by_columns(width, step):
    def run(i, carry):
        step(pl.ds(pl.multiple_of(i * 384, 128), 384))
        return carry

    lax.fori_loop(0, width // 384, run, 0)


def plane_one_sums(*refs, count):
    keeps, gots, (for_x, for_y, held) = refs[:count], refs[count : 2 * count], refs[2 * count :]

    def step(at):
        for i, (keep, got) in enumerate(zip(keeps, gots, strict=True)):
            total = [keep[j, :, at].astype(F32) + got[j, :, at].astype(F32) for j in range(4)]
            for_x[2 * i, :, at] = total[1][:HALF].astype(BF)
            for_x[2 * i + 1, :, at] = total[3][:HALF].astype(BF)
            for_y[2 * i, :, at] = total[2][HALF:].astype(BF)
            for_y[2 * i + 1, :, at] = total[3][HALF:].astype(BF)
            held[i, 0, :, at] = total[0][:HALF]
            held[i, 1, :, at] = total[0][HALF:]
            held[i, 2, :, at] = total[2][:HALF]
            held[i, 3, :, at] = total[1][HALF:]

    by_columns(keeps[0].shape[-1], step)


def plane_two_sums(held, from_x, from_y, next_y, next_x, left):
    def step(at):
        for i in range(held.shape[0]):
            next_y[i, :, at] = (held[i, 2, :, at] + from_x[2 * i + 1, :, at].astype(F32)).astype(BF)
            next_x[i, :, at] = (held[i, 3, :, at] + from_y[2 * i + 1, :, at].astype(F32)).astype(BF)
            left[i, 0, :, at] = held[i, 0, :, at] + from_x[2 * i, :, at].astype(F32)
            left[i, 1, :, at] = held[i, 1, :, at] + from_y[2 * i, :, at].astype(F32)

    by_columns(held.shape[-1], step)


def line_one_sums(where, left, got_y, got_x, out, stays):
    odd = where[1] & 1

    def step(at):
        for i in range(left.shape[0]):
            first = left[i, 0, :, at] + got_y[i, :, at].astype(F32)
            second = left[i, 1, :, at] + got_x[i, :, at].astype(F32)
            out[i, :, at] = jnp.where(odd == 1, first, second).astype(BF)
            stays[i, :, at] = jnp.where(odd == 1, second, first)

    by_columns(left.shape[-1], step)


def pair_sums(one, two, out):
    def step(at):
        for i in range(out.shape[0]):
            out[i, :, at] = (one[i, :, at].astype(F32) + two[i, :, at].astype(F32)).astype(BF)

    by_columns(out.shape[-1], step)


def line_result(where, full, other, *outs, parts):
    odd = where[1] & 1
    for out, (i, first, columns) in zip(outs, parts, strict=True):
        for block in range(columns // D):
            at = slice(first + block * D, first + (block + 1) * D)
            one, two = full[i, :, at].astype(F32), other[i, :, at].astype(F32)
            low = jnp.where(odd == 1, two, one)
            high = jnp.where(odd == 1, one, two)
            if out.shape[1] == D:
                out[block * SHARD : block * SHARD + HALF, :] = low
                out[block * SHARD + HALF : (block + 1) * SHARD, :] = high
            else:
                out[:HALF, block * D : (block + 1) * D] = low
                out[HALF:, block * D : (block + 1) * D] = high


def chain_start(left, got_y, got_x, *outs):
    def step(at):
        for i, out in enumerate(outs):
            out[0, :HALF, at] = (left[i, 0, :, at] + got_y[i, :, at].astype(F32)).astype(BF)
            out[0, HALF:, at] = (left[i, 1, :, at] + got_x[i, :, at].astype(F32)).astype(BF)

    by_columns(left.shape[-1], step)


def chain_result(where, *refs):
    inner = (where[1] == 1) | (where[1] == 2)
    count = len(refs) // 3
    for total, got, out in zip(refs[:count], refs[count : 2 * count], refs[2 * count :], strict=True):
        for block in range(total.shape[-1] // D):
            at = slice(block * D, (block + 1) * D)
            value = jnp.where(inner, total[0, :, at].astype(F32), got[0, :, at].astype(F32))
            if out.shape[1] == D:
                out[block * SHARD : (block + 1) * SHARD, :] = value
            else:
                out[:, at] = value


def put_small(target, at, value):
    target[at : at + 8, :D] = value[:8]
    target[at : at + 8, D : 2 * D] = value[8:]
    target[at : at + 8, 2 * D :] = jnp.zeros((8, target.shape[1] - 2 * D), BF)


def add_small(kept, source, at):
    got = source[at : at + 8, : 2 * D].astype(F32)
    return kept[...].astype(F32) + jnp.concatenate([got[:, :D], got[:, D:]], axis=0)


def plane_one_both(keep, got, small, small_got, for_x, for_y, held, kept):
    def step(at):
        total = [keep[j, :, at].astype(F32) + got[j, :, at].astype(F32) for j in range(4)]
        for_x[:HALF, at] = total[1][:HALF].astype(BF)
        for_x[HALF:SHARD, at] = total[3][:HALF].astype(BF)
        for_y[:HALF, at] = total[2][HALF:].astype(BF)
        for_y[HALF:, at] = total[3][HALF:].astype(BF)
        held[0, :, at] = total[0][:HALF]
        held[1, :, at] = total[0][HALF:]
        held[2, :, at] = total[2][:HALF]
        held[3, :, at] = total[1][HALF:]

    by_columns(keep.shape[-1], step)
    value = (small[...] + small_got[...]).astype(BF)
    kept[...] = value
    put_small(for_x, SHARD, value)


def plane_two_both(held, from_x, from_y, kept, next_y, next_x, left, kept_next):
    def step(at):
        next_y[:HALF, at] = (held[2, :, at] + from_x[HALF:SHARD, at].astype(F32)).astype(BF)
        next_x[:, at] = (held[3, :, at] + from_y[HALF:, at].astype(F32)).astype(BF)
        left[0, :, at] = held[0, :, at] + from_x[:HALF, at].astype(F32)
        left[1, :, at] = held[1, :, at] + from_y[:HALF, at].astype(F32)

    by_columns(held.shape[-1], step)
    value = add_small(kept, from_x, SHARD).astype(BF)
    kept_next[...] = value
    put_small(next_y, HALF, value)


def line_one_both(where, left, got_y, got_x, kept, out, stays, kept_next):
    odd = where[1] & 1

    def step(at):
        first = left[0, :, at] + got_y[:HALF, at].astype(F32)
        second = left[1, :, at] + got_x[:, at].astype(F32)
        out[:HALF, at] = jnp.where(odd == 1, first, second).astype(BF)
        stays[:, at] = jnp.where(odd == 1, second, first)

    by_columns(left.shape[-1], step)
    value = add_small(kept, got_y, HALF).astype(BF)
    kept_next[...] = value
    put_small(out, HALF, value)


def line_two_both(stays, near, kept, pair, kept_next):
    def step(at):
        pair[:HALF, at] = (stays[:, at] + near[:HALF, at].astype(F32)).astype(BF)

    by_columns(stays.shape[-1], step)
    value = add_small(kept, near, HALF).astype(BF)
    kept_next[...] = value
    put_small(pair, HALF, value)


def line_three_both(pair, far, kept, full, small):
    def step(at):
        full[0, :, at] = (pair[:HALF, at].astype(F32) + far[:HALF, at].astype(F32)).astype(BF)

    by_columns(full.shape[-1], step)
    small[...] = add_small(kept, far, HALF)


def shape(*dims, dtype=BF):
    return jax.ShapeDtypeStruct(dims, dtype)


def kept(*dims, dtype=BF):
    return pltpu.HBM(dims, dtype)


NO_COST = pl.CostEstimate(flops=1000, bytes_accessed=1000, transcendentals=0)


def limit(mebibytes):
    return pltpu.CompilerParams(vmem_limit_bytes=mebibytes << 20)


def whole_call(kernel, name, outs, *ins, mebibytes=16, scalars=0, scratch=(), **options):
    specs = [pl.BlockSpec(memory_space=pltpu.SMEM)] * scalars + [VMEM] * (len(ins) - scalars)
    single = not isinstance(outs, (list, tuple))
    return pl.pallas_call(
        functools.partial(kernel, **options),
        name=name,
        out_shape=outs,
        in_specs=specs,
        out_specs=VMEM if single else [VMEM] * len(outs),
        scratch_shapes=scratch,
        compiler_params=limit(mebibytes),
        cost_estimate=NO_COST,
    )(*ins)


CORE = [(i, i ^ 1) for i in range(8)]
ACROSS = [(i, i ^ 2) for i in range(8)]
UP = [(i, i ^ 4) for i in range(8)]
NEAR = [(i, i ^ 1) for i in range(4)]
FAR = [(i, i ^ 2) for i in range(4)]


def swap(value, pairs, axis="fsdp"):
    return lax.ppermute(value, axis, pairs)


def shift(pieces):
    moved = [lax.ppermute(pieces[k], "frame", [(i, i ^ k) for i in range(4)]) for k in (1, 2, 3)]
    return [pieces[0], *moved]


def after(value, *earlier):
    return lax.optimization_barrier((value, *earlier))[0]


class Reduction:
    def __init__(self, where, keep, send):
        self.where, self.keep, self.count, self.width = where, keep, len(keep), keep[0].shape[-1]
        self.got = [swap(v, CORE) for v in send]

    def shape(self, *dims, dtype=BF):
        return shape(*dims, HALF, self.width, dtype=dtype)

    def plane_one(self, *earlier):
        got = [after(g, *earlier) for g in self.got] if earlier else self.got
        n = self.count
        for_x, for_y, self.held = whole_call(
            plane_one_sums,
            "plane_one",
            [self.shape(2 * n), self.shape(2 * n), self.shape(n, 4, dtype=F32)],
            *self.keep,
            *got,
            count=n,
            mebibytes=24,
        )
        self.from_x = swap(for_x, ACROSS)
        self.from_y = swap(for_y, UP)
        return for_x, for_y

    def plane_two(self, *earlier):
        n = self.count
        next_y, next_x, self.left = whole_call(
            plane_two_sums,
            "plane_two",
            [self.shape(n), self.shape(n), self.shape(n, 2, dtype=F32)],
            self.held,
            after(self.from_x, *earlier),
            after(self.from_y, *earlier),
        )
        self.got_y = swap(next_y, UP)
        self.got_x = swap(next_x, ACROSS)
        return next_y, next_x

    def line_one(self, *earlier):
        n = self.count
        out, self.stays = whole_call(
            line_one_sums,
            "line_one",
            [self.shape(n), self.shape(n, dtype=F32)],
            self.where,
            self.left,
            after(self.got_y, *earlier),
            after(self.got_x, *earlier),
            scalars=1,
        )
        self.near = swap(out, NEAR, "frame")
        return (out,)

    def line_two(self, *earlier):
        self.pair = whole_call(
            pair_sums, "line_two", self.shape(self.count), self.stays, after(self.near, *earlier)
        )
        self.far = swap(self.pair, FAR, "frame")
        return (self.pair,)

    def line_three(self, *earlier):
        self.full = whole_call(
            pair_sums, "line_three", self.shape(self.count), self.pair, after(self.far, *earlier)
        )
        self.other = swap(self.full, NEAR, "frame")
        return (self.full,)

    def result(self, parts, outs):
        return whole_call(
            line_result, "line_result", outs, self.where, self.full, self.other, scalars=1, parts=parts
        )


class ReductionChain(Reduction):
    def chain_one(self, *earlier):
        self.mine = whole_call(
            chain_start,
            "chain_start",
            [shape(1, SHARD, self.width)] * self.count,
            self.left,
            after(self.got_y, *earlier),
            after(self.got_x, *earlier),
        )
        self.inward = [swap(v, [(0, 1), (3, 2)], "frame") for v in self.mine]
        self.pair, self.across = [None] * self.count, [None] * self.count
        self.total, self.outward = [None] * self.count, [None] * self.count
        return tuple(self.mine)

    def chain_two(self, i, *earlier):
        out = shape(1, SHARD, self.width)
        self.pair[i] = whole_call(
            pair_sums, "chain_two", out, self.mine[i], after(self.inward[i], *earlier)
        )
        self.across[i] = swap(self.pair[i], [(1, 2), (2, 1)], "frame")
        return (self.pair[i],)

    def chain_three(self, i, *earlier):
        out = shape(1, SHARD, self.width)
        self.total[i] = whole_call(
            pair_sums, "chain_three", out, self.pair[i], after(self.across[i], *earlier)
        )
        self.outward[i] = swap(self.total[i], [(1, 0), (2, 3)], "frame")
        return (self.total[i],)

    def chain_result(self, i, out, *earlier):
        got = after(self.outward[i], *earlier)
        return whole_call(
            chain_result, "chain_result", [out], self.where, self.total[i], got, scalars=1
        )[0]


class ReductionBoth(Reduction):
    def join(self, small):
        self.small, self.small_got = small, swap(small, CORE)

    def flat(self, rows, dtype=BF):
        return shape(rows, self.width, dtype=dtype)

    def plane_one(self, *earlier):
        kept = shape(16, D)
        for_x, for_y, self.held, self.kept = whole_call(
            plane_one_both,
            "plane_one_both",
            [self.flat(SHARD + 8), self.flat(SHARD), self.shape(4, dtype=F32), kept],
            self.keep[0],
            after(self.got[0], *earlier),
            self.small,
            self.small_got,
            mebibytes=24,
        )
        self.from_x, self.from_y = swap(for_x, ACROSS), swap(for_y, UP)
        return for_x, for_y

    def plane_two(self, *earlier):
        next_y, next_x, self.left, self.kept = whole_call(
            plane_two_both,
            "plane_two_both",
            [self.flat(HALF + 8), self.flat(HALF), self.shape(2, dtype=F32), shape(16, D)],
            self.held,
            after(self.from_x, *earlier),
            after(self.from_y, *earlier),
            self.kept,
        )
        self.got_y, self.got_x = swap(next_y, UP), swap(next_x, ACROSS)
        return next_y, next_x

    def line_one(self, *earlier):
        out, self.stays, self.kept = whole_call(
            line_one_both,
            "line_one_both",
            [self.flat(HALF + 8), self.flat(HALF, F32), shape(16, D)],
            self.where,
            self.left,
            after(self.got_y, *earlier),
            after(self.got_x, *earlier),
            self.kept,
            scalars=1,
        )
        self.near = swap(out, NEAR, "frame")
        return (out,)

    def line_two(self, *earlier):
        self.pair, self.kept = whole_call(
            line_two_both,
            "line_two_both",
            [self.flat(HALF + 8), shape(16, D)],
            self.stays,
            after(self.near, *earlier),
            self.kept,
        )
        self.far = swap(self.pair, FAR, "frame")
        return (self.pair,)

    def line_three(self, *earlier):
        self.full, self.small = whole_call(
            line_three_both,
            "line_three_both",
            [self.shape(1), shape(16, D, dtype=F32)],
            self.pair,
            after(self.far, *earlier),
            self.kept,
        )
        self.other = swap(self.full, NEAR, "frame")
        return (self.full,)


def body(
    video,
    temporal_entry,
    temporal_exit,
    spatial_entry,
    spatial_exit,
    expand_weight,
    contract_weight,
    layer_gains,
    layer_shifts,
    branch_biases,
    expand_bias,
    cotangent,
):
    own = lax.axis_index("fsdp")
    where = jnp.stack([own, lax.axis_index("frame")]).astype(jnp.int32)
    rows = lambda *parts: jnp.concatenate(parts, axis=0)

    sources = (temporal_entry, temporal_exit, layer_gains, layer_shifts, branch_biases, expand_bias)
    g1a, g1b = pl.pallas_call(
        arrange_parameters,
        name="arrange_parameters",
        out_shape=[shape(HALF + 8, WIDE), shape(HALF, WIDE)],
        in_specs=[pl.BlockSpec(memory_space=pltpu.SMEM)] + [HBM] * 6,
        out_specs=[VMEM] * 2,
        scratch_shapes=[pltpu.VMEM(v.shape, BF) for v in sources] + [pltpu.SemaphoreType.DMA((6,))],
        compiler_params=limit(8),
        cost_estimate=NO_COST,
    )(
        where,
        *(pltpu.with_memory_space_constraint(v, pltpu.HBM) for v in sources),
    )
    x1, y1 = swap(g1a, ACROSS), swap(g1b, UP)

    tokens, *video_pieces = whole_call(
        arrange_tokens,
        "arrange_tokens",
        [shape(ROWS, D)] + [shape(PIECE, D)] * 4,
        where,
        after(video, g1a),
        scalars=1,
    )
    video_pieces = shift(video_pieces)

    plane = jnp.concatenate([spatial_entry, spatial_exit], axis=1)
    contract = jnp.concatenate([contract_weight[c * SHARD : (c + 1) * SHARD] for c in range(4)], axis=1)
    x1, y1, plane, contract, *_ = lax.optimization_barrier((x1, y1, plane, contract, tokens))
    to_y = rows(g1a, x1, plane[HALF:])
    to_x = rows(g1b, y1, plane[:HALF])
    r2y, r2x = swap(to_y, UP), swap(to_x, ACROSS)
    c1 = swap(rows(g1a, g1b, x1, y1, r2y[:112], r2x[:96]), CORE)
    cot = whole_call(pad_frames, "arrange_cotangent", shape(ROWS, D), after(cotangent, r2y))
    to_y = after(rows(plane[:HALF], r2x[96:], contract), *video_pieces[1:])
    to_x = after(rows(plane[HALF:], r2y[112:], expand_weight), *video_pieces[1:])
    r3y, r3x = swap(to_y, UP), swap(to_x, ACROSS)

    *places, normed_place, packed_place, entry_full, exit_full, params, bias_full = pl.pallas_call(
        temporal_forward,
        name="temporal_forward",
        out_shape=[shape(PIECE, D)] * 4
        + [
            kept(SPOTS, D),
            kept(SPOTS, 3 * D),
            kept(D, 3 * D),
            kept(D, D),
            shape(8, WIDE, dtype=F32),
            shape(8, D, dtype=F32),
        ],
        in_specs=[VMEM] * 4 + [HBM] * 7,
        out_specs=[VMEM] * 4 + [KEPT] * 4 + [VMEM] * 2,
        scratch_shapes=[
            pltpu.VMEM((D, WIDE), BF),
            pltpu.VMEM((8, 8, WIDE), BF),
            pltpu.VMEM((ROWS, D), BF),
            pltpu.VMEM((SPOTS, D), BF),
            pltpu.VMEM((SPOTS, 3 * D), BF),
            pltpu.VMEM((SPOTS, D), BF),
            pltpu.SemaphoreType.DMA((24,)),
            pltpu.SemaphoreType.DMA((4,)),
        ],
        compiler_params=limit(24),
        cost_estimate=NO_COST,
    )(after(video_pieces[0], to_y, to_x), *video_pieces[1:], g1a, g1b, x1, y1, r2y, r2x, c1)
    places = shift(places)

    r3y, r3x = after(r3y, *places[1:]), after(r3x, *places[1:])
    c2 = swap(rows(plane, r2x[96:], r2y[112:], r3y[:96], r3x[:96]), CORE)
    to_y = rows(expand_weight, r3x[96:])
    to_x = rows(contract, r3y[96:])
    r4y, r4x = swap(to_y, UP), swap(to_x, ACROSS)
    (
        after_space,
        normed_three,
        space_full,
        last_full,
        blended_time,
        after_time,
        normed_two,
        packed_space,
        blended_space,
    ) = pl.pallas_call(
        spatial_forward,
        name="spatial_forward",
        out_shape=[
            shape(ROWS, D, dtype=F32),
            shape(ROWS, D),
            kept(D, 3 * D),
            kept(D, D),
            kept(ROWS, D),
            kept(ROWS, D, dtype=F32),
            kept(ROWS, D),
            kept(ROWS, 3 * D),
            kept(ROWS, D),
        ],
        in_specs=[VMEM] * 7 + [HBM] * 6,
        out_specs=[VMEM] * 2 + [KEPT] * 7,
        scratch_shapes=[
            pltpu.VMEM((D, WIDE), BF),
            pltpu.VMEM((ROWS, D), BF),
            pltpu.VMEM((ROWS, D), F32),
            pltpu.VMEM((ROWS, D), BF),
            pltpu.VMEM((ROWS, 3 * D), BF),
            pltpu.VMEM((ROWS, D), BF),
            pltpu.VMEM((ROWS, D), BF),
            pltpu.SemaphoreType.DMA((16,)),
            pltpu.SemaphoreType.DMA((7,)),
        ],
        compiler_params=limit(24),
        cost_estimate=NO_COST,
    )(after(tokens, to_y, to_x, cot), params, exit_full, *places, plane, r2y, r2x, r3y, r3x, c2)

    c3 = swap(after(rows(expand_weight, contract, r3x[96:], r3y[96:]), normed_three), CORE)
    c4, c5 = swap(r4y, CORE), swap(r4x, CORE)
    output, grad_after, branch_last, keep_we, send_we, keep_wc, send_wc, small = pl.pallas_call(
        feed_forward,
        name="feed_forward",
        out_shape=[
            shape(*video.shape),
            shape(ROWS, D, dtype=F32),
            shape(ROWS, D),
            shape(4, SHARD, WIDE),
            shape(4, SHARD, WIDE),
            shape(4, SHARD, WIDE),
            shape(4, SHARD, WIDE),
            shape(16, D, dtype=F32),
        ],
        in_specs=[pl.BlockSpec(memory_space=pltpu.SMEM)] + [VMEM] * 5 + [HBM] * 9,
        out_specs=[VMEM] * 8,
        scratch_shapes=[
            pltpu.VMEM((D, WIDE), BF),
            pltpu.VMEM((WIDE, D), BF),
            pltpu.VMEM((ROWS, D), BF),
            pltpu.VMEM((ROWS, D), F32),
            pltpu.VMEM((ROWS, D), F32),
            pltpu.VMEM((D, D), BF),
            pltpu.SemaphoreType.DMA((40,)),
        ],
        compiler_params=limit(28),
        cost_estimate=NO_COST,
    )(
        *(where, normed_three, after_space, cot, params, bias_full),
        *(expand_weight, contract, r3x, r3y, r4y, r4x, c3, c4, c5),
    )
    forward_sum = ReductionChain(where, [keep_we, keep_wc], [send_we, send_wc])

    grad_packed = pl.pallas_call(
        spatial_back,
        name="spatial_back",
        out_shape=shape(ROWS, 3 * D),
        in_specs=[VMEM] * 3,
        out_specs=VMEM,
        scratch_shapes=[pltpu.VMEM((ROWS, D), BF)],
        compiler_params=limit(16),
        cost_estimate=NO_COST,
    )(branch_last, packed_space, last_full)
    placed = forward_sum.plane_one(grad_packed)
    grad_first, branch_first, small, *grad_pieces = whole_call(
        spatial_back_norm,
        "spatial_back_norm",
        [shape(ROWS, D, dtype=F32), shape(ROWS, D), shape(16, D, dtype=F32)] + [shape(PIECE, D)] * 4,
        where,
        grad_packed,
        branch_last,
        grad_after,
        after_time,
        params,
        after(small, *placed),
        space_full,
        exit_full,
        mebibytes=20,
        scalars=1,
    )
    grad_pieces = shift(grad_pieces)

    whole = lambda *dims: pl.BlockSpec(dims, lambda i, w: (0,) * len(dims))

    def grads(*pairs):
        tiles = tuple(b.shape[1] // D for _, b in pairs)
        specs, first = [], 0
        for (a, b), count in zip(pairs, tiles, strict=True):
            at = lambda i, w, first=first, count=count: (0, jnp.clip(i - first, 0, count - 1))
            specs += [whole(*a.shape), pl.BlockSpec((b.shape[0], D), at)]
            first += count
        return pl.pallas_call(
            functools.partial(weight_grads, tiles=tiles),
            name="weight_grads",
            out_shape=[shape(4, SHARD, D * first)] * 2,
            grid_spec=pltpu.PrefetchScalarGridSpec(
                num_scalar_prefetch=1,
                grid=(first,),
                in_specs=specs,
                out_specs=[pl.BlockSpec((4, SHARD, D), lambda i, w: (0, 0, i))] * 2,
                scratch_shapes=[pltpu.VMEM((D, D), BF)],
            ),
            compiler_params=limit(16),
            cost_estimate=NO_COST,
        )(where, *(v for pair in pairs for v in pair))

    keep_space, send_space = grads(
        (blended_time, branch_first), (normed_two, grad_packed), (blended_space, branch_last)
    )
    output = after(jnp.swapaxes(output, 1, 2), send_space)

    grad_place, small, *normed_back = pl.pallas_call(
        temporal_back,
        name="temporal_back",
        out_shape=[shape(SPOTS, 3 * D), shape(16, D, dtype=F32)] + [shape(PIECE, D)] * 4,
        in_specs=[VMEM] * 11,
        out_specs=[VMEM] * 6,
        scratch_shapes=[pltpu.VMEM((ROWS, D), BF), pltpu.VMEM((SPOTS, D), BF)],
        compiler_params=limit(20),
        cost_estimate=NO_COST,
    )(*video_pieces, after(grad_pieces[0], output), *grad_pieces[1:], packed_place, small, entry_full)

    placed = forward_sum.plane_two(small)
    space_sum = ReductionBoth(where, [keep_space], [after(send_space, *placed)])
    space_sum.join(after(small, *placed))
    normed_back = shift([after(v, *placed) for v in normed_back])
    keep_time, send_time = grads((after(normed_place, *placed), grad_place))
    placed = space_sum.plane_one(send_time)
    placed = forward_sum.chain_one(*placed, *normed_back[1:])
    time_sum = Reduction(where, [keep_time], [after(send_time, *placed)])
    input_grad = whole_call(
        input_back,
        "input_back",
        shape(*video.shape, dtype=F32),
        where,
        after(tokens, *placed),
        grad_first,
        params,
        *normed_back,
        scalars=1,
        scratch=[pltpu.VMEM((ROWS, D), BF)],
    )
    placed = forward_sum.chain_two(0, *placed, input_grad)
    placed = space_sum.plane_two(*placed)
    placed = forward_sum.chain_two(1, *placed)
    placed = forward_sum.chain_three(0, *placed)
    placed = space_sum.line_one(*placed)
    placed = time_sum.plane_one(*placed)
    placed = forward_sum.chain_three(1, *placed)
    wide = lambda rows, columns: shape(rows, columns, dtype=F32)
    grad_expand = forward_sum.chain_result(0, wide(SHARD, WIDE), *placed)
    placed = time_sum.plane_two(*placed, grad_expand)
    placed = space_sum.line_two(*placed)
    placed = time_sum.line_one(*placed)
    placed = time_sum.line_two(*placed)
    grad_contract = forward_sum.chain_result(1, wide(4 * SHARD, D), *placed)
    placed = space_sum.line_three(*placed)
    small = space_sum.small
    placed = time_sum.line_three(*placed, grad_contract)
    input_grad = jnp.swapaxes(input_grad, 1, 2)
    grad_exit_time, grad_entry_space, grad_exit_space = space_sum.result(
        ((0, 0, D), (0, D, 3 * D), (0, 4 * D, D)),
        [wide(SHARD, D), wide(SHARD, 3 * D), wide(SHARD, D)],
    )
    time_sum.other = after(time_sum.other, grad_exit_space)
    (grad_entry_time,) = time_sum.result(((0, 0, 3 * D),), [wide(SHARD, 3 * D)])

    mine = lax.dynamic_slice_in_dim(small[:9], own * SHARD, SHARD, axis=1)
    return (
        jnp.swapaxes(output, 1, 2),
        jnp.swapaxes(input_grad, 1, 2),
        grad_entry_time,
        grad_exit_time,
        grad_entry_space,
        grad_exit_space,
        grad_expand,
        grad_contract,
        mine[0:3],
        mine[3:6],
        mine[6:9],
        lax.dynamic_slice_in_dim(small[9:13].reshape(WIDE), own * 384, 384),
    )


def solution(mesh):
    placed = (
        P("fsdp", "frame", None, None),
        P("fsdp", None),
        P("fsdp", None),
        P("fsdp", None),
        P("fsdp", None),
        P("fsdp", None),
        P("fsdp", None),
        P(None, "fsdp"),
        P(None, "fsdp"),
        P(None, "fsdp"),
        P("fsdp"),
        P("fsdp", "frame", None, None),
    )
    special = mesh.shape["fsdp"] == 8 and mesh.shape["frame"] == 4
    return jax.shard_map(
        body if special else general_body,
        mesh=mesh,
        in_specs=placed,
        out_specs=(
            P("fsdp", "frame", None, None),
            P("fsdp", "frame", None, None),
            P("fsdp", None),
            P("fsdp", None),
            P("fsdp", None),
            P("fsdp", None),
            P("fsdp", None),
            P("fsdp", None),
            P(None, "fsdp"),
            P(None, "fsdp"),
            P(None, "fsdp"),
            P("fsdp"),
        ),
        check_vma=False,
    )
```
